512 devices in a mesh: seq: 64 (over y_hi, z, core), tp: 8 (over x, y_lo).
Axes of the slice: x: 4, y: 8 (y_hi: 4, y_lo: 2; y = y_hi * 2 + y_lo), z: 8, core: 2. Of those that a mesh axis runs over, the one named last changes fastest.
Arguments:
- frames_in: bfloat16 [1536, 32768], P('tp', 'seq'), may hold values from -30 to 30
- norm_gain: float32 [1536], P('tp'), may hold values from 0.5 to 2
- value_weight: bfloat16 [1536, 1536], P('tp'), may hold values from -0.15625 to 0.15625
- gate_weight: bfloat16 [1536, 1536], P('tp'), may hold values from -0.15625 to 0.15625
- depth_kernel: float32 [1536, 32], P('tp'), may hold values from -6 to 6
- conv_gain: float32 [1536], P('tp'), may hold values from 0.5 to 2
- out_weight: bfloat16 [1536, 1536], P('tp'), may hold values from -0.15625 to 0.15625
- cotangent: bfloat16 [1536, 32768], P('tp', 'seq'), may hold values from -15 to 15
Outputs:
- block_out: bfloat16 [1536, 32768], P('tp', 'seq')
- input_grad: bfloat16 [1536, 32768], P('tp', 'seq')
- grad_norm_gain: float32 [1536], P('tp')
- grad_value: bfloat16 [1536, 1536], P('tp')
- grad_gate: bfloat16 [1536, 1536], P('tp')
- grad_kernel: float32 [1536, 32], P('tp')
- grad_conv_gain: float32 [1536], P('tp')
- grad_out: bfloat16 [1536, 1536], P('tp')
The draws below stay inside these ranges and needn't reach their ends.
All inputs are finite; a program needn't handle non-finite values.
Results may differ from the reference program's by a relative error of at most 0.027.
Values may be sent and summed in bfloat16 or wider, within the bound.
A program may use at most 64 MiB of HBM per device.

```python
import math
import jax
import jax.numpy as jnp
from jax import lax

D = 1536
KERNEL = 32
FRAMES = 32768
N_TP = 8


def spread_draw(key, rows, cols, base):
    k_noise, k_rows, k_cols = jax.random.split(key, 3)
    place = jnp.arange(cols, dtype=jnp.float32) / max(cols - 1, 1)
    row_scale = jnp.exp(jax.random.uniform(k_rows, (rows, 1), jnp.float32, jnp.log(0.3), jnp.log(3.0)))
    jitter = jnp.exp(jax.random.uniform(k_cols, (1, cols), jnp.float32, -0.35, 0.35))
    ramp = jnp.exp(jnp.log(3.0) * (place - 0.5))
    noise = jnp.clip(jax.random.normal(k_noise, (rows, cols), jnp.float32), -4.0, 4.0)
    return base * noise * row_scale * ramp[None, :] * jitter


def draw_frames_in(key, part):
    return spread_draw(jax.random.fold_in(key, 11), FRAMES, D, 1.0).T.astype(jnp.bfloat16)


def draw_depth_kernel(key, part):
    return spread_draw(jax.random.fold_in(key, 12), KERNEL, D, KERNEL ** (-0.5)).T.astype(jnp.float32)


def draw_cotangent(key, part):
    return spread_draw(jax.random.fold_in(key, 13), FRAMES, D, 0.5).T.astype(jnp.bfloat16)


def block_scale(stream_key, shape, shards, least, top_value):
    loudness, own = 1.0, jax.random.fold_in(stream_key, 6)
    for position, parts in shards:
        heights = jnp.exp(jax.random.uniform(jax.random.fold_in(own, position), (parts,), jnp.float32, least / len(shards), top_value / len(shards)))
        loudness = loudness * jnp.repeat(heights, shape[position] // parts).reshape([-1 if axis == position else 1 for axis in range(len(shape))])
    return loudness


def scatter_about(own_key, dims, scale, bound, shards=(), kind=jnp.bfloat16):
    factor_of = block_scale(own_key, dims, shards, -0.22, 0.18) if shards else 1.0
    values = jax.random.normal(own_key, dims, jnp.float32) * scale * factor_of
    return jnp.minimum(jnp.maximum(values, -bound), bound).astype(kind)


def setup_inputs(seed: int = 0) -> dict:
    keys = jax.random.split(jax.random.key(seed), 9)
    frames_in = draw_frames_in(jax.random.fold_in(keys[8], 71), 0)
    norm_gain = jnp.clip(jnp.exp(math.log(2.0) - 1.3862944 * jax.random.uniform(keys[1], (D,), jnp.float32) ** block_scale(keys[1], (D,), ((0, 8),), -0.2, 0.2)), 0.5, 2.0)
    value_weight = scatter_about(keys[2], (D, D), D ** -0.5, 0.15625, ((0, 8),))
    gate_weight = scatter_about(keys[3], (D, D), D ** -0.5, 0.15625, ((0, 8),))
    depth_kernel = draw_depth_kernel(jax.random.fold_in(keys[8], 71), 0)
    conv_gain = jnp.clip(jnp.exp(math.log(2.0) - 1.3862944 * jax.random.uniform(keys[5], (D,), jnp.float32) ** block_scale(keys[5], (D,), ((0, 8),), -0.2, 0.2)), 0.5, 2.0)
    out_weight = scatter_about(keys[6], (D, D), D ** -0.5, 0.15625, ((0, 8),))
    cotangent = draw_cotangent(jax.random.fold_in(keys[8], 71), 0)
    return {"frames_in": frames_in, "norm_gain": norm_gain, "value_weight": value_weight, "gate_weight": gate_weight, "depth_kernel": depth_kernel, "conv_gain": conv_gain, "out_weight": out_weight, "cotangent": cotangent}


EPS = 1e-05

def widen(values):
    return lax.optimization_barrier(values).astype(jnp.float32)

def norm_parts(values):
    mean = lax.optimization_barrier(jnp.mean(values, axis=0, keepdims=True))
    centred = values - mean
    spread = lax.optimization_barrier(jnp.mean(centred * centred, axis=0, keepdims=True))
    inverse = lax.rsqrt(spread + EPS)
    return (centred * inverse, inverse)

def norm_back(d_hat, hat, inverse):
    first = lax.optimization_barrier(jnp.mean(d_hat, axis=0, keepdims=True))
    second = lax.optimization_barrier(jnp.mean(d_hat * hat, axis=0, keepdims=True))
    return (d_hat - first - hat * second) * inverse

def block_sum(pairs, frames):
    block = D // N_TP
    total = jnp.zeros((D, frames), jnp.float32)
    for index in range(N_TP):
        low = index * block
        term = jnp.zeros((D, frames), jnp.float32)
        for values, weight in pairs:
            term = term + jnp.dot(weight[low:low + block].T, values[low:low + block], preferred_element_type=jnp.float32)
        total = total + widen(term.astype(jnp.bfloat16))
    return total

def reference(frames_in, norm_gain, value_weight, gate_weight, depth_kernel, conv_gain, out_weight, cotangent):
    frames = frames_in.shape[1]
    reach = KERNEL // 2
    scale = jnp.float32(FRAMES) ** (-0.5)
    inputs = frames_in.astype(jnp.float32)
    hat_in, inverse_in = norm_parts(inputs)
    normed = (hat_in * norm_gain[:, None]).astype(jnp.bfloat16)
    value = jnp.dot(value_weight, normed, preferred_element_type=jnp.float32)
    gate = jnp.dot(gate_weight, normed, preferred_element_type=jnp.float32)
    gate_sig = jax.nn.sigmoid(gate)
    glu = (value * gate_sig).astype(jnp.bfloat16)
    glu_wide = jnp.pad(widen(glu), ((0, 0), (reach, reach)))
    conv = jnp.zeros((D, frames), jnp.float32)
    for tap in range(KERNEL):
        conv = conv + depth_kernel[:, tap:tap + 1] * glu_wide[:, tap:tap + frames]
    hat_conv, inverse_conv = norm_parts(conv)
    scaled = hat_conv * conv_gain[:, None]
    swish_sig = jax.nn.sigmoid(scaled)
    act = (scaled * swish_sig).astype(jnp.bfloat16)
    block_out = (inputs + jnp.dot(out_weight, act, preferred_element_type=jnp.float32)).astype(jnp.bfloat16)
    grad_out = (jnp.dot(cotangent, act.T, preferred_element_type=jnp.float32) * scale).astype(jnp.bfloat16)
    d_act = block_sum(((cotangent, out_weight),), frames)
    d_scaled = d_act * (swish_sig + scaled * swish_sig * (1.0 - swish_sig))
    grad_conv_gain = lax.optimization_barrier(jnp.sum(d_scaled * hat_conv, axis=1)) * scale
    d_conv = norm_back(d_scaled * conv_gain[:, None], hat_conv, inverse_conv).astype(jnp.bfloat16)
    d_conv_f = widen(d_conv)
    d_conv_wide = jnp.pad(d_conv_f, ((0, 0), (reach, reach)))
    d_glu = jnp.zeros((D, frames), jnp.float32)
    kernel_cols = []
    for tap in range(KERNEL):
        start = 2 * reach - tap
        d_glu = d_glu + depth_kernel[:, tap:tap + 1] * d_conv_wide[:, start:start + frames]
        kernel_cols.append(lax.optimization_barrier(jnp.sum(glu_wide[:, tap:tap + frames] * d_conv_f, axis=1)))
    grad_kernel = jnp.stack(kernel_cols, axis=1) * scale
    d_value = (d_glu * gate_sig).astype(jnp.bfloat16)
    d_gate = (d_glu * value * gate_sig * (1.0 - gate_sig)).astype(jnp.bfloat16)
    grad_value = (jnp.dot(d_value, normed.T, preferred_element_type=jnp.float32) * scale).astype(jnp.bfloat16)
    grad_gate = (jnp.dot(d_gate, normed.T, preferred_element_type=jnp.float32) * scale).astype(jnp.bfloat16)
    d_normed = block_sum(((d_value, value_weight), (d_gate, gate_weight)), frames)
    grad_norm_gain = lax.optimization_barrier(jnp.sum(d_normed * hat_in, axis=1)) * scale
    input_grad = (cotangent.astype(jnp.float32) + norm_back(d_normed * norm_gain[:, None], hat_in, inverse_in)).astype(jnp.bfloat16)
    return (block_out, input_grad, grad_norm_gain, grad_value, grad_gate, grad_kernel, grad_conv_gain, grad_out)
```

```python
import functools

import jax
import jax.numpy as jnp
from jax import lax
from jax.experimental import pallas as pl
from jax.experimental.pallas import tpu as pltpu
from jax.sharding import PartitionSpec as P

EPS = 1e-05
F32 = jnp.float32
BF16 = jnp.bfloat16
MESH = pl.DeviceIdType.MESH

TP = 8
SEQ = 64
NZ = 8
NY = 4
CH = 192
FR = 512
D = CH * TP
TAPS = 32
REACH = TAPS // 2
PAD = 128
WIDE = FR + 2 * PAD
HALF = CH // 2
ZR = HALF // 2
ZL = D // 4
SR = CH // NZ
BLK = 32
GAIN_CONV = TAPS
GAIN_NORM = TAPS + 1


def fold8(v):
    out = v[0:8]
    for i in range(8, v.shape[0], 8):
        out = out + v[i : i + 8]
    return out


def row_block(i, blk):
    return pl.ds(pl.multiple_of(i * blk, blk), blk)


def put_tile(ref, a, b):
    for j in range(4):
        ref[j : j + 1, :] = a[:, 128 * j : 128 * j + 128]
        ref[4 + j : 5 + j, :] = b[:, 128 * j : 128 * j + 128]


def tile_row(t):
    return jnp.concatenate([t[j : j + 1] for j in range(4)], axis=1)


def kernel(
    x_ref, par_ref, wv_ref, wg_ref, wo_ref, cot_ref,
    block_out, input_grad, gval_out, ggate_out, gout_out, small_out,
    hat_in, value, sig, conv, hatc, dact, dglu,
    normed, act_all, da_s, da_r, dn_s, dn_r,
    glu_w, dcv_w, dv_b, dg_b, prod,
    st_s, st_r,
    g16, c1, s16, zr, y16, yr, r16,
    sm_s, sm_c, sm_t, sm_z, sm_y, sm_r,
    st_ss, st_rs, ag_ss, ag_rs, rs_ss, rs_rs, ha_ss, ha_rs,
    c1_ss, c1_rs, z_ss, z_rs, y_ss, y_rs, w_ss, w_rs, f_ss, f_rs,
    sc_ss, sc_rs, sz_ss, sz_rs, sy_ss, sy_rs, sw_ss, sw_rs,
):
    p = lax.axis_index("tp")
    q = lax.axis_index("seq")
    core = lax.rem(q, 2)
    chip = q // 2
    z = lax.rem(chip, NZ)
    yh = chip // NZ
    scale = float(FR * SEQ) ** (-0.5)
    sends = []

    def send(src, dst, ss, rs, dev):
        copy = pltpu.make_async_remote_copy(
            src_ref=src, dst_ref=dst, send_sem=ss, recv_sem=rs, device_id=dev, device_id_type=MESH
        )
        copy.start()
        sends.append(copy)

    def arrived(dst, ss, rs, dev):
        pltpu.make_async_remote_copy(
            src_ref=dst, dst_ref=dst, send_sem=ss, recv_sem=rs, device_id=dev, device_id_type=MESH
        ).wait_recv()

    def tp_dev(k):
        return {"tp": lax.rem(p + k, TP), "seq": q}

    def z_dev(k):
        return {"tp": p, "seq": (yh * NZ + lax.rem(z + k, NZ)) * 2 + core}

    def y_dev(k):
        return {"tp": p, "seq": (lax.rem(yh + k, NY) * NZ + z) * 2 + core}

    mate = {"tp": p, "seq": chip * 2 + (1 - core)}
    right = {"tp": p, "seq": lax.rem(q + 1, SEQ)}
    left = {"tp": p, "seq": lax.rem(q + SEQ - 1, SEQ)}

    barrier = pltpu.get_barrier_semaphore()
    peers = [tp_dev(k) for k in range(1, TP)] + [z_dev(k) for k in range(1, NZ)]
    peers += [y_dev(k) for k in range(1, NY)] + [mate, right, left]
    for dev in peers:
        pl.semaphore_signal(barrier, inc=1, device_id=dev, device_id_type=MESH)

    zero8 = jnp.zeros((8, FR), F32)

    def loop(n, body, init):
        return lax.fori_loop(0, n, body, init)

    def collapse(v):
        return jnp.sum(v, axis=0, keepdims=True)

    def local_moments(ref, slot):
        total = loop(CH // BLK, lambda i, a: a + fold8(ref[row_block(i, BLK), :].astype(F32)), zero8)
        mean = collapse(total) / CH

        def body(i, a):
            c = ref[row_block(i, BLK), :].astype(F32) - mean
            return a + fold8(c * c)

        put_tile(st_s.at[slot], mean, collapse(loop(CH // BLK, body, zero8)))

    def share(slot):
        st_r[slot, p] = st_s[slot]
        for k in range(1, TP):
            send(st_s.at[slot], st_r.at[slot, p], st_ss.at[slot, k - 1], st_rs.at[slot, k - 1], tp_dev(k))

    def shared(slot):
        for k in range(1, TP):
            arrived(st_r.at[slot, lax.rem(p + TP - k, TP)], st_ss.at[slot, k - 1], st_rs.at[slot, k - 1], tp_dev(k))
        return [st_r[slot, j] for j in range(TP)]

    def merged(slot):
        parts = shared(slot)
        total = parts[0]
        for t in parts[1:]:
            total = total + t
        mean = total[0:4] / TP
        spread = total[4:8]
        for t in parts:
            off = t[0:4] - mean
            spread = spread + CH * (off * off)
        inverse = lax.rsqrt(spread / D + EPS)
        return tile_row(mean), tile_row(inverse)

    def summed(slot):
        parts = shared(slot)
        total = parts[0]
        for t in parts[1:]:
            total = total + t
        return tile_row(total[0:4]) / D, tile_row(total[4:8]) / D

    def gather_send(buf, n):
        for k in range(1, TP):
            send(buf.at[p], buf.at[p], ag_ss.at[n, k - 1], ag_rs.at[n, k - 1], tp_dev(k))

    def gather_wait(buf, n):
        for k in range(1, TP):
            arrived(buf.at[lax.rem(p + TP - k, TP)], ag_ss.at[n, k - 1], ag_rs.at[n, k - 1], tp_dev(k))

    def scatter_send(out, into, n):
        for k in range(1, TP):
            send(
                out.at[lax.rem(p + k, TP)], into.at[p], rs_ss.at[n, k - 1], rs_rs.at[n, k - 1], tp_dev(k)
            )

    def scatter_wait(into, n):
        for k in range(1, TP):
            arrived(into.at[lax.rem(p + TP - k, TP)], rs_ss.at[n, k - 1], rs_rs.at[n, k - 1], tp_dev(k))

    def halo_send(buf, n):
        send(buf.at[:, PAD : 2 * PAD], buf.at[:, PAD + FR : WIDE], ha_ss.at[n, 0], ha_rs.at[n, 0], left)
        send(buf.at[:, FR : FR + PAD], buf.at[:, 0:PAD], ha_ss.at[n, 1], ha_rs.at[n, 1], right)

    def halo_wait(buf, n):
        arrived(buf.at[:, PAD + FR : WIDE], ha_ss.at[n, 0], ha_rs.at[n, 0], left)
        arrived(buf.at[:, 0:PAD], ha_ss.at[n, 1], ha_rs.at[n, 1], right)

        @pl.when(q == 0)
        def _():
            buf[:, 0:PAD] = jnp.zeros((CH, PAD), buf.dtype)

        @pl.when(q == SEQ - 1)
        def _():
            buf[:, PAD + FR : WIDE] = jnp.zeros((CH, PAD), buf.dtype)

    def contract_rows(w, v):
        return lax.dot_general(w, v, (((0,), (0,)), ((), ())), preferred_element_type=F32)

    def contract_cols(a, b):
        return lax.dot_general(a, b, (((1,), (1,)), ((), ())), preferred_element_type=F32)

    local_moments(x_ref, 0)
    pl.semaphore_wait(barrier, len(peers))
    share(0)

    def dact_body(d, c):
        lanes = pl.ds(pl.multiple_of(d * (2 * CH), 128), 2 * CH)
        term = contract_rows(wo_ref[:, lanes], cot_ref[...]).astype(BF16)
        da_s[2 * d] = term[0:CH]
        da_s[2 * d + 1] = term[CH : 2 * CH]
        return c

    loop(TP // 2, dact_body, 0)

    mean_in, inv_in = merged(0)

    def norm_body(i, c):
        r = row_block(i, BLK)
        h = (x_ref[r, :].astype(F32) - mean_in) * inv_in
        hat_in[r, :] = h
        normed[p, r, :] = (h * par_ref[r, GAIN_NORM : GAIN_NORM + 1]).astype(BF16)
        return c

    loop(CH // BLK, norm_body, 0)
    gather_send(normed, 0)
    da_r[p] = da_s[p]
    scatter_send(da_s, da_r, 0)

    gather_wait(normed, 0)
    everything = normed[...].reshape(D, FR)
    value[...] = jnp.dot(wv_ref[...], everything, preferred_element_type=F32)
    sig[...] = jnp.dot(wg_ref[...], everything, preferred_element_type=F32)

    def glu_body(i, c):
        r = row_block(i, BLK)
        s = jax.nn.sigmoid(sig[r, :])
        sig[r, :] = s
        glu_w[r, PAD : PAD + FR] = (value[r, :] * s).astype(BF16)
        return c

    loop(CH // BLK, glu_body, 0)
    halo_send(glu_w, 0)
    halo_wait(glu_w, 0)

    def conv_body(i, c):
        r = row_block(i, 16)
        w = glu_w[r, :].astype(F32)
        taps = par_ref[r, 0:TAPS]
        acc = jnp.zeros((16, FR), F32)
        for k in range(TAPS):
            acc = acc + taps[:, k : k + 1] * pltpu.roll(w, (REACH - k) % WIDE, 1)[:, PAD : PAD + FR]
        conv[r, :] = acc
        return c

    loop(CH // 16, conv_body, 0)
    local_moments(conv, 1)
    share(1)

    scatter_wait(da_r, 0)

    def dsum_body(i, c):
        r = row_block(i, BLK)
        total = da_r[0, r, :].astype(F32)
        for j in range(1, TP):
            total = total + da_r[j, r, :].astype(F32)
        dact[r, :] = total
        return c

    loop(CH // BLK, dsum_body, 0)
    mean_c, inv_c = merged(1)

    def act_body(i, carry):
        a, b = carry
        r = row_block(i, BLK)
        h = (conv[r, :] - mean_c) * inv_c
        hatc[r, :] = h
        g = par_ref[r, GAIN_CONV : GAIN_CONV + 1]
        scaled = h * g
        s = jax.nn.sigmoid(scaled)
        act_all[p, r, :] = (scaled * s).astype(BF16)
        ds = dact[r, :] * (s + scaled * s * (1.0 - s))
        sm_s[r, GAIN_CONV : GAIN_CONV + 1] = jnp.sum(ds * h, axis=1, keepdims=True)
        e = ds * g
        dact[r, :] = e
        return a + fold8(e), b + fold8(e * h)

    sm_s[...] = jnp.zeros((CH, 128), F32)
    first, second = loop(CH // BLK, act_body, (zero8, zero8))
    put_tile(st_s.at[2], collapse(first), collapse(second))
    share(2)
    gather_send(act_all, 1)
    first, second = summed(2)

    def dconv_body(i, c):
        r = row_block(i, BLK)
        dcv_w[r, PAD : PAD + FR] = ((dact[r, :] - first - hatc[r, :] * second) * inv_c).astype(BF16)
        return c

    loop(CH // BLK, dconv_body, 0)
    halo_send(dcv_w, 1)
    halo_wait(dcv_w, 1)

    def back_body(i, c):
        r = row_block(i, 16)
        w = dcv_w[r, :].astype(F32)
        taps = par_ref[r, 0:TAPS]
        u = glu_w[r, PAD : PAD + FR].astype(F32)
        acc = jnp.zeros((16, FR), F32)
        for k in range(TAPS):
            moved = pltpu.roll(w, (k - REACH) % WIDE, 1)[:, PAD : PAD + FR]
            acc = acc + taps[:, k : k + 1] * moved
            m = u * moved
            prod[k, r, :] = (m[:, 0:128] + m[:, 128:256]) + (m[:, 256:384] + m[:, 384:512])
        s = sig[r, :]
        dv = acc * s
        dv_b[r, :] = dv.astype(BF16)
        dg_b[r, :] = (dv * value[r, :] * (1.0 - s)).astype(BF16)
        return c

    loop(CH // 16, back_body, 0)

    other = pl.ds(pl.multiple_of((1 - core) * HALF, HALF), HALF)
    mine = pl.ds(pl.multiple_of(core * HALF, HALF), HALF)

    def pair_send(g):
        send(g16.at[g, other, :], c1.at[g], c1_ss.at[g], c1_rs.at[g], mate)

    def weight_grad(g, left_ref, all_ref):
        g16[g] = contract_cols(left_ref[...], all_ref[...].reshape(D, FR)).astype(BF16)
        pair_send(g)

    weight_grad(0, dv_b, normed)
    weight_grad(1, dg_b, normed)

    def dn_body(d, c):
        lanes = pl.ds(pl.multiple_of(d * (2 * CH), 128), 2 * CH)
        term = contract_rows(wv_ref[:, lanes], dv_b[...]) + contract_rows(wg_ref[:, lanes], dg_b[...])
        term = term.astype(BF16)
        dn_s[2 * d] = term[0:CH]
        dn_s[2 * d + 1] = term[CH : 2 * CH]
        return c

    loop(TP // 2, dn_body, 0)
    dn_r[p] = dn_s[p]
    scatter_send(dn_s, dn_r, 1)

    def z_block(zz):
        return (
            pl.ds(pl.multiple_of((zz // 4) * ZR, 16), ZR),
            pl.ds(pl.multiple_of(lax.rem(zz, 4) * ZL, 128), ZL),
        )

    def z_send(g):
        arrived(c1.at[g], c1_ss.at[g], c1_rs.at[g], mate)
        s16[g] = (g16[g, mine, :].astype(F32) + c1[g].astype(F32)).astype(BF16)
        for k in range(1, NZ):
            rr, ll = z_block(lax.rem(z + k, NZ))
            send(s16.at[g, rr, ll], zr.at[g, z], z_ss.at[g, k - 1], z_rs.at[g, k - 1], z_dev(k))
        rr, ll = z_block(z)
        zr[g, z] = s16[g, rr, ll]

    def y_send(g):
        for k in range(1, NZ):
            arrived(zr.at[g, lax.rem(z + NZ - k, NZ)], z_ss.at[g, k - 1], z_rs.at[g, k - 1], z_dev(k))
        total = zr[g, 0].astype(F32)
        for j in range(1, NZ):
            total = total + zr[g, j].astype(F32)
        y16[g] = total.astype(BF16)
        yr[g, yh] = total.astype(BF16)
        for k in range(1, NY):
            send(y16.at[g], yr.at[g, yh], y_ss.at[g, k - 1], y_rs.at[g, k - 1], y_dev(k))

    outs = (gval_out, ggate_out, gout_out)

    def out_block(zz, cc):
        rr, ll = z_block(zz)
        return pl.ds(pl.multiple_of(cc * HALF + (zz // 4) * ZR, 16), ZR), ll

    def w_send(g):
        for k in range(1, NY):
            arrived(yr.at[g, lax.rem(yh + NY - k, NY)], y_ss.at[g, k - 1], y_rs.at[g, k - 1], y_dev(k))
        total = yr[g, 0].astype(F32)
        for j in range(1, NY):
            total = total + yr[g, j].astype(F32)
        r16[g] = (total * scale).astype(BF16)
        rr, ll = out_block(z, core)
        outs[g][rr, ll] = r16[g]
        for k in range(1, NZ):
            send(r16.at[g], outs[g].at[rr, ll], w_ss.at[g, k - 1], w_rs.at[g, k - 1], z_dev(k))
        send(r16.at[g], outs[g].at[rr, ll], f_ss.at[g, 0], f_rs.at[g, 0], mate)

    def f_send(g):
        for k in range(1, NZ):
            rr, ll = out_block(lax.rem(z + NZ - k, NZ), core)
            arrived(outs[g].at[rr, ll], w_ss.at[g, k - 1], w_rs.at[g, k - 1], z_dev(k))
            send(outs[g].at[rr, ll], outs[g].at[rr, ll], f_ss.at[g, k], f_rs.at[g, k], mate)

    def f_wait(g):
        for k in range(NZ):
            rr, ll = out_block(lax.rem(z + NZ - k, NZ), 1 - core)
            arrived(outs[g].at[rr, ll], f_ss.at[g, k], f_rs.at[g, k], mate)

    z_send(0)
    z_send(1)

    gather_wait(act_all, 1)
    act_flat = act_all[...].reshape(D, FR)
    value[...] = jnp.dot(wo_ref[...], act_flat, preferred_element_type=F32)
    weight_grad(2, cot_ref, act_all)

    def out_body(i, c):
        r = row_block(i, BLK)
        block_out[r, :] = (x_ref[r, :].astype(F32) + value[r, :]).astype(BF16)
        return c

    loop(CH // BLK, out_body, 0)

    for k in range(TAPS):
        sm_s[:, k : k + 1] = jnp.sum(prod[k], axis=1, keepdims=True)

    z_send(2)

    scatter_wait(dn_r, 1)

    def dnorm_body(i, carry):
        a, b = carry
        r = row_block(i, BLK)
        total = dn_r[0, r, :].astype(F32)
        for j in range(1, TP):
            total = total + dn_r[j, r, :].astype(F32)
        h = hat_in[r, :]
        sm_s[r, GAIN_NORM : GAIN_NORM + 1] = jnp.sum(total * h, axis=1, keepdims=True)
        e = total * par_ref[r, GAIN_NORM : GAIN_NORM + 1]
        dact[r, :] = e
        return a + fold8(e), b + fold8(e * h)

    first, second = loop(CH // BLK, dnorm_body, (zero8, zero8))
    put_tile(st_s.at[3], collapse(first), collapse(second))
    share(3)
    send(sm_s, sm_c, sc_ss.at[0], sc_rs.at[0], mate)

    y_send(0)
    y_send(1)

    first, second = summed(3)

    def grad_body(i, c):
        r = row_block(i, BLK)
        back = (dact[r, :] - first - hat_in[r, :] * second) * inv_in
        input_grad[r, :] = (cot_ref[r, :].astype(F32) + back).astype(BF16)
        return c

    loop(CH // BLK, grad_body, 0)

    arrived(sm_c, sc_ss.at[0], sc_rs.at[0], mate)
    sm_t[...] = sm_s[...] + sm_c[...]

    def sm_rows(zz):
        return pl.ds(pl.multiple_of(zz * SR, 8), SR)

    for k in range(1, NZ):
        send(sm_t.at[sm_rows(lax.rem(z + k, NZ)), :], sm_z.at[z], sz_ss.at[k - 1], sz_rs.at[k - 1], z_dev(k))
    sm_z[z] = sm_t[sm_rows(z), :]

    w_send(0)
    w_send(1)
    y_send(2)

    for k in range(1, NZ):
        arrived(sm_z.at[lax.rem(z + NZ - k, NZ)], sz_ss.at[k - 1], sz_rs.at[k - 1], z_dev(k))
    total = sm_z[0]
    for j in range(1, NZ):
        total = total + sm_z[j]
    sm_r[0] = total
    sm_y[yh] = total
    for k in range(1, NY):
        send(sm_r.at[0], sm_y.at[yh], sy_ss.at[k - 1], sy_rs.at[k - 1], y_dev(k))

    f_send(0)
    f_send(1)
    w_send(2)

    for k in range(1, NY):
        arrived(sm_y.at[lax.rem(yh + NY - k, NY)], sy_ss.at[k - 1], sy_rs.at[k - 1], y_dev(k))
    total = sm_y[0]
    for j in range(1, NY):
        total = total + sm_y[j]
    sm_r[1] = total * scale
    small_out[sm_rows(z), :] = total * scale
    for k in range(1, NZ):
        send(sm_r.at[1], small_out.at[sm_rows(z), :], sw_ss.at[k - 1], sw_rs.at[k - 1], z_dev(k))

    f_send(2)
    for k in range(1, NZ):
        arrived(small_out.at[sm_rows(lax.rem(z + NZ - k, NZ)), :], sw_ss.at[k - 1], sw_rs.at[k - 1], z_dev(k))
    for g in range(3):
        f_wait(g)
    for copy in sends:
        copy.wait_send()


def local(
    frames_in, norm_gain, value_weight, gate_weight, depth_kernel, conv_gain, out_weight, cotangent
):
    par = jnp.concatenate(
        [depth_kernel, conv_gain[:, None], norm_gain[:, None], jnp.zeros((CH, 128 - TAPS - 2), F32)], axis=1
    )
    act = jax.ShapeDtypeStruct((CH, FR), BF16)
    mat = jax.ShapeDtypeStruct((CH, D), BF16)
    vm = pltpu.VMEM
    dma = pltpu.SemaphoreType.DMA
    full = vm((CH, FR), F32)
    eight = vm((TP, CH, FR), BF16)
    wide = vm((CH, WIDE), BF16)
    block = vm((CH, FR), BF16)
    scratch = [full] * 7 + [eight] * 6 + [wide, wide, block, block, vm((TAPS, CH, 128), F32)]
    scratch += [vm((4, 8, 128), F32), vm((4, TP, 8, 128), F32)]
    scratch += [
        vm((3, CH, D), BF16),
        vm((3, HALF, D), BF16),
        vm((3, HALF, D), BF16),
        vm((3, NZ, ZR, ZL), BF16),
        vm((3, ZR, ZL), BF16),
        vm((3, NY, ZR, ZL), BF16),
        vm((3, ZR, ZL), BF16),
    ]
    small = vm((CH, 128), F32)
    scratch += [small, small, small, vm((NZ, SR, 128), F32), vm((NY, SR, 128), F32), vm((2, SR, 128), F32)]
    for shape in ((4, 7), (2, 7), (2, 7), (2, 2), (3,), (3, 7), (3, 3), (3, 7), (3, 8), (1,), (7,), (3,), (7,)):
        scratch += [dma(shape), dma(shape)]
    vmem = pl.BlockSpec(memory_space=pltpu.VMEM)
    block_out, input_grad, gval, ggate, gout, small_grads = pl.pallas_call(
        kernel,
        out_shape=(act, act, mat, mat, mat, jax.ShapeDtypeStruct((CH, 128), F32)),
        in_specs=[vmem] * 6,
        out_specs=(vmem,) * 6,
        scratch_shapes=scratch,
        compiler_params=pltpu.CompilerParams(
            collective_id=0, has_side_effects=True, vmem_limit_bytes=60 * 1024 * 1024
        ),
    )(frames_in, par, value_weight, gate_weight, out_weight, cotangent)
    return (
        block_out,
        input_grad,
        small_grads[:, GAIN_NORM],
        gval,
        ggate,
        small_grads[:, 0:TAPS],
        small_grads[:, GAIN_CONV],
        gout,
    )


def solution(mesh):
    return jax.shard_map(
        local,
        mesh=mesh,
        in_specs=(
            P("tp", "seq"),
            P("tp"),
            P("tp", None),
            P("tp", None),
            P("tp", None),
            P("tp"),
            P("tp", None),
            P("tp", "seq"),
        ),
        out_specs=(
            P("tp", "seq"),
            P("tp", "seq"),
            P("tp"),
            P("tp", None),
            P("tp", None),
            P("tp", None),
            P("tp"),
            P("tp", None),
        ),
        check_vma=False,
    )
```

```python
import functools

import jax
import jax.numpy as jnp
from jax import lax
from jax.experimental import pallas as pl
from jax.experimental.pallas import tpu as pltpu
from jax.sharding import PartitionSpec as P

EPS = 1e-05
F32 = jnp.float32
BF16 = jnp.bfloat16
MESH = pl.DeviceIdType.MESH

TP = 8
SEQ = 64
NZ = 8
NY = 4
CH = 192
FR = 512
D = CH * TP
TAPS = 32
REACH = TAPS // 2
PAD = 128
WIDE = FR + 2 * PAD
HALF = CH // 2
ZR = HALF // 2
ZL = D // 4
SR = CH // NZ
BLK = 32
VMEM_LIMIT = 63 * 1024 * 1024
GAIN_CONV = TAPS
GAIN_NORM = TAPS + 1


def fold8(v):
    out = v[0:8]
    for i in range(8, v.shape[0], 8):
        out = out + v[i : i + 8]
    return out


def row_block(i, blk):
    return pl.ds(pl.multiple_of(i * blk, blk), blk)


def put_tile(ref, a, b):
    for j in range(4):
        ref[j : j + 1, :] = a[:, 128 * j : 128 * j + 128]
        ref[4 + j : 5 + j, :] = b[:, 128 * j : 128 * j + 128]


def tile_row(t):
    return jnp.concatenate([t[j : j + 1] for j in range(4)], axis=1)


def kernel(
    x_hbm, ng_hbm, wv_hbm, wg_hbm, dk_hbm, cg_hbm, wo_hbm, cot_hbm,
    *rest,
):
    finals, landed, rest = rest[0:6], rest[6:12], rest[12:]
    block_out, input_grad, gval_out, ggate_out, gout_out, small_out = landed
    (
        x_ref, ng_ref, wv_ref, wg_ref, dk_ref, cg_ref, wo_ref, cot_ref, par_t, par_ref,
        hat_in, value, sig, conv, hatc, dact,
        normed, act_all, da_s, dn_s, rs_r,
        glu_w, dcv_w, dv_b, dg_b, prod,
        st_s, st_r,
        g16, c1, s16, zr, y16, yr, r16,
        sm_s, sm_c, sm_t, sm_z, sm_y, sm_r,
        ld, fin,
        st_ss, st_rs, ag_ss, ag_rs, rs_ss, rs_rs, ha_ss, ha_rs,
        c1_ss, c1_rs, z_ss, z_rs, y_ss, y_rs, w_ss, w_rs, f_ss, f_rs,
        sc_ss, sc_rs, sz_ss, sz_rs, sy_ss, sy_rs, sw_ss, sw_rs,
    ) = rest
    stores = [pltpu.make_async_copy(landed[i], finals[i], fin.at[i]) for i in range(6)]
    fetch = (
        (x_hbm, x_ref), (dk_hbm, dk_ref), (cg_hbm, cg_ref), (ng_hbm, ng_ref),
        (wo_hbm, wo_ref), (cot_hbm, cot_ref), (wv_hbm, wv_ref), (wg_hbm, wg_ref),
    )
    loads = [pltpu.make_async_copy(src, dst, ld.at[i]) for i, (src, dst) in enumerate(fetch)]
    for copy in loads:
        copy.start()
    p = lax.axis_index("tp")
    q = lax.axis_index("seq")
    core = lax.rem(q, 2)
    chip = q // 2
    z = lax.rem(chip, NZ)
    yh = chip // NZ
    scale = float(FR * SEQ) ** (-0.5)
    sends = []

    sems = {
        "st": (st_ss, st_rs), "ag": (ag_ss, ag_rs), "rs": (rs_ss, rs_rs), "ha": (ha_ss, ha_rs),
        "c1": (c1_ss, c1_rs), "z": (z_ss, z_rs), "y": (y_ss, y_rs), "w": (w_ss, w_rs), "f": (f_ss, f_rs),
        "sc": (sc_ss, sc_rs), "sz": (sz_ss, sz_rs), "sy": (sy_ss, sy_rs), "sw": (sw_ss, sw_rs),
    }

    def remote(src, dst, key, dev):
        out, into = sems[key[0]]
        return pltpu.make_async_remote_copy(
            src_ref=src, dst_ref=dst, send_sem=out.at[key[1:]], recv_sem=into.at[key[1:]],
            device_id=dev, device_id_type=MESH,
        )

    def send(src, dst, key, dev):
        copy = remote(src, dst, key, dev)
        copy.start()
        sends.append(copy)

    def arrived(dst, key, dev):
        remote(dst, dst, key, dev).wait_recv()

    tx, ty = p // 2, lax.rem(p, 2)

    def at_tp(dx, dy):
        return lax.rem(tx + dx, 4) * 2 + lax.rem(ty + dy, 2)

    def hop(dx, dy):
        return {"tp": at_tp(dx, dy), "seq": q}

    def half(h):
        return pl.ds(h * HALF, HALF)

    def tp_dev(k):
        return {"tp": lax.rem(p + k, TP), "seq": q}

    def z_dev(k):
        return {"tp": p, "seq": (yh * NZ + lax.rem(z + k, NZ)) * 2 + core}

    def y_dev(k):
        return {"tp": p, "seq": (lax.rem(yh + k, NY) * NZ + z) * 2 + core}

    mate = {"tp": p, "seq": chip * 2 + (1 - core)}
    right = {"tp": p, "seq": lax.rem(q + 1, SEQ)}
    left = {"tp": p, "seq": lax.rem(q + SEQ - 1, SEQ)}

    barrier = pltpu.get_barrier_semaphore()
    peers = [tp_dev(k) for k in range(1, TP)] + [z_dev(k) for k in range(1, NZ)]
    peers += [y_dev(k) for k in range(1, NY)] + [mate, right, left]
    for dev in peers:
        pl.semaphore_signal(barrier, inc=1, device_id=dev, device_id_type=MESH)

    zero8 = jnp.zeros((8, FR), F32)

    def loop(n, body, init):
        return lax.fori_loop(0, n, body, init)

    def collapse(v):
        return jnp.sum(v, axis=0, keepdims=True)

    def local_moments(ref, slot):
        total = loop(CH // BLK, lambda i, a: a + fold8(ref[row_block(i, BLK), :].astype(F32)), zero8)
        mean = collapse(total) / CH

        def body(i, a):
            c = ref[row_block(i, BLK), :].astype(F32) - mean
            return a + fold8(c * c)

        put_tile(st_s.at[slot], mean, collapse(loop(CH // BLK, body, zero8)))

    def share(slot):
        st_r[slot, p] = st_s[slot]
        for k in range(1, TP):
            send(st_s.at[slot], st_r.at[slot, p], ("st", slot, k - 1), tp_dev(k))

    def shared(slot):
        for k in range(1, TP):
            arrived(st_r.at[slot, lax.rem(p + TP - k, TP)], ("st", slot, k - 1), tp_dev(k))
        return [st_r[slot, j] for j in range(TP)]

    def merged(slot):
        parts = shared(slot)
        total = parts[0]
        for t in parts[1:]:
            total = total + t
        mean = total[0:4] / TP
        spread = total[4:8]
        for t in parts:
            off = t[0:4] - mean
            spread = spread + CH * (off * off)
        inverse = lax.rsqrt(spread / D + EPS)
        return tile_row(mean), tile_row(inverse)

    def summed(slot):
        parts = shared(slot)
        total = parts[0]
        for t in parts[1:]:
            total = total + t
        return tile_row(total[0:4]) / D, tile_row(total[4:8]) / D

    RIGHT, LEFT, SIDE = (1, 0), (3, 0), (0, 1)

    gather_plan = (
        ((0, 0), 0, RIGHT), ((0, 0), 1, RIGHT), ((0, 0), 1, LEFT), ((0, 0), 0, LEFT),
        ((0, 0), 0, SIDE), ((0, 0), 1, SIDE), ((3, 0), 0, RIGHT), ((1, 0), 1, LEFT),
        ((0, 1), 0, RIGHT), ((0, 1), 0, LEFT), ((3, 0), 1, SIDE), ((1, 0), 1, SIDE),
        ((2, 0), 1, SIDE), ((3, 1), 0, RIGHT),
    )

    def gather_put(buf, n, i):
        (dx, dy), h, to = gather_plan[i]
        piece = buf.at[at_tp(dx, dy), half(h), :]
        send(piece, piece, ("ag", n, i), hop(*to))

    def gather_got(buf, n, i):
        (dx, dy), h, to = gather_plan[i]
        piece = buf.at[at_tp(dx + 4 - to[0], dy + to[1]), half(h), :]
        arrived(piece, ("ag", n, i), hop(*to))

    def gather_send(buf, n):
        for i in (0, 2, 4, 1, 3, 5):
            gather_put(buf, n, i)

    def gather_relay(buf, n):
        gather_got(buf, n, 4)
        gather_put(buf, n, 8)
        gather_got(buf, n, 2)
        gather_put(buf, n, 7)
        gather_put(buf, n, 11)
        gather_got(buf, n, 0)
        gather_put(buf, n, 6)
        gather_put(buf, n, 9)
        gather_got(buf, n, 1)
        gather_put(buf, n, 10)

    def gather_last(buf, n):
        gather_got(buf, n, 7)
        gather_put(buf, n, 12)
        gather_got(buf, n, 8)
        gather_put(buf, n, 13)

    def gather_wait(buf, n):
        for i in (3, 5, 6, 9, 10, 11, 12, 13):
            gather_got(buf, n, i)

    scatter_plan = (
        ((3, 0), 0, LEFT), ((3, 0), 1, LEFT), ((1, 0), 1, RIGHT), ((1, 0), 0, RIGHT),
        ((0, 1), 0, SIDE), ((0, 1), 1, SIDE), ((2, 0), 0, LEFT), ((2, 0), 1, RIGHT),
        ((3, 1), 0, LEFT), ((1, 1), 0, RIGHT), ((3, 1), 1, SIDE), ((1, 1), 1, SIDE),
        ((2, 1), 1, SIDE), ((2, 1), 0, LEFT),
    )

    def scatter_put(buf, n, i, merge=()):
        (dx, dy), h, to = scatter_plan[i]
        d = at_tp(dx, dy)
        for m in merge:
            arrived(rs_r.at[n, m], ("rs", n, m), hop(*scatter_plan[m][2]))
        if merge:

            def body(j, c):
                r = pl.ds(pl.multiple_of(h * HALF + j * BLK, BLK), BLK)
                total = buf[d, r, :].astype(F32)
                for m in merge:
                    total = total + rs_r[n, m, row_block(j, BLK), :].astype(F32)
                buf[d, r, :] = total.astype(BF16)
                return c

            loop(HALF // BLK, body, 0)
        send(buf.at[d, half(h), :], rs_r.at[n, i], ("rs", n, i), hop(*to))

    def scatter_send(buf, n):
        for i in (13, 12, 9, 6, 10, 3, 11, 5):
            scatter_put(buf, n, i)

    def scatter_relay(buf, n):
        scatter_put(buf, n, 8, (13,))
        scatter_put(buf, n, 7, (12,))
        scatter_put(buf, n, 0, (6,))
        scatter_put(buf, n, 1, (10,))

    def scatter_last(buf, n):
        scatter_put(buf, n, 4, (8, 9))
        scatter_put(buf, n, 2, (7, 11))

    def scatter_wait(n):
        for m in range(6):
            arrived(rs_r.at[n, m], ("rs", n, m), hop(*scatter_plan[m][2]))

    def scatter_sum(buf, n, r, j, h):
        total = buf[p, r, :].astype(F32)
        for m in ((0, 3, 4), (1, 2, 5))[h]:
            total = total + rs_r[n, m, row_block(j, BLK), :].astype(F32)
        return total

    def halo_send(buf, n):
        send(buf.at[:, PAD : 2 * PAD], buf.at[:, PAD + FR : WIDE], ("ha", n, 0), left)
        send(buf.at[:, FR : FR + PAD], buf.at[:, 0:PAD], ("ha", n, 1), right)

    def halo_wait(buf, n):
        arrived(buf.at[:, PAD + FR : WIDE], ("ha", n, 0), left)
        arrived(buf.at[:, 0:PAD], ("ha", n, 1), right)

        @pl.when(q == 0)
        def _():
            buf[:, 0:PAD] = jnp.zeros((CH, PAD), buf.dtype)

        @pl.when(q == SEQ - 1)
        def _():
            buf[:, PAD + FR : WIDE] = jnp.zeros((CH, PAD), buf.dtype)

    def contract_rows(w, v):
        return lax.dot_general(w, v, (((0,), (0,)), ((), ())), preferred_element_type=F32)

    def contract_cols(a, b):
        return lax.dot_general(a, b, (((1,), (1,)), ((), ())), preferred_element_type=F32)

    for copy in loads[0:4]:
        copy.wait()
    par_t[...] = jnp.zeros((128, 2 * 128), F32)
    par_t[0:TAPS, 0:CH] = dk_ref[...]
    par_t[GAIN_CONV : GAIN_CONV + 1, 0:CH] = cg_ref[...]
    par_t[GAIN_NORM : GAIN_NORM + 1, 0:CH] = ng_ref[...]
    par_ref[...] = par_t[...].T[0:CH]

    local_moments(x_ref, 0)
    pl.semaphore_wait(barrier, len(peers))
    share(0)
    mean_in, inv_in = merged(0)

    def norm_body(i, c):
        r = row_block(i, BLK)
        h = (x_ref[r, :].astype(F32) - mean_in) * inv_in
        hat_in[r, :] = h
        normed[p, r, :] = (h * par_ref[r, GAIN_NORM : GAIN_NORM + 1]).astype(BF16)
        return c

    loop(CH // BLK, norm_body, 0)
    gather_send(normed, 0)

    loads[4].wait()
    loads[5].wait()
    def dact_body(d, c):
        lanes = pl.ds(pl.multiple_of(d * (2 * CH), 128), 2 * CH)
        term = contract_rows(wo_ref[:, lanes], cot_ref[...]).astype(BF16)
        da_s[2 * d] = term[0:CH]
        da_s[2 * d + 1] = term[CH : 2 * CH]
        return c

    loop(TP // 2, dact_body, 0)
    gather_relay(normed, 0)
    gather_last(normed, 0)
    scatter_send(da_s, 0)
    loads[6].wait()
    loads[7].wait()
    gather_wait(normed, 0)
    everything = normed[...].reshape(D, FR)
    value[...] = jnp.dot(wv_ref[...], everything, preferred_element_type=F32)
    sig[...] = jnp.dot(wg_ref[...], everything, preferred_element_type=F32)

    def glu_body(i, c):
        r = row_block(i, BLK)
        s = jax.nn.sigmoid(sig[r, :])
        sig[r, :] = s
        glu_w[r, PAD : PAD + FR] = (value[r, :] * s).astype(BF16)
        return c

    loop(CH // BLK, glu_body, 0)
    halo_send(glu_w, 0)
    scatter_relay(da_s, 0)
    halo_wait(glu_w, 0)

    def conv_body(i, c):
        r = row_block(i, 16)
        w = glu_w[r, :].astype(F32)
        taps = par_ref[r, 0:TAPS]
        acc = jnp.zeros((16, FR), F32)
        for k in range(TAPS):
            acc = acc + taps[:, k : k + 1] * pltpu.roll(w, (REACH - k) % WIDE, 1)[:, PAD : PAD + FR]
        conv[r, :] = acc
        return c

    lax.fori_loop(0, CH // 32, conv_body, 0)
    scatter_last(da_s, 0)
    lax.fori_loop(CH // 32, CH // 16, conv_body, 0)
    local_moments(conv, 1)
    share(1)

    scatter_wait(0)
    for h in range(2):

        def dsum_body(j, c):
            r = pl.ds(pl.multiple_of(h * HALF + j * BLK, BLK), BLK)
            dact[r, :] = scatter_sum(da_s, 0, r, j, h)
            return c

        loop(HALF // BLK, dsum_body, 0)
    mean_c, inv_c = merged(1)

    def act_body(i, carry):
        a, b = carry
        r = row_block(i, BLK)
        h = (conv[r, :] - mean_c) * inv_c
        hatc[r, :] = h
        g = par_ref[r, GAIN_CONV : GAIN_CONV + 1]
        scaled = h * g
        s = jax.nn.sigmoid(scaled)
        act_all[p, r, :] = (scaled * s).astype(BF16)
        ds = dact[r, :] * (s + scaled * s * (1.0 - s))
        sm_s[r, GAIN_CONV : GAIN_CONV + 1] = jnp.sum(ds * h, axis=1, keepdims=True)
        e = ds * g
        dact[r, :] = e
        return a + fold8(e), b + fold8(e * h)

    sm_s[...] = jnp.zeros((CH, 128), F32)
    first, second = loop(CH // BLK, act_body, (zero8, zero8))
    put_tile(st_s.at[2], collapse(first), collapse(second))
    share(2)
    gather_send(act_all, 1)
    first, second = summed(2)

    def dconv_body(i, c):
        r = row_block(i, BLK)
        dcv_w[r, PAD : PAD + FR] = ((dact[r, :] - first - hatc[r, :] * second) * inv_c).astype(BF16)
        return c

    loop(CH // BLK, dconv_body, 0)
    halo_send(dcv_w, 1)
    gather_relay(act_all, 1)
    halo_wait(dcv_w, 1)

    def back_body(i, c):
        r = row_block(i, 16)
        w = dcv_w[r, :].astype(F32)
        taps = par_ref[r, 0:TAPS]
        u = glu_w[r, PAD : PAD + FR].astype(F32)
        acc = jnp.zeros((16, FR), F32)
        for k in range(TAPS):
            moved = pltpu.roll(w, (k - REACH) % WIDE, 1)[:, PAD : PAD + FR]
            acc = acc + taps[:, k : k + 1] * moved
            m = u * moved
            prod[k, r, :] = (m[:, 0:128] + m[:, 128:256]) + (m[:, 256:384] + m[:, 384:512])
        s = sig[r, :]
        dv = acc * s
        dv_b[r, :] = dv.astype(BF16)
        dg_b[r, :] = (dv * value[r, :] * (1.0 - s)).astype(BF16)
        return c

    lax.fori_loop(0, CH // 32, back_body, 0)
    gather_last(act_all, 1)
    lax.fori_loop(CH // 32, CH // 16, back_body, 0)

    other = pl.ds(pl.multiple_of((1 - core) * HALF, HALF), HALF)
    mine = pl.ds(pl.multiple_of(core * HALF, HALF), HALF)

    def pair_send(g):
        send(g16.at[g, other, :], c1.at[g], ("c1", g), mate)

    def weight_grad(g, left_ref, all_ref):
        g16[g] = contract_cols(left_ref[...], all_ref[...].reshape(D, FR)).astype(BF16)
        pair_send(g)

    weight_grad(0, dv_b, normed)
    weight_grad(1, dg_b, normed)
    gather_wait(act_all, 1)
    weight_grad(2, cot_ref, act_all)

    def dn_body(d, c):
        lanes = pl.ds(pl.multiple_of(d * (2 * CH), 128), 2 * CH)
        term = contract_rows(wv_ref[:, lanes], dv_b[...]) + contract_rows(wg_ref[:, lanes], dg_b[...])
        term = term.astype(BF16)
        dn_s[2 * d] = term[0:CH]
        dn_s[2 * d + 1] = term[CH : 2 * CH]
        return c

    loop(TP // 2, dn_body, 0)
    scatter_send(dn_s, 1)

    def z_block(zz):
        return (
            pl.ds(pl.multiple_of((zz // 4) * ZR, 16), ZR),
            pl.ds(pl.multiple_of(lax.rem(zz, 4) * ZL, 128), ZL),
        )

    def chains(g):
        sign = 1 if g % 2 == 0 else NZ - 1
        return ((0, 4, sign), (1, 3, NZ - sign))

    def z_start(g):
        arrived(c1.at[g], ("c1", g), mate)
        s16[g] = (g16[g, mine, :].astype(F32) + c1[g].astype(F32)).astype(BF16)
        z_hop(g, 1)

    def z_got(g, i, sign):
        arrived(zr.at[g, i], ("z", g, i), z_dev(sign))
        return zr[g, i].astype(F32)

    def z_hop(g, step):
        for chain, n, sign in chains(g):
            if step <= n:
                rr, ll = z_block(lax.rem(z + sign * (n + 1 - step), NZ))
                i = chain * 4 + step - 1
                if step > 1:
                    s16[g, rr, ll] = (s16[g, rr, ll].astype(F32) + z_got(g, i - 1, sign)).astype(BF16)
                send(s16.at[g, rr, ll], zr.at[g, i], ("z", g, i), z_dev(sign))

    def y_send(g):
        rr, ll = z_block(z)
        total = s16[g, rr, ll].astype(F32)
        for chain, n, sign in chains(g):
            total = total + z_got(g, chain * 4 + n - 1, sign)
        y16[g] = total.astype(BF16)
        yr[g, yh] = total.astype(BF16)
        for k in range(1, NY):
            send(y16.at[g], yr.at[g, yh], ("y", g, k - 1), y_dev(k))

    outs = (gval_out, ggate_out, gout_out)

    def out_block(zz, cc):
        rr, ll = z_block(zz)
        return pl.ds(pl.multiple_of(cc * HALF + (zz // 4) * ZR, 16), ZR), ll

    def w_start(g):
        for k in range(1, NY):
            arrived(yr.at[g, lax.rem(yh + NY - k, NY)], ("y", g, k - 1), y_dev(k))
        total = yr[g, 0].astype(F32)
        for j in range(1, NY):
            total = total + yr[g, j].astype(F32)
        r16[g] = (total * scale).astype(BF16)
        rr, ll = out_block(z, core)
        outs[g][rr, ll] = r16[g]
        for chain, n, sign in chains(g):
            send(r16.at[g], outs[g].at[rr, ll], ("w", g, chain * 4), z_dev(sign))
        send(r16.at[g], outs[g].at[rr, ll], ("f", g, 0), mate)

    def w_hop(g, step):
        for chain, n, sign in chains(g):
            if step <= n + 1:
                i = chain * 4 + step - 2
                rr, ll = out_block(lax.rem(z + (NZ - sign) * (step - 1), NZ), core)
                piece = outs[g].at[rr, ll]
                arrived(piece, ("w", g, i), z_dev(sign))
                if step <= n:
                    send(piece, piece, ("w", g, i + 1), z_dev(sign))
                send(piece, piece, ("f", g, 1 + i), mate)

    def f_wait(g):
        rr, ll = out_block(z, 1 - core)
        arrived(outs[g].at[rr, ll], ("f", g, 0), mate)
        for chain, n, sign in chains(g):
            for step in range(2, n + 2):
                rr, ll = out_block(lax.rem(z + (NZ - sign) * (step - 1), NZ), 1 - core)
                arrived(outs[g].at[rr, ll], ("f", g, 1 + chain * 4 + step - 2), mate)

    z_start(0)
    z_start(1)

    value[...] = jnp.dot(wo_ref[...], act_all[...].reshape(D, FR), preferred_element_type=F32)
    z_hop(0, 2)
    z_hop(1, 2)
    z_start(2)

    def out_body(i, c):
        r = row_block(i, BLK)
        block_out[r, :] = (x_ref[r, :].astype(F32) + value[r, :]).astype(BF16)
        return c

    loop(CH // BLK, out_body, 0)
    stores[0].start()
    scatter_relay(dn_s, 1)
    z_hop(0, 3)
    z_hop(1, 3)
    z_hop(2, 2)

    for k in range(TAPS):
        sm_s[:, k : k + 1] = jnp.sum(prod[k], axis=1, keepdims=True)

    scatter_last(dn_s, 1)
    z_hop(0, 4)
    z_hop(1, 4)
    z_hop(2, 3)
    y_send(0)
    y_send(1)
    z_hop(2, 4)
    scatter_wait(1)

    carry = (zero8, zero8)
    for h in range(2):

        def dnorm_body(j, carry):
            a, b = carry
            r = pl.ds(pl.multiple_of(h * HALF + j * BLK, BLK), BLK)
            total = scatter_sum(dn_s, 1, r, j, h)
            hat = hat_in[r, :]
            sm_s[r, GAIN_NORM : GAIN_NORM + 1] = jnp.sum(total * hat, axis=1, keepdims=True)
            e = total * par_ref[r, GAIN_NORM : GAIN_NORM + 1]
            dact[r, :] = e
            return a + fold8(e), b + fold8(e * hat)

        carry = loop(HALF // BLK, dnorm_body, carry)
    first, second = carry
    put_tile(st_s.at[3], collapse(first), collapse(second))
    share(3)
    send(sm_s, sm_c, ("sc", 0), mate)

    y_send(2)
    first, second = summed(3)

    def grad_body(i, c):
        r = row_block(i, BLK)
        back = (dact[r, :] - first - hat_in[r, :] * second) * inv_in
        input_grad[r, :] = (cot_ref[r, :].astype(F32) + back).astype(BF16)
        return c

    loop(CH // BLK, grad_body, 0)
    stores[1].start()

    arrived(sm_c, ("sc", 0), mate)
    sm_t[...] = sm_s[...] + sm_c[...]

    def sm_rows(zz):
        return pl.ds(pl.multiple_of(zz * SR, 8), SR)

    for k in range(1, NZ):
        send(sm_t.at[sm_rows(lax.rem(z + k, NZ)), :], sm_z.at[z], ("sz", k - 1), z_dev(k))
    sm_z[z] = sm_t[sm_rows(z), :]

    w_start(0)
    w_start(1)
    w_hop(0, 2)
    w_hop(1, 2)
    w_start(2)

    for k in range(1, NZ):
        arrived(sm_z.at[lax.rem(z + NZ - k, NZ)], ("sz", k - 1), z_dev(k))
    total = sm_z[0]
    for j in range(1, NZ):
        total = total + sm_z[j]
    sm_r[0] = total
    sm_y[yh] = total
    for k in range(1, NY):
        send(sm_r.at[0], sm_y.at[yh], ("sy", k - 1), y_dev(k))

    w_hop(0, 3)
    w_hop(1, 3)
    w_hop(2, 2)
    w_hop(0, 4)
    w_hop(1, 4)
    w_hop(2, 3)

    for k in range(1, NY):
        arrived(sm_y.at[lax.rem(yh + NY - k, NY)], ("sy", k - 1), y_dev(k))
    total = sm_y[0]
    for j in range(1, NY):
        total = total + sm_y[j]
    sm_r[1] = total * scale
    small_out[sm_rows(z), :] = total * scale
    for k in range(1, NZ):
        send(sm_r.at[1], small_out.at[sm_rows(z), :], ("sw", k - 1), z_dev(k))

    w_hop(0, 5)
    w_hop(1, 5)
    w_hop(2, 4)
    w_hop(2, 5)
    for k in range(1, NZ):
        arrived(small_out.at[sm_rows(lax.rem(z + NZ - k, NZ)), :], ("sw", k - 1), z_dev(k))
    stores[5].start()
    for g in range(3):
        f_wait(g)
        stores[2 + g].start()
    for copy in sends:
        copy.wait_send()
    for copy in stores:
        copy.wait()


def copy_out(*refs):
    ins, outs, stage, small, sem = refs[0:6], refs[6:14], refs[14:19], refs[19], refs[20]
    loads = [pltpu.make_async_copy(ins[i], stage[i], sem.at[i]) for i in range(5)]
    stores = [pltpu.make_async_copy(stage[i], outs[i], sem.at[5 + i]) for i in range(5)]
    last = pltpu.make_async_copy(ins[5], small, sem.at[10])
    for copy in loads + [last]:
        copy.start()
    for i in range(5):
        loads[i].wait()
        stores[i].start()
    last.wait()
    cols = jnp.concatenate([small[...], jnp.zeros((2 * 128 - CH, 128), F32)], axis=0).T
    outs[5][...] = cols[0:TAPS, 0:CH]
    outs[6][...] = cols[GAIN_CONV : GAIN_CONV + 1, 0:CH]
    outs[7][...] = cols[GAIN_NORM : GAIN_NORM + 1, 0:CH]
    for copy in stores:
        copy.wait()


def local(
    frames_in, norm_gain, value_weight, gate_weight, depth_kernel, conv_gain, out_weight, cotangent
):
    act = jax.ShapeDtypeStruct((CH, FR), BF16)
    mat = jax.ShapeDtypeStruct((CH, D), BF16)
    row = jax.ShapeDtypeStruct((1, CH), F32)
    vm = pltpu.VMEM
    dma = pltpu.SemaphoreType.DMA
    full = vm((CH, FR), F32)
    eight = vm((TP, CH, FR), BF16)
    wide = vm((CH, WIDE), BF16)
    block = vm((CH, FR), BF16)
    weight = vm((CH, D), BF16)
    small = vm((CH, 128), F32)
    line = vm((1, CH), F32)
    scratch = [block, block, weight, weight, weight, small]
    scratch += [block, line, weight, weight, vm((TAPS, CH), F32), line, weight, block, vm((128, 256), F32), small] + [full] * 6 + [eight] * 4
    scratch += [vm((2, 14, HALF, FR), BF16), wide, wide, block, block, vm((TAPS, CH, 128), F32)]
    scratch += [vm((4, 8, 128), F32), vm((4, TP, 8, 128), F32)]
    scratch += [
        vm((3, CH, D), BF16),
        vm((3, HALF, D), BF16),
        vm((3, HALF, D), BF16),
        vm((3, 8, ZR, ZL), BF16),
        vm((3, ZR, ZL), BF16),
        vm((3, NY, ZR, ZL), BF16),
        vm((3, ZR, ZL), BF16),
    ]
    scratch += [small, small, small, vm((NZ, SR, 128), F32), vm((NY, SR, 128), F32), vm((2, SR, 128), F32)]
    scratch += [dma((8,)), dma((6,))]
    for shape in ((4, 7), (2, 14), (2, 14), (2, 2), (3,), (3, 8), (3, 3), (3, 8), (3, 8), (1,), (7,), (3,), (7,)):
        scratch += [dma(shape), dma(shape)]
    vmem = pl.BlockSpec(memory_space=pltpu.VMEM)
    anywhere = pl.BlockSpec(memory_space=pl.ANY)
    results = pl.pallas_call(
        kernel,
        out_shape=(act, act, mat, mat, mat, jax.ShapeDtypeStruct((CH, 128), F32)),
        in_specs=[anywhere] * 8,
        out_specs=(anywhere,) * 6,
        scratch_shapes=scratch,
        compiler_params=pltpu.CompilerParams(
            collective_id=0, has_side_effects=True, vmem_limit_bytes=VMEM_LIMIT
        ),
    )(
        frames_in,
        norm_gain.reshape(1, CH),
        value_weight,
        gate_weight,
        depth_kernel.T,
        conv_gain.reshape(1, CH),
        out_weight,
        cotangent,
    )
    block_out, input_grad, gval, ggate, gout, gkernel, gconv, gnorm = pl.pallas_call(
        copy_out,
        out_shape=(act, act, mat, mat, mat, jax.ShapeDtypeStruct((TAPS, CH), F32), row, row),
        in_specs=[anywhere] * 6,
        out_specs=(anywhere,) * 5 + (vmem,) * 3,
        scratch_shapes=[block, block, weight, weight, weight, small, dma((11,))],
    )(*results)
    return (
        block_out,
        input_grad,
        gnorm.reshape(CH),
        gval,
        ggate,
        gkernel.T,
        gconv.reshape(CH),
        gout,
    )


def solution(mesh):
    return jax.shard_map(
        local,
        mesh=mesh,
        in_specs=(
            P("tp", "seq"),
            P("tp"),
            P("tp", None),
            P("tp", None),
            P("tp", None),
            P("tp"),
            P("tp", None),
            P("tp", "seq"),
        ),
        out_specs=(
            P("tp", "seq"),
            P("tp", "seq"),
            P("tp"),
            P("tp", None),
            P("tp", None),
            P("tp", None),
            P("tp"),
            P("tp", None),
        ),
        check_vma=False,
    )
```

```python
import functools

import jax
import jax.numpy as jnp
from jax import lax
from jax.experimental import pallas as pl
from jax.experimental.pallas import tpu as pltpu
from jax.sharding import PartitionSpec as P

EPS = 1e-05
F32 = jnp.float32
BF16 = jnp.bfloat16
MESH = pl.DeviceIdType.MESH

TP = 8
SEQ = 64
NZ = 8
NY = 4
CH = 192
FR = 512
D = CH * TP
TAPS = 32
REACH = TAPS // 2
PAD = 128
WIDE = FR + 2 * PAD
HALF = CH // 2
ZR = HALF // 2
ZL = D // 4
SR = CH // NZ
BLK = 32
VMEM_LIMIT = 63 * 1024 * 1024
GAIN_CONV = TAPS
GAIN_NORM = TAPS + 1


def fold8(v):
    out = v[0:8]
    for i in range(8, v.shape[0], 8):
        out = out + v[i : i + 8]
    return out


def row_block(i, blk):
    return pl.ds(pl.multiple_of(i * blk, blk), blk)


def put_tile(ref, a, b):
    for j in range(4):
        ref[j : j + 1, :] = a[:, 128 * j : 128 * j + 128]
        ref[4 + j : 5 + j, :] = b[:, 128 * j : 128 * j + 128]


def tile_row(t):
    return jnp.concatenate([t[j : j + 1] for j in range(4)], axis=1)


def kernel(
    x_hbm, ng_hbm, wv_hbm, wg_hbm, dk_hbm, cg_hbm, wo_hbm, cot_hbm,
    *rest,
):
    finals, landed, rest = rest[0:7], rest[7:14], rest[14:]
    block_out, input_grad, gval_out, ggate_out, gout_out, small_out, norm_out = landed
    (
        ng_ref, wv_ref, wg_ref, dk_ref, cg_ref, wo_ref, cot_ref, par_t, par_ref,
        hat_in, value, sig, conv, hatc, dact,
        x_all, gains_t, gains, st0_s, st0_r, normed, act_all, da_s, dn_s, rs_r,
        glu_w, dcv_w, dv_b, dg_b, prod,
        st_s, st_r,
        g16, c1, s16, zr, y16, yr, r16,
        ncol, nt_s, nt_z, nt_y, nt_c, sm_s, sm_c, sm_t, sm_z, sm_y, sm_r,
        ld, fin,
        st_ss, st_rs, ag_ss, ag_rs, rs_ss, rs_rs, ha_ss, ha_rs,
        c1_ss, c1_rs, z_ss, z_rs, y_ss, y_rs, w_ss, w_rs, f_ss, f_rs,
        nz_ss, nz_rs, ny_ss, ny_rs, nc_ss, nc_rs, sc_ss, sc_rs, sz_ss, sz_rs, sy_ss, sy_rs, sw_ss, sw_rs,
    ) = rest
    stores = [pltpu.make_async_copy(landed[i], finals[i], fin.at[i]) for i in range(7)]
    p = lax.axis_index("tp")
    fetch = (
        (x_hbm, x_all.at[p]), (dk_hbm, dk_ref), (cg_hbm, cg_ref), (ng_hbm, ng_ref),
        (wo_hbm, wo_ref), (cot_hbm, cot_ref), (wv_hbm, wv_ref), (wg_hbm, wg_ref),
    )
    loads = [pltpu.make_async_copy(src, dst, ld.at[i]) for i, (src, dst) in enumerate(fetch)]
    for copy in loads:
        copy.start()
    q = lax.axis_index("seq")
    core = lax.rem(q, 2)
    chip = q // 2
    z = lax.rem(chip, NZ)
    yh = chip // NZ
    scale = float(FR * SEQ) ** (-0.5)
    sends = []

    sems = {
        "st": (st_ss, st_rs), "ag": (ag_ss, ag_rs), "rs": (rs_ss, rs_rs), "ha": (ha_ss, ha_rs),
        "c1": (c1_ss, c1_rs), "z": (z_ss, z_rs), "y": (y_ss, y_rs), "w": (w_ss, w_rs), "f": (f_ss, f_rs),
        "nz": (nz_ss, nz_rs), "ny": (ny_ss, ny_rs), "nc": (nc_ss, nc_rs), "sc": (sc_ss, sc_rs), "sz": (sz_ss, sz_rs), "sy": (sy_ss, sy_rs), "sw": (sw_ss, sw_rs),
    }

    def remote(src, dst, key, dev):
        out, into = sems[key[0]]
        return pltpu.make_async_remote_copy(
            src_ref=src, dst_ref=dst, send_sem=out.at[key[1:]], recv_sem=into.at[key[1:]],
            device_id=dev, device_id_type=MESH,
        )

    def send(src, dst, key, dev):
        copy = remote(src, dst, key, dev)
        copy.start()
        sends.append(copy)

    def arrived(dst, key, dev):
        remote(dst, dst, key, dev).wait_recv()

    tx, ty = p // 2, lax.rem(p, 2)

    def at_tp(dx, dy):
        return lax.rem(tx + dx, 4) * 2 + lax.rem(ty + dy, 2)

    def hop(dx, dy):
        return {"tp": at_tp(dx, dy), "seq": q}

    def half(h):
        return pl.ds(h * HALF, HALF)

    def tp_dev(k):
        return {"tp": lax.rem(p + k, TP), "seq": q}

    def z_dev(k):
        return {"tp": p, "seq": (yh * NZ + lax.rem(z + k, NZ)) * 2 + core}

    def y_dev(k):
        return {"tp": p, "seq": (lax.rem(yh + k, NY) * NZ + z) * 2 + core}

    mate = {"tp": p, "seq": chip * 2 + (1 - core)}
    right = {"tp": p, "seq": lax.rem(q + 1, SEQ)}
    left = {"tp": p, "seq": lax.rem(q + SEQ - 1, SEQ)}

    barrier = pltpu.get_barrier_semaphore()
    peers = [tp_dev(k) for k in range(1, TP)] + [z_dev(k) for k in range(1, NZ)]
    peers += [y_dev(k) for k in range(1, NY)] + [mate, right, left]
    for dev in peers:
        pl.semaphore_signal(barrier, inc=1, device_id=dev, device_id_type=MESH)

    zero8 = jnp.zeros((8, FR), F32)

    def loop(n, body, init):
        return lax.fori_loop(0, n, body, init)

    def collapse(v):
        return jnp.sum(v, axis=0, keepdims=True)

    def local_moments(rows, tile):
        total = loop(CH // BLK, lambda i, a: a + fold8(rows(row_block(i, BLK))), zero8)
        mean = collapse(total) / CH

        def body(i, a):
            c = rows(row_block(i, BLK)) - mean
            return a + fold8(c * c)

        put_tile(tile, mean, collapse(loop(CH // BLK, body, zero8)))

    def share(slot):
        st_r[slot, p] = st_s[slot]
        for k in range(1, TP):
            send(st_s.at[slot], st_r.at[slot, p], ("st", slot, k - 1), tp_dev(k))

    def shared(slot):
        for k in range(1, TP):
            arrived(st_r.at[slot, lax.rem(p + TP - k, TP)], ("st", slot, k - 1), tp_dev(k))
        return [st_r[slot, j] for j in range(TP)]

    def merged(parts):
        total = parts[0]
        for t in parts[1:]:
            total = total + t
        mean = total[0:4] / TP
        spread = total[4:8]
        for t in parts:
            off = t[0:4] - mean
            spread = spread + CH * (off * off)
        inverse = lax.rsqrt(spread / D + EPS)
        return tile_row(mean), tile_row(inverse)

    def summed(slot):
        parts = shared(slot)
        total = parts[0]
        for t in parts[1:]:
            total = total + t
        return tile_row(total[0:4]) / D, tile_row(total[4:8]) / D

    RIGHT, LEFT, SIDE = (1, 0), (3, 0), (0, 1)

    gather_plan = (
        ((0, 0), 0, RIGHT), ((0, 0), 1, RIGHT), ((0, 0), 1, LEFT), ((0, 0), 0, LEFT),
        ((0, 0), 0, SIDE), ((0, 0), 1, SIDE), ((3, 0), 0, RIGHT), ((1, 0), 1, LEFT),
        ((0, 1), 0, RIGHT), ((0, 1), 0, LEFT), ((3, 0), 1, SIDE), ((1, 0), 1, SIDE),
        ((2, 0), 1, SIDE), ((3, 1), 0, RIGHT),
    )

    def gather_put(buf, n, i):
        (dx, dy), h, to = gather_plan[i]
        piece = buf.at[at_tp(dx, dy), half(h), :]
        send(piece, piece, ("ag", n, i), hop(*to))

    def gather_got(buf, n, i):
        (dx, dy), h, to = gather_plan[i]
        piece = buf.at[at_tp(dx + 4 - to[0], dy + to[1]), half(h), :]
        arrived(piece, ("ag", n, i), hop(*to))

    def gather_send(buf, n):
        for i in (0, 2, 4, 1, 3, 5):
            gather_put(buf, n, i)

    def gather_relay(buf, n):
        gather_got(buf, n, 4)
        gather_put(buf, n, 8)
        gather_got(buf, n, 2)
        gather_put(buf, n, 7)
        gather_put(buf, n, 11)
        gather_got(buf, n, 0)
        gather_put(buf, n, 6)
        gather_put(buf, n, 9)
        gather_got(buf, n, 1)
        gather_put(buf, n, 10)

    def gather_last(buf, n):
        gather_got(buf, n, 7)
        gather_put(buf, n, 12)
        gather_got(buf, n, 8)
        gather_put(buf, n, 13)

    def gather_wait(buf, n):
        for i in (3, 5, 6, 9, 10, 11, 12, 13):
            gather_got(buf, n, i)

    scatter_plan = (
        ((3, 0), 0, LEFT), ((3, 0), 1, LEFT), ((1, 0), 1, RIGHT), ((1, 0), 0, RIGHT),
        ((0, 1), 0, SIDE), ((0, 1), 1, SIDE), ((2, 0), 0, LEFT), ((2, 0), 1, RIGHT),
        ((3, 1), 0, LEFT), ((1, 1), 0, RIGHT), ((3, 1), 1, SIDE), ((1, 1), 1, SIDE),
        ((2, 1), 1, SIDE), ((2, 1), 0, LEFT),
    )

    def scatter_put(buf, n, i, merge=()):
        (dx, dy), h, to = scatter_plan[i]
        d = at_tp(dx, dy)
        for m in merge:
            arrived(rs_r.at[n, m], ("rs", n, m), hop(*scatter_plan[m][2]))
        if merge:

            def body(j, c):
                r = pl.ds(pl.multiple_of(h * HALF + j * BLK, BLK), BLK)
                total = buf[d, r, :].astype(F32)
                for m in merge:
                    total = total + rs_r[n, m, row_block(j, BLK), :].astype(F32)
                buf[d, r, :] = total.astype(BF16)
                return c

            loop(HALF // BLK, body, 0)
        send(buf.at[d, half(h), :], rs_r.at[n, i], ("rs", n, i), hop(*to))

    def scatter_send(buf, n):
        for i in (13, 12, 9, 6, 10, 3, 11, 5):
            scatter_put(buf, n, i)

    def scatter_relay(buf, n):
        scatter_put(buf, n, 8, (13,))
        scatter_put(buf, n, 7, (12,))
        scatter_put(buf, n, 0, (6,))
        scatter_put(buf, n, 1, (10,))

    def scatter_last(buf, n):
        scatter_put(buf, n, 4, (8, 9))
        scatter_put(buf, n, 2, (7, 11))

    def scatter_wait(n):
        for m in range(6):
            arrived(rs_r.at[n, m], ("rs", n, m), hop(*scatter_plan[m][2]))

    def scatter_sum(buf, n, r, j, h):
        total = buf[p, r, :].astype(F32)
        for m in ((0, 3, 4), (1, 2, 5))[h]:
            total = total + rs_r[n, m, row_block(j, BLK), :].astype(F32)
        return total

    def halo_send(buf, n):
        send(buf.at[:, PAD : 2 * PAD], buf.at[:, PAD + FR : WIDE], ("ha", n, 0), left)
        send(buf.at[:, FR : FR + PAD], buf.at[:, 0:PAD], ("ha", n, 1), right)

    def halo_wait(buf, n):
        arrived(buf.at[:, PAD + FR : WIDE], ("ha", n, 0), left)
        arrived(buf.at[:, 0:PAD], ("ha", n, 1), right)

        @pl.when(q == 0)
        def _():
            buf[:, 0:PAD] = jnp.zeros((CH, PAD), buf.dtype)

        @pl.when(q == SEQ - 1)
        def _():
            buf[:, PAD + FR : WIDE] = jnp.zeros((CH, PAD), buf.dtype)

    def contract_rows(w, v):
        return lax.dot_general(w, v, (((0,), (0,)), ((), ())), preferred_element_type=F32)

    def contract_cols(a, b):
        return lax.dot_general(a, b, (((1,), (1,)), ((), ())), preferred_element_type=F32)

    for copy in loads[0:4]:
        copy.wait()
    par_t[...] = jnp.zeros((128, 2 * 128), F32)
    par_t[0:TAPS, 0:CH] = dk_ref[...]
    par_t[GAIN_CONV : GAIN_CONV + 1, 0:CH] = cg_ref[...]
    par_t[GAIN_NORM : GAIN_NORM + 1, 0:CH] = ng_ref[...]
    par_ref[...] = par_t[...].T[0:CH]

    local_moments(lambda r: x_all[p, r, :].astype(F32), st0_s)
    st0_s[8:16, :] = jnp.zeros((8, 128), F32)
    st0_s[8:9, :] = par_t[GAIN_NORM : GAIN_NORM + 1, 0:128]
    st0_s[9:10, :] = par_t[GAIN_NORM : GAIN_NORM + 1, 128:256]
    pl.semaphore_wait(barrier, len(peers))
    st0_r[p] = st0_s[...]
    for k in range(1, TP):
        send(st0_s, st0_r.at[p], ("st", 0, k - 1), tp_dev(k))
    gather_send(x_all, 0)

    loads[4].wait()
    loads[5].wait()
    def dact_body(d, c):
        lanes = pl.ds(pl.multiple_of(d * (2 * CH), 128), 2 * CH)
        term = contract_rows(wo_ref[:, lanes], cot_ref[...]).astype(BF16)
        da_s[2 * d] = term[0:CH]
        da_s[2 * d + 1] = term[CH : 2 * CH]
        return c

    loop(TP // 2, dact_body, 0)
    gather_relay(x_all, 0)
    gather_last(x_all, 0)

    for k in range(1, TP):
        arrived(st0_r.at[lax.rem(p + TP - k, TP)], ("st", 0, k - 1), tp_dev(k))
    gains_t[...] = jnp.zeros((128, 256), F32)
    for j in range(TP):
        gains_t[j : j + 1, 0:128] = st0_r[j, 8:9, :]
        gains_t[j : j + 1, 128:256] = st0_r[j, 9:10, :]
    gains[...] = gains_t[...].T
    mean_in, inv_in = merged([st0_r[j] for j in range(TP)])

    def own_body(i, c):
        r = row_block(i, BLK)
        h = (x_all[p, r, :].astype(F32) - mean_in) * inv_in
        hat_in[r, :] = h
        normed[p, r, :] = (h * par_ref[r, GAIN_NORM : GAIN_NORM + 1]).astype(BF16)
        return c

    loop(CH // BLK, own_body, 0)
    scatter_send(da_s, 0)
    loads[6].wait()
    loads[7].wait()
    gather_wait(x_all, 0)
    for j in range(TP):

        @pl.when(p != j)
        def _():
            def body(i, c):
                r = row_block(i, BLK)
                h = (x_all[j, r, :].astype(F32) - mean_in) * inv_in
                normed[j, r, :] = (h * gains[r, j : j + 1]).astype(BF16)
                return c

            loop(CH // BLK, body, 0)

    everything = normed[...].reshape(D, FR)
    value[...] = jnp.dot(wv_ref[...], everything, preferred_element_type=F32)
    sig[...] = jnp.dot(wg_ref[...], everything, preferred_element_type=F32)

    def glu_body(i, c):
        r = row_block(i, BLK)
        s = jax.nn.sigmoid(sig[r, :])
        sig[r, :] = s
        glu_w[r, PAD : PAD + FR] = (value[r, :] * s).astype(BF16)
        return c

    loop(CH // BLK, glu_body, 0)
    halo_send(glu_w, 0)
    scatter_relay(da_s, 0)
    halo_wait(glu_w, 0)

    def conv_body(i, c):
        r = row_block(i, 16)
        w = glu_w[r, :].astype(F32)
        taps = par_ref[r, 0:TAPS]
        acc = jnp.zeros((16, FR), F32)
        for k in range(TAPS):
            acc = acc + taps[:, k : k + 1] * pltpu.roll(w, (REACH - k) % WIDE, 1)[:, PAD : PAD + FR]
        conv[r, :] = acc
        return c

    lax.fori_loop(0, CH // 32, conv_body, 0)
    scatter_last(da_s, 0)
    lax.fori_loop(CH // 32, CH // 16, conv_body, 0)
    local_moments(lambda r: conv[r, :], st_s.at[1])
    share(1)

    scatter_wait(0)
    for h in range(2):

        def dsum_body(j, c):
            r = pl.ds(pl.multiple_of(h * HALF + j * BLK, BLK), BLK)
            dact[r, :] = scatter_sum(da_s, 0, r, j, h)
            return c

        loop(HALF // BLK, dsum_body, 0)
    mean_c, inv_c = merged(shared(1))

    def act_body(i, carry):
        a, b = carry
        r = row_block(i, BLK)
        h = (conv[r, :] - mean_c) * inv_c
        hatc[r, :] = h
        g = par_ref[r, GAIN_CONV : GAIN_CONV + 1]
        scaled = h * g
        s = jax.nn.sigmoid(scaled)
        act_all[p, r, :] = (scaled * s).astype(BF16)
        ds = dact[r, :] * (s + scaled * s * (1.0 - s))
        sm_s[r, GAIN_CONV : GAIN_CONV + 1] = jnp.sum(ds * h, axis=1, keepdims=True)
        e = ds * g
        dact[r, :] = e
        return a + fold8(e), b + fold8(e * h)

    sm_s[...] = jnp.zeros((CH, 128), F32)
    first, second = loop(CH // BLK, act_body, (zero8, zero8))
    put_tile(st_s.at[2], collapse(first), collapse(second))
    share(2)
    gather_send(act_all, 1)
    first, second = summed(2)

    def dconv_body(i, c):
        r = row_block(i, BLK)
        dcv_w[r, PAD : PAD + FR] = ((dact[r, :] - first - hatc[r, :] * second) * inv_c).astype(BF16)
        return c

    loop(CH // BLK, dconv_body, 0)
    halo_send(dcv_w, 1)
    gather_relay(act_all, 1)
    halo_wait(dcv_w, 1)

    def back_body(i, c):
        r = row_block(i, 16)
        w = dcv_w[r, :].astype(F32)
        taps = par_ref[r, 0:TAPS]
        u = glu_w[r, PAD : PAD + FR].astype(F32)
        acc = jnp.zeros((16, FR), F32)
        for k in range(TAPS):
            moved = pltpu.roll(w, (k - REACH) % WIDE, 1)[:, PAD : PAD + FR]
            acc = acc + taps[:, k : k + 1] * moved
            m = u * moved
            prod[k, r, :] = (m[:, 0:128] + m[:, 128:256]) + (m[:, 256:384] + m[:, 384:512])
        s = sig[r, :]
        dv = acc * s
        dv_b[r, :] = dv.astype(BF16)
        dg_b[r, :] = (dv * value[r, :] * (1.0 - s)).astype(BF16)
        return c

    lax.fori_loop(0, CH // 32, back_body, 0)
    gather_last(act_all, 1)
    lax.fori_loop(CH // 32, CH // 16, back_body, 0)

    other = pl.ds(pl.multiple_of((1 - core) * HALF, HALF), HALF)
    mine = pl.ds(pl.multiple_of(core * HALF, HALF), HALF)

    def pair_send(g):
        send(g16.at[g, other, :], c1.at[g], ("c1", g), mate)

    def weight_grad(g, left_ref, all_ref):
        g16[g] = contract_cols(left_ref[...], all_ref[...].reshape(D, FR)).astype(BF16)
        pair_send(g)

    weight_grad(0, dv_b, normed)
    weight_grad(1, dg_b, normed)

    def dn_pair(dx, entries):
        xx = lax.rem(tx + dx, 4)
        lanes = pl.ds(pl.multiple_of(xx * (2 * CH), 128), 2 * CH)
        term = contract_rows(wv_ref[:, lanes], dv_b[...]) + contract_rows(wg_ref[:, lanes], dg_b[...])
        term = term.astype(BF16)
        dn_s[2 * xx] = term[0:CH]
        dn_s[2 * xx + 1] = term[CH : 2 * CH]
        for i in entries:
            scatter_put(dn_s, 1, i)

    def z_block(zz):
        return (
            pl.ds(pl.multiple_of((zz // 4) * ZR, 16), ZR),
            pl.ds(pl.multiple_of(lax.rem(zz, 4) * ZL, 128), ZL),
        )

    def chains(g):
        sign = 1 if g % 2 == 0 else NZ - 1
        return ((0, 4, sign), (1, 3, NZ - sign))

    def z_start(g):
        arrived(c1.at[g], ("c1", g), mate)
        s16[g] = (g16[g, mine, :].astype(F32) + c1[g].astype(F32)).astype(BF16)
        z_hop(g, 1)

    def z_got(g, i, sign):
        arrived(zr.at[g, i], ("z", g, i), z_dev(sign))
        return zr[g, i].astype(F32)

    def z_hop(g, step):
        for chain, n, sign in chains(g):
            if step <= n:
                rr, ll = z_block(lax.rem(z + sign * (n + 1 - step), NZ))
                i = chain * 4 + step - 1
                if step > 1:
                    s16[g, rr, ll] = (s16[g, rr, ll].astype(F32) + z_got(g, i - 1, sign)).astype(BF16)
                send(s16.at[g, rr, ll], zr.at[g, i], ("z", g, i), z_dev(sign))

    def y_send(g):
        rr, ll = z_block(z)
        total = s16[g, rr, ll].astype(F32)
        for chain, n, sign in chains(g):
            total = total + z_got(g, chain * 4 + n - 1, sign)
        y16[g] = total.astype(BF16)
        yr[g, yh] = total.astype(BF16)
        for k in range(1, NY):
            send(y16.at[g], yr.at[g, yh], ("y", g, k - 1), y_dev(k))

    outs = (gval_out, ggate_out, gout_out)

    def out_block(zz, cc):
        rr, ll = z_block(zz)
        return pl.ds(pl.multiple_of(cc * HALF + (zz // 4) * ZR, 16), ZR), ll

    def w_start(g):
        for k in range(1, NY):
            arrived(yr.at[g, lax.rem(yh + NY - k, NY)], ("y", g, k - 1), y_dev(k))
        total = yr[g, 0].astype(F32)
        for j in range(1, NY):
            total = total + yr[g, j].astype(F32)
        r16[g] = (total * scale).astype(BF16)
        rr, ll = out_block(z, core)
        outs[g][rr, ll] = r16[g]
        for chain, n, sign in chains(g):
            send(r16.at[g], outs[g].at[rr, ll], ("w", g, chain * 4), z_dev(sign))
        send(r16.at[g], outs[g].at[rr, ll], ("f", g, 0), mate)

    def w_hop(g, step):
        for chain, n, sign in chains(g):
            if step <= n + 1:
                i = chain * 4 + step - 2
                rr, ll = out_block(lax.rem(z + (NZ - sign) * (step - 1), NZ), core)
                piece = outs[g].at[rr, ll]
                arrived(piece, ("w", g, i), z_dev(sign))
                if step <= n:
                    send(piece, piece, ("w", g, i + 1), z_dev(sign))
                send(piece, piece, ("f", g, 1 + i), mate)

    def f_wait(g):
        rr, ll = out_block(z, 1 - core)
        arrived(outs[g].at[rr, ll], ("f", g, 0), mate)
        for chain, n, sign in chains(g):
            for step in range(2, n + 2):
                rr, ll = out_block(lax.rem(z + (NZ - sign) * (step - 1), NZ), 1 - core)
                arrived(outs[g].at[rr, ll], ("f", g, 1 + chain * 4 + step - 2), mate)

    dn_pair(2, (13, 12, 6))
    dn_pair(1, (9, 3, 11))
    z_start(0)
    z_start(1)
    dn_pair(3, (10,))
    dn_pair(0, (5,))
    gather_wait(act_all, 1)
    weight_grad(2, cot_ref, act_all)
    z_hop(0, 2)
    z_hop(1, 2)
    scatter_relay(dn_s, 1)
    z_start(2)

    for k in range(TAPS):
        sm_s[:, k : k + 1] = jnp.sum(prod[k], axis=1, keepdims=True)
    send(sm_s, sm_c, ("sc", 0), mate)

    z_hop(0, 3)
    z_hop(1, 3)
    scatter_last(dn_s, 1)
    z_hop(2, 2)

    value[...] = jnp.dot(wo_ref[...], act_all[...].reshape(D, FR), preferred_element_type=F32)

    def out_body(i, c):
        r = row_block(i, BLK)
        block_out[r, :] = (x_all[p, r, :].astype(F32) + value[r, :]).astype(BF16)
        return c

    z_hop(0, 4)
    z_hop(1, 4)
    loop(CH // BLK, out_body, 0)
    stores[0].start()
    z_hop(2, 3)

    arrived(sm_c, ("sc", 0), mate)
    sm_t[...] = sm_s[...] + sm_c[...]

    def sm_rows(zz):
        return pl.ds(pl.multiple_of(zz * SR, 8), SR)

    for k in range(1, NZ):
        send(sm_t.at[sm_rows(lax.rem(z + k, NZ)), :], sm_z.at[z], ("sz", k - 1), z_dev(k))
    sm_z[z] = sm_t[sm_rows(z), :]

    y_send(0)
    y_send(1)
    z_hop(2, 4)
    ncol[...] = jnp.zeros((256, 128), F32)
    scatter_wait(1)

    carry = (zero8, zero8)
    for h in range(2):

        def dnorm_body(j, carry):
            a, b = carry
            r = pl.ds(pl.multiple_of(h * HALF + j * BLK, BLK), BLK)
            total = scatter_sum(dn_s, 1, r, j, h)
            hat = hat_in[r, :]
            ncol[r, 0:1] = jnp.sum(total * hat, axis=1, keepdims=True)
            e = total * par_ref[r, GAIN_NORM : GAIN_NORM + 1]
            dact[r, :] = e
            return a + fold8(e), b + fold8(e * hat)

        carry = loop(HALF // BLK, dnorm_body, carry)
    first, second = carry
    put_tile(st_s.at[3], collapse(first), collapse(second))
    share(3)

    def all_sum(buf, count):
        total = buf[0]
        for j in range(1, count):
            total = total + buf[j]
        return total

    flat = ncol[...].T
    nt_s[0] = jnp.zeros((8, 128), F32)
    nt_s[0, 0:1] = flat[0:1, 0:128]
    nt_s[0, 1:2] = flat[0:1, 128:256]
    nt_z[z] = nt_s[0]
    for k in range(1, NZ):
        send(nt_s.at[0], nt_z.at[z], ("nz", k - 1), z_dev(k))
    y_send(2)

    for k in range(1, NZ):
        arrived(sm_z.at[lax.rem(z + NZ - k, NZ)], ("sz", k - 1), z_dev(k))
    total = all_sum(sm_z, NZ)
    sm_r[0] = total
    sm_y[yh] = total
    for k in range(1, NY):
        send(sm_r.at[0], sm_y.at[yh], ("sy", k - 1), y_dev(k))

    w_start(0)
    w_start(1)
    first, second = summed(3)

    def grad_body(i, c):
        r = row_block(i, BLK)
        back = (dact[r, :] - first - hat_in[r, :] * second) * inv_in
        input_grad[r, :] = (cot_ref[r, :].astype(F32) + back).astype(BF16)
        return c

    loop(CH // BLK, grad_body, 0)
    stores[1].start()

    for k in range(1, NZ):
        arrived(nt_z.at[lax.rem(z + NZ - k, NZ)], ("nz", k - 1), z_dev(k))
    nt_s[1] = all_sum(nt_z, NZ)
    nt_y[yh] = nt_s[1]
    for k in range(1, NY):
        send(nt_s.at[1], nt_y.at[yh], ("ny", k - 1), y_dev(k))

    w_hop(0, 2)
    w_hop(1, 2)
    w_start(2)

    for k in range(1, NY):
        arrived(sm_y.at[lax.rem(yh + NY - k, NY)], ("sy", k - 1), y_dev(k))
    total = all_sum(sm_y, NY)
    sm_r[1] = total * scale
    small_out[sm_rows(z), :] = total * scale
    for k in range(1, NZ):
        send(sm_r.at[1], small_out.at[sm_rows(z), :], ("sw", k - 1), z_dev(k))

    w_hop(0, 3)
    w_hop(1, 3)
    w_hop(2, 2)

    for k in range(1, NY):
        arrived(nt_y.at[lax.rem(yh + NY - k, NY)], ("ny", k - 1), y_dev(k))
    nt_s[2] = all_sum(nt_y, NY)
    send(nt_s.at[2], nt_c, ("nc", 0), mate)

    w_hop(0, 4)
    w_hop(1, 4)
    w_hop(2, 3)
    w_hop(0, 5)
    w_hop(1, 5)
    w_hop(2, 4)
    w_hop(2, 5)
    for k in range(1, NZ):
        arrived(small_out.at[sm_rows(lax.rem(z + NZ - k, NZ)), :], ("sw", k - 1), z_dev(k))
    stores[5].start()
    arrived(nt_c, ("nc", 0), mate)
    norm_out[...] = (nt_s[2] + nt_c[...]) * scale
    stores[6].start()
    for g in range(3):
        f_wait(g)
        stores[2 + g].start()
    for copy in sends:
        copy.wait_send()
    for copy in stores:
        copy.wait()


def copy_out(*refs):
    ins, outs, stage, small, norm, sem = refs[0:7], refs[7:15], refs[15:20], refs[20], refs[21], refs[22]
    loads = [pltpu.make_async_copy(ins[i], stage[i], sem.at[i]) for i in range(5)]
    stores = [pltpu.make_async_copy(stage[i], outs[i], sem.at[5 + i]) for i in range(5)]
    last = [pltpu.make_async_copy(ins[5], small, sem.at[10]), pltpu.make_async_copy(ins[6], norm, sem.at[11])]
    for copy in last + loads:
        copy.start()
    for copy in last:
        copy.wait()
    outs[7][:, 0:128] = norm[0:1, :]
    outs[7][:, 128:CH] = norm[1:2, 0 : CH - 128]
    for i in range(5):
        loads[i].wait()
        stores[i].start()
    cols = jnp.concatenate([small[...], jnp.zeros((2 * 128 - CH, 128), F32)], axis=0).T
    outs[5][...] = cols[0:TAPS, 0:CH]
    outs[6][...] = cols[GAIN_CONV : GAIN_CONV + 1, 0:CH]
    for copy in stores:
        copy.wait()


def local(
    frames_in, norm_gain, value_weight, gate_weight, depth_kernel, conv_gain, out_weight, cotangent
):
    act = jax.ShapeDtypeStruct((CH, FR), BF16)
    mat = jax.ShapeDtypeStruct((CH, D), BF16)
    row = jax.ShapeDtypeStruct((1, CH), F32)
    vm = pltpu.VMEM
    dma = pltpu.SemaphoreType.DMA
    full = vm((CH, FR), F32)
    eight = vm((TP, CH, FR), BF16)
    wide = vm((CH, WIDE), BF16)
    block = vm((CH, FR), BF16)
    weight = vm((CH, D), BF16)
    small = vm((CH, 128), F32)
    line = vm((1, CH), F32)
    tile = vm((8, 128), F32)
    scratch = [block, block, weight, weight, weight, small, tile]
    scratch += [line, weight, weight, vm((TAPS, CH), F32), line, weight, block, vm((128, 256), F32), small] + [full] * 6
    scratch += [eight, vm((128, 256), F32), vm((256, 128), F32), vm((16, 128), F32), vm((TP, 16, 128), F32)]
    scratch += [eight] * 4
    scratch += [vm((2, 14, HALF, FR), BF16), wide, wide, block, block, vm((TAPS, CH, 128), F32)]
    scratch += [vm((4, 8, 128), F32), vm((4, TP, 8, 128), F32)]
    scratch += [
        vm((3, CH, D), BF16),
        vm((3, HALF, D), BF16),
        vm((3, HALF, D), BF16),
        vm((3, 8, ZR, ZL), BF16),
        vm((3, ZR, ZL), BF16),
        vm((3, NY, ZR, ZL), BF16),
        vm((3, ZR, ZL), BF16),
    ]
    scratch += [vm((256, 128), F32), vm((3, 8, 128), F32), vm((NZ, 8, 128), F32), vm((NY, 8, 128), F32), tile]
    scratch += [small, small, small, vm((NZ, SR, 128), F32), vm((NY, SR, 128), F32), vm((2, SR, 128), F32)]
    scratch += [dma((8,)), dma((7,))]
    for shape in ((4, 7), (2, 14), (2, 14), (2, 2), (3,), (3, 8), (3, 3), (3, 8), (3, 8), (7,), (3,), (1,), (1,), (7,), (3,), (7,)):
        scratch += [dma(shape), dma(shape)]
    vmem = pl.BlockSpec(memory_space=pltpu.VMEM)
    anywhere = pl.BlockSpec(memory_space=pl.ANY)
    results = pl.pallas_call(
        kernel,
        out_shape=(act, act, mat, mat, mat, jax.ShapeDtypeStruct((CH, 128), F32), jax.ShapeDtypeStruct((8, 128), F32)),
        in_specs=[anywhere] * 8,
        out_specs=(anywhere,) * 7,
        scratch_shapes=scratch,
        compiler_params=pltpu.CompilerParams(
            collective_id=0, has_side_effects=True, vmem_limit_bytes=VMEM_LIMIT
        ),
    )(
        frames_in,
        norm_gain.reshape(1, CH),
        value_weight,
        gate_weight,
        depth_kernel.T,
        conv_gain.reshape(1, CH),
        out_weight,
        cotangent,
    )
    block_out, input_grad, gval, ggate, gout, gkernel, gconv, gnorm = pl.pallas_call(
        copy_out,
        out_shape=(act, act, mat, mat, mat, jax.ShapeDtypeStruct((TAPS, CH), F32), row, row),
        in_specs=[anywhere] * 7,
        out_specs=(anywhere,) * 5 + (vmem,) * 3,
        scratch_shapes=[block, block, weight, weight, weight, small, tile, dma((12,))],
    )(*results)
    return (
        block_out,
        input_grad,
        gnorm.reshape(CH),
        gval,
        ggate,
        gkernel.T,
        gconv.reshape(CH),
        gout,
    )


def solution(mesh):
    return jax.shard_map(
        local,
        mesh=mesh,
        in_specs=(
            P("tp", "seq"),
            P("tp"),
            P("tp", None),
            P("tp", None),
            P("tp", None),
            P("tp"),
            P("tp", None),
            P("tp", "seq"),
        ),
        out_specs=(
            P("tp", "seq"),
            P("tp", "seq"),
            P("tp"),
            P("tp", None),
            P("tp", None),
            P("tp", None),
            P("tp"),
            P("tp", None),
        ),
        check_vma=False,
    )
```

```python
import functools

import jax
import jax.numpy as jnp
from jax import lax
from jax.experimental import pallas as pl
from jax.experimental.pallas import tpu as pltpu
from jax.sharding import PartitionSpec as P

EPS = 1e-05
F32 = jnp.float32
BF16 = jnp.bfloat16
MESH = pl.DeviceIdType.MESH

TP = 8
SEQ = 64
NZ = 8
NY = 4
CH = 192
FR = 512
D = CH * TP
TAPS = 32
REACH = TAPS // 2
PAD = 128
WIDE = FR + 2 * PAD
HALF = CH // 2
ZR = HALF // 2
ZL = D // 4
SR = CH // NZ
BLK = 32
VMEM_LIMIT = 63 * 1024 * 1024
GAIN_CONV = TAPS
GAIN_NORM = TAPS + 1


def fold8(v):
    out = v[0:8]
    for i in range(8, v.shape[0], 8):
        out = out + v[i : i + 8]
    return out


def row_block(i, blk):
    return pl.ds(pl.multiple_of(i * blk, blk), blk)


def put_tile(ref, a, b):
    for j in range(4):
        ref[j : j + 1, :] = a[:, 128 * j : 128 * j + 128]
        ref[4 + j : 5 + j, :] = b[:, 128 * j : 128 * j + 128]


def tile_row(t):
    return jnp.concatenate([t[j : j + 1] for j in range(4)], axis=1)


def kernel(
    x_hbm, ng_hbm, wv_hbm, wg_hbm, dk_hbm, cg_hbm, wo_hbm, cot_hbm,
    *rest,
):
    finals, landed, rest = rest[0:7], rest[7:14], rest[14:]
    block_out, input_grad, gval_out, ggate_out, gout_out, small_out, norm_out = landed
    (
        ng_ref, wv_ref, wg_ref, dk_ref, cg_ref, wo_ref, cot_ref, par_t, par_ref,
        hat_in, value, sig, conv, hatc, dact,
        x_all, gains_t, gains, st0_s, st0_r, normed, act_all, da_s, dn_s, rs_r,
        glu_w, dcv_w, dv_b, dg_b, prod,
        st_s, st_r,
        g16, c1, s16, zr, y16, yr, r16,
        ncol, nt_s, nt_z, nt_y, nt_c, sm_s, sm_c, sm_t, sm_z, sm_y, sm_r,
        ld, fin,
        st_ss, st_rs, ag_ss, ag_rs, rs_ss, rs_rs, ha_ss, ha_rs,
        c1_ss, c1_rs, z_ss, z_rs, y_ss, y_rs, w_ss, w_rs, f_ss, f_rs,
        nz_ss, nz_rs, ny_ss, ny_rs, nc_ss, nc_rs, sc_ss, sc_rs, sz_ss, sz_rs, sy_ss, sy_rs, sw_ss, sw_rs,
    ) = rest
    stores = [pltpu.make_async_copy(landed[i], finals[i], fin.at[i]) for i in range(7)]
    p = lax.axis_index("tp")
    fetch = (
        (x_hbm, x_all.at[p]), (dk_hbm, dk_ref), (cg_hbm, cg_ref), (ng_hbm, ng_ref),
        (wo_hbm, wo_ref), (cot_hbm, cot_ref), (wv_hbm, wv_ref), (wg_hbm, wg_ref),
    )
    loads = [pltpu.make_async_copy(src, dst, ld.at[i]) for i, (src, dst) in enumerate(fetch)]
    for copy in loads:
        copy.start()
    q = lax.axis_index("seq")
    core = lax.rem(q, 2)
    chip = q // 2
    z = lax.rem(chip, NZ)
    yh = chip // NZ
    scale = float(FR * SEQ) ** (-0.5)
    sends = []

    sems = {
        "st": (st_ss, st_rs), "ag": (ag_ss, ag_rs), "rs": (rs_ss, rs_rs), "ha": (ha_ss, ha_rs),
        "c1": (c1_ss, c1_rs), "z": (z_ss, z_rs), "y": (y_ss, y_rs), "w": (w_ss, w_rs), "f": (f_ss, f_rs),
        "nz": (nz_ss, nz_rs), "ny": (ny_ss, ny_rs), "nc": (nc_ss, nc_rs), "sc": (sc_ss, sc_rs), "sz": (sz_ss, sz_rs), "sy": (sy_ss, sy_rs), "sw": (sw_ss, sw_rs),
    }

    def remote(src, dst, key, dev):
        out, into = sems[key[0]]
        return pltpu.make_async_remote_copy(
            src_ref=src, dst_ref=dst, send_sem=out.at[key[1:]], recv_sem=into.at[key[1:]],
            device_id=dev, device_id_type=MESH,
        )

    def send(src, dst, key, dev):
        copy = remote(src, dst, key, dev)
        copy.start()
        sends.append(copy)

    def arrived(dst, key, dev):
        remote(dst, dst, key, dev).wait_recv()

    tx, ty = p // 2, lax.rem(p, 2)

    def at_tp(dx, dy):
        return lax.rem(tx + dx, 4) * 2 + lax.rem(ty + dy, 2)

    def hop(dx, dy):
        return {"tp": at_tp(dx, dy), "seq": q}

    def half(h):
        return pl.ds(h * HALF, HALF)

    def tp_dev(k):
        return {"tp": lax.rem(p + k, TP), "seq": q}

    def z_dev(k):
        return {"tp": p, "seq": (yh * NZ + lax.rem(z + k, NZ)) * 2 + core}

    def y_dev(k):
        return {"tp": p, "seq": (lax.rem(yh + k, NY) * NZ + z) * 2 + core}

    mate = {"tp": p, "seq": chip * 2 + (1 - core)}
    right = {"tp": p, "seq": lax.rem(q + 1, SEQ)}
    left = {"tp": p, "seq": lax.rem(q + SEQ - 1, SEQ)}

    barrier = pltpu.get_barrier_semaphore()
    peers = [tp_dev(k) for k in range(1, TP)] + [z_dev(k) for k in range(1, NZ)]
    peers += [y_dev(k) for k in range(1, NY)] + [mate, right, left]
    for dev in peers:
        pl.semaphore_signal(barrier, inc=1, device_id=dev, device_id_type=MESH)

    zero8 = jnp.zeros((8, FR), F32)

    def loop(n, body, init):
        return lax.fori_loop(0, n, body, init)

    def collapse(v):
        return jnp.sum(v, axis=0, keepdims=True)

    def local_moments(rows, tile):
        total = loop(CH // BLK, lambda i, a: a + fold8(rows(row_block(i, BLK))), zero8)
        mean = collapse(total) / CH

        def body(i, a):
            c = rows(row_block(i, BLK)) - mean
            return a + fold8(c * c)

        put_tile(tile, mean, collapse(loop(CH // BLK, body, zero8)))

    def share(slot):
        st_r[slot, p] = st_s[slot]
        for k in range(1, TP):
            send(st_s.at[slot], st_r.at[slot, p], ("st", slot, k - 1), tp_dev(k))

    def shared(slot):
        for k in range(1, TP):
            arrived(st_r.at[slot, lax.rem(p + TP - k, TP)], ("st", slot, k - 1), tp_dev(k))
        return [st_r[slot, j] for j in range(TP)]

    def merged(parts):
        total = parts[0]
        for t in parts[1:]:
            total = total + t
        mean = total[0:4] / TP
        spread = total[4:8]
        for t in parts:
            off = t[0:4] - mean
            spread = spread + CH * (off * off)
        inverse = lax.rsqrt(spread / D + EPS)
        return tile_row(mean), tile_row(inverse)

    def summed(slot):
        parts = shared(slot)
        total = parts[0]
        for t in parts[1:]:
            total = total + t
        return tile_row(total[0:4]) / D, tile_row(total[4:8]) / D

    RIGHT, LEFT, SIDE = (1, 0), (3, 0), (0, 1)

    gather_plan = (
        ((0, 0), 0, RIGHT), ((0, 0), 1, RIGHT), ((0, 0), 1, LEFT), ((0, 0), 0, LEFT),
        ((0, 0), 0, SIDE), ((0, 0), 1, SIDE), ((3, 0), 0, RIGHT), ((1, 0), 1, LEFT),
        ((0, 1), 0, RIGHT), ((0, 1), 0, LEFT), ((3, 0), 1, SIDE), ((1, 0), 1, SIDE),
        ((2, 0), 1, SIDE), ((3, 1), 0, RIGHT),
    )

    def gather_put(buf, n, i):
        (dx, dy), h, to = gather_plan[i]
        piece = buf.at[at_tp(dx, dy), half(h), :]
        send(piece, piece, ("ag", n, i), hop(*to))

    def gather_got(buf, n, i):
        (dx, dy), h, to = gather_plan[i]
        piece = buf.at[at_tp(dx + 4 - to[0], dy + to[1]), half(h), :]
        arrived(piece, ("ag", n, i), hop(*to))

    def gather_send(buf, n):
        for i in (0, 2, 4, 1, 3, 5):
            gather_put(buf, n, i)

    def gather_relay(buf, n):
        gather_got(buf, n, 4)
        gather_put(buf, n, 8)
        gather_got(buf, n, 2)
        gather_put(buf, n, 7)
        gather_put(buf, n, 11)
        gather_got(buf, n, 0)
        gather_put(buf, n, 6)
        gather_put(buf, n, 9)
        gather_got(buf, n, 1)
        gather_put(buf, n, 10)

    def gather_last(buf, n):
        gather_got(buf, n, 7)
        gather_put(buf, n, 12)
        gather_got(buf, n, 8)
        gather_put(buf, n, 13)

    def gather_wait(buf, n):
        for i in (3, 5, 6, 9, 10, 11, 12, 13):
            gather_got(buf, n, i)

    scatter_plan = (
        ((3, 0), 0, LEFT), ((3, 0), 1, LEFT), ((1, 0), 1, RIGHT), ((1, 0), 0, RIGHT),
        ((0, 1), 0, SIDE), ((0, 1), 1, SIDE), ((2, 0), 0, LEFT), ((2, 0), 1, RIGHT),
        ((3, 1), 0, LEFT), ((1, 1), 0, RIGHT), ((3, 1), 1, SIDE), ((1, 1), 1, SIDE),
        ((2, 1), 1, SIDE), ((2, 1), 0, LEFT),
    )

    def scatter_put(buf, n, i, merge=()):
        (dx, dy), h, to = scatter_plan[i]
        d = at_tp(dx, dy)
        for m in merge:
            arrived(rs_r.at[n, m], ("rs", n, m), hop(*scatter_plan[m][2]))
        if merge:

            def body(j, c):
                r = pl.ds(pl.multiple_of(h * HALF + j * BLK, BLK), BLK)
                total = buf[d, r, :].astype(F32)
                for m in merge:
                    total = total + rs_r[n, m, row_block(j, BLK), :].astype(F32)
                buf[d, r, :] = total.astype(BF16)
                return c

            loop(HALF // BLK, body, 0)
        send(buf.at[d, half(h), :], rs_r.at[n, i], ("rs", n, i), hop(*to))

    def scatter_send(buf, n):
        for i in (13, 12, 9, 6, 10, 3, 11, 5):
            scatter_put(buf, n, i)

    def scatter_relay(buf, n):
        scatter_put(buf, n, 8, (13,))
        scatter_put(buf, n, 7, (12,))
        scatter_put(buf, n, 0, (6,))
        scatter_put(buf, n, 1, (10,))

    def scatter_last(buf, n):
        scatter_put(buf, n, 4, (8, 9))
        scatter_put(buf, n, 2, (7, 11))

    def scatter_wait(n):
        for m in range(6):
            arrived(rs_r.at[n, m], ("rs", n, m), hop(*scatter_plan[m][2]))

    def scatter_sum(buf, n, r, j, h):
        total = buf[p, r, :].astype(F32)
        for m in ((0, 3, 4), (1, 2, 5))[h]:
            total = total + rs_r[n, m, row_block(j, BLK), :].astype(F32)
        return total

    def halo_send(buf, n):
        send(buf.at[:, PAD : 2 * PAD], buf.at[:, PAD + FR : WIDE], ("ha", n, 0), left)
        send(buf.at[:, FR : FR + PAD], buf.at[:, 0:PAD], ("ha", n, 1), right)

    def halo_wait(buf, n):
        arrived(buf.at[:, PAD + FR : WIDE], ("ha", n, 0), left)
        arrived(buf.at[:, 0:PAD], ("ha", n, 1), right)

        @pl.when(q == 0)
        def _():
            buf[:, 0:PAD] = jnp.zeros((CH, PAD), buf.dtype)

        @pl.when(q == SEQ - 1)
        def _():
            buf[:, PAD + FR : WIDE] = jnp.zeros((CH, PAD), buf.dtype)

    def contract_rows(w, v):
        return lax.dot_general(w, v, (((0,), (0,)), ((), ())), preferred_element_type=F32)

    def contract_cols(a, b):
        return lax.dot_general(a, b, (((1,), (1,)), ((), ())), preferred_element_type=F32)

    for copy in loads[0:4]:
        copy.wait()
    par_t[...] = jnp.zeros((128, 2 * 128), F32)
    par_t[0:TAPS, 0:CH] = dk_ref[...]
    par_t[GAIN_CONV : GAIN_CONV + 1, 0:CH] = cg_ref[...]
    par_t[GAIN_NORM : GAIN_NORM + 1, 0:CH] = ng_ref[...]
    par_ref[...] = par_t[...].T[0:CH]

    local_moments(lambda r: x_all[p, r, :].astype(F32), st0_s)
    st0_s[8:16, :] = jnp.zeros((8, 128), F32)
    st0_s[8:9, :] = par_t[GAIN_NORM : GAIN_NORM + 1, 0:128]
    st0_s[9:10, :] = par_t[GAIN_NORM : GAIN_NORM + 1, 128:256]
    pl.semaphore_wait(barrier, len(peers))
    st0_r[p] = st0_s[...]
    for k in range(1, TP):
        send(st0_s, st0_r.at[p], ("st", 0, k - 1), tp_dev(k))
    gather_send(x_all, 0)

    loads[4].wait()
    loads[5].wait()
    def dact_body(d, c):
        lanes = pl.ds(pl.multiple_of(d * (2 * CH), 128), 2 * CH)
        term = contract_rows(wo_ref[:, lanes], cot_ref[...]).astype(BF16)
        da_s[2 * d] = term[0:CH]
        da_s[2 * d + 1] = term[CH : 2 * CH]
        return c

    loop(TP // 2, dact_body, 0)
    gather_relay(x_all, 0)
    gather_last(x_all, 0)

    for k in range(1, TP):
        arrived(st0_r.at[lax.rem(p + TP - k, TP)], ("st", 0, k - 1), tp_dev(k))
    gains_t[...] = jnp.zeros((128, 256), F32)
    for j in range(TP):
        gains_t[j : j + 1, 0:128] = st0_r[j, 8:9, :]
        gains_t[j : j + 1, 128:256] = st0_r[j, 9:10, :]
    gains[...] = gains_t[...].T
    mean_in, inv_in = merged([st0_r[j] for j in range(TP)])

    def own_body(i, c):
        r = row_block(i, BLK)
        h = (x_all[p, r, :].astype(F32) - mean_in) * inv_in
        hat_in[r, :] = h
        normed[p, r, :] = (h * par_ref[r, GAIN_NORM : GAIN_NORM + 1]).astype(BF16)
        return c

    loop(CH // BLK, own_body, 0)
    scatter_send(da_s, 0)
    loads[6].wait()
    loads[7].wait()
    gather_wait(x_all, 0)
    for j in range(TP):

        @pl.when(p != j)
        def _():
            def body(i, c):
                r = row_block(i, BLK)
                h = (x_all[j, r, :].astype(F32) - mean_in) * inv_in
                normed[j, r, :] = (h * gains[r, j : j + 1]).astype(BF16)
                return c

            loop(CH // BLK, body, 0)

    def glu_part(low, high):
        part = normed[:, :, low:high].reshape(D, high - low)
        v = jnp.dot(wv_ref[...], part, preferred_element_type=F32)
        s = jax.nn.sigmoid(jnp.dot(wg_ref[...], part, preferred_element_type=F32))
        value[:, low:high] = v
        sig[:, low:high] = s
        glu_w[:, PAD + low : PAD + high] = (v * s).astype(BF16)

    glu_part(0, 128)
    glu_part(FR - 128, FR)
    halo_send(glu_w, 0)
    glu_part(128, FR - 128)
    scatter_relay(da_s, 0)
    halo_wait(glu_w, 0)

    def conv_body(i, c):
        r = row_block(i, 16)
        w = glu_w[r, :].astype(F32)
        taps = par_ref[r, 0:TAPS]
        spans = ((0, FR + PAD), (0, FR + PAD), (PAD, FR + PAD), (PAD, WIDE))
        acc = [None] * 4
        for b in range(8):
            moved = pltpu.roll(w, WIDE - b, 1) if b else w
            for a in range(4):
                k = 8 * a + b
                term = taps[:, k : k + 1] * moved[:, spans[a][0] : spans[a][1]]
                acc[a] = term if acc[a] is None else acc[a] + term
        total = acc[2] + pltpu.roll(acc[0], 16, 1)[:, PAD:] + pltpu.roll(acc[1], 8, 1)[:, PAD:]
        conv[r, :] = total + pltpu.roll(acc[3], FR + PAD - 8, 1)[:, 0:FR]
        return c

    lax.fori_loop(0, CH // 32, conv_body, 0)
    scatter_last(da_s, 0)
    lax.fori_loop(CH // 32, CH // 16, conv_body, 0)
    local_moments(lambda r: conv[r, :], st_s.at[1])
    share(1)

    scatter_wait(0)
    for h in range(2):

        def dsum_body(j, c):
            r = pl.ds(pl.multiple_of(h * HALF + j * BLK, BLK), BLK)
            dact[r, :] = scatter_sum(da_s, 0, r, j, h)
            return c

        loop(HALF // BLK, dsum_body, 0)
    mean_c, inv_c = merged(shared(1))

    def act_body(i, carry):
        a, b = carry
        r = row_block(i, BLK)
        h = (conv[r, :] - mean_c) * inv_c
        hatc[r, :] = h
        g = par_ref[r, GAIN_CONV : GAIN_CONV + 1]
        scaled = h * g
        s = jax.nn.sigmoid(scaled)
        act_all[p, r, :] = (scaled * s).astype(BF16)
        ds = dact[r, :] * (s + scaled * s * (1.0 - s))
        sm_s[r, GAIN_CONV : GAIN_CONV + 1] = jnp.sum(ds * h, axis=1, keepdims=True)
        e = ds * g
        dact[r, :] = e
        return a + fold8(e), b + fold8(e * h)

    sm_s[...] = jnp.zeros((CH, 128), F32)
    first, second = loop(CH // BLK, act_body, (zero8, zero8))
    put_tile(st_s.at[2], collapse(first), collapse(second))
    share(2)
    gather_send(act_all, 1)
    first, second = summed(2)

    def dconv_body(i, c):
        r = row_block(i, BLK)
        dcv_w[r, PAD : PAD + FR] = ((dact[r, :] - first - hatc[r, :] * second) * inv_c).astype(BF16)
        return c

    loop(CH // BLK, dconv_body, 0)
    halo_send(dcv_w, 1)
    gather_relay(act_all, 1)
    halo_wait(dcv_w, 1)

    at_end = (q == SEQ - 1).astype(F32)

    def back_body(i, c):
        r = row_block(i, 16)
        w = dcv_w[r, :].astype(F32)
        taps = par_ref[r, 0:TAPS]
        u = glu_w[r, :].astype(F32)
        spans = ((PAD, WIDE), (PAD, WIDE), (PAD, FR + PAD), (0, FR + PAD))
        glus = []
        for a in range(4):
            g = pltpu.roll(u, (16 - 8 * a) % WIDE, 1) if a != 2 else u
            glus.append((g[:, PAD : PAD + FR], g[:, PAD + FR :] * at_end if a < 2 else None))
        acc = [None] * 4
        for b in range(8):
            moved = pltpu.roll(w, b, 1) if b else w
            for a in range(4):
                k = 8 * a + b
                term = taps[:, k : k + 1] * moved[:, spans[a][0] : spans[a][1]]
                acc[a] = term if acc[a] is None else acc[a] + term
                body, tail = glus[a]
                m = body * moved[:, PAD : PAD + FR]
                m = (m[:, 0:128] + m[:, 128:256]) + (m[:, 256:384] + m[:, 384:512])
                if tail is not None and b:
                    m = m + tail * moved[:, PAD + FR :]
                prod[k, r, :] = m
        total = acc[2] + pltpu.roll(acc[0], FR + PAD - 16, 1)[:, 0:FR]
        total = total + pltpu.roll(acc[1], FR + PAD - 8, 1)[:, 0:FR] + pltpu.roll(acc[3], 8, 1)[:, PAD:]
        s = sig[r, :]
        dv = total * s
        dv_b[r, :] = dv.astype(BF16)
        dg_b[r, :] = (dv * value[r, :] * (1.0 - s)).astype(BF16)
        return c

    lax.fori_loop(0, CH // 32, back_body, 0)
    gather_last(act_all, 1)
    lax.fori_loop(CH // 32, CH // 16, back_body, 0)

    other = pl.ds(pl.multiple_of((1 - core) * HALF, HALF), HALF)
    mine = pl.ds(pl.multiple_of(core * HALF, HALF), HALF)

    def pair_send(g):
        send(g16.at[g, other, :], c1.at[g], ("c1", g), mate)

    def weight_grad(g, left_ref, all_ref):
        g16[g] = contract_cols(left_ref[...], all_ref[...].reshape(D, FR)).astype(BF16)
        pair_send(g)

    weight_grad(0, dv_b, normed)
    weight_grad(1, dg_b, normed)

    def dn_pair(dx, entries):
        xx = lax.rem(tx + dx, 4)
        lanes = pl.ds(pl.multiple_of(xx * (2 * CH), 128), 2 * CH)
        term = contract_rows(wv_ref[:, lanes], dv_b[...]) + contract_rows(wg_ref[:, lanes], dg_b[...])
        term = term.astype(BF16)
        dn_s[2 * xx] = term[0:CH]
        dn_s[2 * xx + 1] = term[CH : 2 * CH]
        for i in entries:
            scatter_put(dn_s, 1, i)

    def z_block(zz):
        return (
            pl.ds(pl.multiple_of((zz // 4) * ZR, 16), ZR),
            pl.ds(pl.multiple_of(lax.rem(zz, 4) * ZL, 128), ZL),
        )

    def chains(g):
        sign = 1 if g % 2 == 0 else NZ - 1
        return ((0, 4, sign), (1, 3, NZ - sign))

    def z_start(g):
        arrived(c1.at[g], ("c1", g), mate)
        s16[g] = (g16[g, mine, :].astype(F32) + c1[g].astype(F32)).astype(BF16)
        z_hop(g, 1)

    def z_got(g, i, sign):
        arrived(zr.at[g, i], ("z", g, i), z_dev(sign))
        return zr[g, i].astype(F32)

    def z_hop(g, step):
        for chain, n, sign in chains(g):
            if step <= n:
                rr, ll = z_block(lax.rem(z + sign * (n + 1 - step), NZ))
                i = chain * 4 + step - 1
                if step > 1:
                    s16[g, rr, ll] = (s16[g, rr, ll].astype(F32) + z_got(g, i - 1, sign)).astype(BF16)
                send(s16.at[g, rr, ll], zr.at[g, i], ("z", g, i), z_dev(sign))

    def y_send(g):
        rr, ll = z_block(z)
        total = s16[g, rr, ll].astype(F32)
        for chain, n, sign in chains(g):
            total = total + z_got(g, chain * 4 + n - 1, sign)
        y16[g] = total.astype(BF16)
        yr[g, yh] = total.astype(BF16)
        for k in range(1, NY):
            send(y16.at[g], yr.at[g, yh], ("y", g, k - 1), y_dev(k))

    outs = (gval_out, ggate_out, gout_out)

    def out_block(zz, cc):
        rr, ll = z_block(zz)
        return pl.ds(pl.multiple_of(cc * HALF + (zz // 4) * ZR, 16), ZR), ll

    def w_start(g):
        for k in range(1, NY):
            arrived(yr.at[g, lax.rem(yh + NY - k, NY)], ("y", g, k - 1), y_dev(k))
        total = yr[g, 0].astype(F32)
        for j in range(1, NY):
            total = total + yr[g, j].astype(F32)
        r16[g] = (total * scale).astype(BF16)
        rr, ll = out_block(z, core)
        outs[g][rr, ll] = r16[g]
        for chain, n, sign in chains(g):
            send(r16.at[g], outs[g].at[rr, ll], ("w", g, chain * 4), z_dev(sign))
        send(r16.at[g], outs[g].at[rr, ll], ("f", g, 0), mate)

    def w_hop(g, step):
        for chain, n, sign in chains(g):
            if step <= n + 1:
                i = chain * 4 + step - 2
                rr, ll = out_block(lax.rem(z + (NZ - sign) * (step - 1), NZ), core)
                piece = outs[g].at[rr, ll]
                arrived(piece, ("w", g, i), z_dev(sign))
                if step <= n:
                    send(piece, piece, ("w", g, i + 1), z_dev(sign))
                send(piece, piece, ("f", g, 1 + i), mate)

    def f_wait(g):
        rr, ll = out_block(z, 1 - core)
        arrived(outs[g].at[rr, ll], ("f", g, 0), mate)
        for chain, n, sign in chains(g):
            for step in range(2, n + 2):
                rr, ll = out_block(lax.rem(z + (NZ - sign) * (step - 1), NZ), 1 - core)
                arrived(outs[g].at[rr, ll], ("f", g, 1 + chain * 4 + step - 2), mate)

    gather_wait(act_all, 1)
    weight_grad(2, cot_ref, act_all)
    z_start(0)
    z_start(1)
    dn_pair(2, (13, 12, 6))
    z_start(2)
    dn_pair(1, (9, 3, 11))
    z_hop(0, 2)
    z_hop(1, 2)
    dn_pair(3, (10,))
    dn_pair(0, (5,))
    z_hop(2, 2)
    z_hop(0, 3)
    z_hop(1, 3)
    scatter_relay(dn_s, 1)
    z_hop(2, 3)
    z_hop(0, 4)
    z_hop(1, 4)
    scatter_last(dn_s, 1)
    z_hop(2, 4)
    y_send(0)
    y_send(1)

    for k in range(TAPS):
        sm_s[:, k : k + 1] = jnp.sum(prod[k], axis=1, keepdims=True)
    send(sm_s, sm_c, ("sc", 0), mate)
    y_send(2)
    ncol[...] = jnp.zeros((256, 128), F32)
    scatter_wait(1)

    carry = (zero8, zero8)
    for h in range(2):

        def dnorm_body(j, carry):
            a, b = carry
            r = pl.ds(pl.multiple_of(h * HALF + j * BLK, BLK), BLK)
            total = scatter_sum(dn_s, 1, r, j, h)
            hat = hat_in[r, :]
            ncol[r, 0:1] = jnp.sum(total * hat, axis=1, keepdims=True)
            e = total * par_ref[r, GAIN_NORM : GAIN_NORM + 1]
            dact[r, :] = e
            return a + fold8(e), b + fold8(e * hat)

        carry = loop(HALF // BLK, dnorm_body, carry)
    first, second = carry
    put_tile(st_s.at[3], collapse(first), collapse(second))
    share(3)

    def all_sum(buf, count):
        total = buf[0]
        for j in range(1, count):
            total = total + buf[j]
        return total

    flat = ncol[...].T
    nt_s[0] = jnp.zeros((8, 128), F32)
    nt_s[0, 0:1] = flat[0:1, 0:128]
    nt_s[0, 1:2] = flat[0:1, 128:256]
    nt_z[z] = nt_s[0]
    for k in range(1, NZ):
        send(nt_s.at[0], nt_z.at[z], ("nz", k - 1), z_dev(k))

    arrived(sm_c, ("sc", 0), mate)
    sm_t[...] = sm_s[...] + sm_c[...]

    def sm_rows(zz):
        return pl.ds(pl.multiple_of(zz * SR, 8), SR)

    for k in range(1, NZ):
        send(sm_t.at[sm_rows(lax.rem(z + k, NZ)), :], sm_z.at[z], ("sz", k - 1), z_dev(k))
    sm_z[z] = sm_t[sm_rows(z), :]

    w_start(0)
    w_start(1)
    first, second = summed(3)

    def grad_body(i, c):
        r = row_block(i, BLK)
        back = (dact[r, :] - first - hat_in[r, :] * second) * inv_in
        input_grad[r, :] = (cot_ref[r, :].astype(F32) + back).astype(BF16)
        return c

    loop(CH // BLK, grad_body, 0)
    stores[1].start()
    w_hop(0, 2)
    w_hop(1, 2)
    w_start(2)

    value[...] = jnp.dot(wo_ref[...], act_all[...].reshape(D, FR), preferred_element_type=F32)

    def out_body(i, c):
        r = row_block(i, BLK)
        block_out[r, :] = (x_all[p, r, :].astype(F32) + value[r, :]).astype(BF16)
        return c

    loop(CH // BLK, out_body, 0)
    stores[0].start()

    w_hop(0, 3)
    w_hop(1, 3)
    for k in range(1, NZ):
        arrived(nt_z.at[lax.rem(z + NZ - k, NZ)], ("nz", k - 1), z_dev(k))
    nt_s[1] = all_sum(nt_z, NZ)
    nt_y[yh] = nt_s[1]
    for k in range(1, NY):
        send(nt_s.at[1], nt_y.at[yh], ("ny", k - 1), y_dev(k))

    for k in range(1, NZ):
        arrived(sm_z.at[lax.rem(z + NZ - k, NZ)], ("sz", k - 1), z_dev(k))
    total = all_sum(sm_z, NZ)
    sm_r[0] = total
    sm_y[yh] = total
    for k in range(1, NY):
        send(sm_r.at[0], sm_y.at[yh], ("sy", k - 1), y_dev(k))

    w_hop(2, 2)
    w_hop(0, 4)
    w_hop(1, 4)
    for k in range(1, NY):
        arrived(nt_y.at[lax.rem(yh + NY - k, NY)], ("ny", k - 1), y_dev(k))
    nt_s[2] = all_sum(nt_y, NY)
    send(nt_s.at[2], nt_c, ("nc", 0), mate)

    for k in range(1, NY):
        arrived(sm_y.at[lax.rem(yh + NY - k, NY)], ("sy", k - 1), y_dev(k))
    total = all_sum(sm_y, NY)
    sm_r[1] = total * scale
    small_out[sm_rows(z), :] = total * scale
    for k in range(1, NZ):
        send(sm_r.at[1], small_out.at[sm_rows(z), :], ("sw", k - 1), z_dev(k))

    w_hop(2, 3)
    w_hop(0, 5)
    w_hop(1, 5)
    w_hop(2, 4)
    w_hop(2, 5)
    for k in range(1, NZ):
        arrived(small_out.at[sm_rows(lax.rem(z + NZ - k, NZ)), :], ("sw", k - 1), z_dev(k))
    stores[5].start()
    arrived(nt_c, ("nc", 0), mate)
    norm_out[...] = (nt_s[2] + nt_c[...]) * scale
    stores[6].start()
    for g in range(3):
        f_wait(g)
        stores[2 + g].start()
    for copy in sends:
        copy.wait_send()
    for copy in stores:
        copy.wait()


def copy_out(*refs):
    ins, outs, stage, small, norm, sem = refs[0:7], refs[7:15], refs[15:20], refs[20], refs[21], refs[22]
    loads = [pltpu.make_async_copy(ins[i], stage[i], sem.at[i]) for i in range(5)]
    stores = [pltpu.make_async_copy(stage[i], outs[i], sem.at[5 + i]) for i in range(5)]
    last = [pltpu.make_async_copy(ins[5], small, sem.at[10]), pltpu.make_async_copy(ins[6], norm, sem.at[11])]
    for copy in last + loads:
        copy.start()
    for copy in last:
        copy.wait()
    outs[7][:, 0:128] = norm[0:1, :]
    outs[7][:, 128:CH] = norm[1:2, 0 : CH - 128]
    for i in range(5):
        loads[i].wait()
        stores[i].start()
    cols = jnp.concatenate([small[...], jnp.zeros((2 * 128 - CH, 128), F32)], axis=0).T
    outs[5][...] = cols[0:TAPS, 0:CH]
    outs[6][...] = cols[GAIN_CONV : GAIN_CONV + 1, 0:CH]
    for copy in stores:
        copy.wait()


def local(
    frames_in, norm_gain, value_weight, gate_weight, depth_kernel, conv_gain, out_weight, cotangent
):
    act = jax.ShapeDtypeStruct((CH, FR), BF16)
    mat = jax.ShapeDtypeStruct((CH, D), BF16)
    row = jax.ShapeDtypeStruct((1, CH), F32)
    vm = pltpu.VMEM
    dma = pltpu.SemaphoreType.DMA
    full = vm((CH, FR), F32)
    eight = vm((TP, CH, FR), BF16)
    wide = vm((CH, WIDE), BF16)
    block = vm((CH, FR), BF16)
    weight = vm((CH, D), BF16)
    small = vm((CH, 128), F32)
    line = vm((1, CH), F32)
    tile = vm((8, 128), F32)
    scratch = [block, block, weight, weight, weight, small, tile]
    scratch += [line, weight, weight, vm((TAPS, CH), F32), line, weight, block, vm((128, 256), F32), small] + [full] * 6
    scratch += [eight, vm((128, 256), F32), vm((256, 128), F32), vm((16, 128), F32), vm((TP, 16, 128), F32)]
    scratch += [eight] * 4
    scratch += [vm((2, 14, HALF, FR), BF16), wide, wide, block, block, vm((TAPS, CH, 128), F32)]
    scratch += [vm((4, 8, 128), F32), vm((4, TP, 8, 128), F32)]
    scratch += [
        vm((3, CH, D), BF16),
        vm((3, HALF, D), BF16),
        vm((3, HALF, D), BF16),
        vm((3, 8, ZR, ZL), BF16),
        vm((3, ZR, ZL), BF16),
        vm((3, NY, ZR, ZL), BF16),
        vm((3, ZR, ZL), BF16),
    ]
    scratch += [vm((256, 128), F32), vm((3, 8, 128), F32), vm((NZ, 8, 128), F32), vm((NY, 8, 128), F32), tile]
    scratch += [small, small, small, vm((NZ, SR, 128), F32), vm((NY, SR, 128), F32), vm((2, SR, 128), F32)]
    scratch += [dma((8,)), dma((7,))]
    for shape in ((4, 7), (2, 14), (2, 14), (2, 2), (3,), (3, 8), (3, 3), (3, 8), (3, 8), (7,), (3,), (1,), (1,), (7,), (3,), (7,)):
        scratch += [dma(shape), dma(shape)]
    vmem = pl.BlockSpec(memory_space=pltpu.VMEM)
    anywhere = pl.BlockSpec(memory_space=pl.ANY)
    results = pl.pallas_call(
        kernel,
        out_shape=(act, act, mat, mat, mat, jax.ShapeDtypeStruct((CH, 128), F32), jax.ShapeDtypeStruct((8, 128), F32)),
        in_specs=[anywhere] * 8,
        out_specs=(anywhere,) * 7,
        scratch_shapes=scratch,
        compiler_params=pltpu.CompilerParams(
            collective_id=0, has_side_effects=True, vmem_limit_bytes=VMEM_LIMIT
        ),
    )(
        frames_in,
        norm_gain.reshape(1, CH),
        value_weight,
        gate_weight,
        depth_kernel.T,
        conv_gain.reshape(1, CH),
        out_weight,
        cotangent,
    )
    block_out, input_grad, gval, ggate, gout, gkernel, gconv, gnorm = pl.pallas_call(
        copy_out,
        out_shape=(act, act, mat, mat, mat, jax.ShapeDtypeStruct((TAPS, CH), F32), row, row),
        in_specs=[anywhere] * 7,
        out_specs=(anywhere,) * 5 + (vmem,) * 3,
        scratch_shapes=[block, block, weight, weight, weight, small, tile, dma((12,))],
    )(*results)
    return (
        block_out,
        input_grad,
        gnorm.reshape(CH),
        gval,
        ggate,
        gkernel.T,
        gconv.reshape(CH),
        gout,
    )


def solution(mesh):
    return jax.shard_map(
        local,
        mesh=mesh,
        in_specs=(
            P("tp", "seq"),
            P("tp"),
            P("tp", None),
            P("tp", None),
            P("tp", None),
            P("tp"),
            P("tp", None),
            P("tp", "seq"),
        ),
        out_specs=(
            P("tp", "seq"),
            P("tp", "seq"),
            P("tp"),
            P("tp", None),
            P("tp", None),
            P("tp", None),
            P("tp"),
            P("tp", None),
        ),
        check_vma=False,
    )
```

```python
import functools

import jax
import jax.numpy as jnp
from jax import lax
from jax.experimental import pallas as pl
from jax.experimental.pallas import tpu as pltpu
from jax.sharding import PartitionSpec as P

EPS = 1e-05
F32 = jnp.float32
BF16 = jnp.bfloat16
MESH = pl.DeviceIdType.MESH

TP = 8
SEQ = 64
NZ = 8
NY = 4
CH = 192
FR = 512
D = CH * TP
TAPS = 32
REACH = TAPS // 2
PAD = 128
WIDE = FR + 2 * PAD
HALF = CH // 2
ZR = HALF // 2
ZL = D // 4
SR = CH // NZ
BLK = 32
VMEM_LIMIT = 63 * 1024 * 1024
GAIN_CONV = TAPS
GAIN_NORM = TAPS + 1


def fold8(v):
    out = v[0:8]
    for i in range(8, v.shape[0], 8):
        out = out + v[i : i + 8]
    return out


def row_block(i, blk):
    return pl.ds(pl.multiple_of(i * blk, blk), blk)


def put_tile(ref, a, b):
    for j in range(4):
        ref[j : j + 1, :] = a[:, 128 * j : 128 * j + 128]
        ref[4 + j : 5 + j, :] = b[:, 128 * j : 128 * j + 128]


def tile_row(t):
    return jnp.concatenate([t[j : j + 1] for j in range(4)], axis=1)


def kernel(
    x_hbm, ng_hbm, wv_hbm, wg_hbm, dk_hbm, cg_hbm, wo_hbm, cot_hbm,
    *rest,
):
    finals, landed, rest = rest[0:7], rest[7:14], rest[14:]
    block_out, input_grad, gval_out, ggate_out, gout_out, small_out, norm_out = landed
    (
        ng_ref, wv_ref, wg_ref, dk_ref, cg_ref, wo_ref, cot_ref, par_t, par_ref,
        hat_in, value, sig, conv, hatc, dact,
        x_all, gains_t, gains, st0_s, st0_r, normed, act_all, da_s, dn_s, rs_r,
        glu_w, dcv_w, dv_b, dg_b, prod,
        st_s, st_r,
        g16, c1, s16, zr, y16, yr, r16,
        ncol, nt_s, nt_z, nt_y, nt_c, sm_s, sm_c, sm_t, sm_z, sm_y, sm_r,
        ld, fin,
        st_ss, st_rs, ag_ss, ag_rs, rs_ss, rs_rs, ha_ss, ha_rs,
        c1_ss, c1_rs, z_ss, z_rs, y_ss, y_rs, w_ss, w_rs, f_ss, f_rs,
        nz_ss, nz_rs, ny_ss, ny_rs, nc_ss, nc_rs, sc_ss, sc_rs, sz_ss, sz_rs, sy_ss, sy_rs, sw_ss, sw_rs,
    ) = rest
    stores = [pltpu.make_async_copy(landed[i], finals[i], fin.at[i]) for i in range(7)]
    p = lax.axis_index("tp")
    fetch = (
        (x_hbm, x_all.at[p]), (dk_hbm, dk_ref), (cg_hbm, cg_ref), (ng_hbm, ng_ref),
        (wo_hbm, wo_ref), (cot_hbm, cot_ref), (wv_hbm, wv_ref), (wg_hbm, wg_ref),
    )
    loads = [pltpu.make_async_copy(src, dst, ld.at[i]) for i, (src, dst) in enumerate(fetch)]
    for copy in loads:
        copy.start()
    q = lax.axis_index("seq")
    core = lax.rem(q, 2)
    chip = q // 2
    z = lax.rem(chip, NZ)
    yh = chip // NZ
    scale = float(FR * SEQ) ** (-0.5)
    sends = []

    sems = {
        "st": (st_ss, st_rs), "ag": (ag_ss, ag_rs), "rs": (rs_ss, rs_rs), "ha": (ha_ss, ha_rs),
        "c1": (c1_ss, c1_rs), "z": (z_ss, z_rs), "y": (y_ss, y_rs), "w": (w_ss, w_rs), "f": (f_ss, f_rs),
        "nz": (nz_ss, nz_rs), "ny": (ny_ss, ny_rs), "nc": (nc_ss, nc_rs), "sc": (sc_ss, sc_rs), "sz": (sz_ss, sz_rs), "sy": (sy_ss, sy_rs), "sw": (sw_ss, sw_rs),
    }

    def remote(src, dst, key, dev):
        out, into = sems[key[0]]
        return pltpu.make_async_remote_copy(
            src_ref=src, dst_ref=dst, send_sem=out.at[key[1:]], recv_sem=into.at[key[1:]],
            device_id=dev, device_id_type=MESH,
        )

    def send(src, dst, key, dev):
        copy = remote(src, dst, key, dev)
        copy.start()
        sends.append(copy)

    def arrived(dst, key, dev):
        remote(dst, dst, key, dev).wait_recv()

    tx, ty = p // 2, lax.rem(p, 2)

    def at_tp(dx, dy):
        return lax.rem(tx + dx, 4) * 2 + lax.rem(ty + dy, 2)

    def hop(dx, dy):
        return {"tp": at_tp(dx, dy), "seq": q}

    def half(h):
        return pl.ds(h * HALF, HALF)

    def tp_dev(k):
        return {"tp": lax.rem(p + k, TP), "seq": q}

    def z_dev(k):
        return {"tp": p, "seq": (yh * NZ + lax.rem(z + k, NZ)) * 2 + core}

    def y_dev(k):
        return {"tp": p, "seq": (lax.rem(yh + k, NY) * NZ + z) * 2 + core}

    mate = {"tp": p, "seq": chip * 2 + (1 - core)}
    right = {"tp": p, "seq": lax.rem(q + 1, SEQ)}
    left = {"tp": p, "seq": lax.rem(q + SEQ - 1, SEQ)}

    barrier = pltpu.get_barrier_semaphore()
    peers = [tp_dev(k) for k in range(1, TP)] + [z_dev(k) for k in range(1, NZ)]
    peers += [y_dev(k) for k in range(1, NY)] + [mate, right, left]
    for dev in peers:
        pl.semaphore_signal(barrier, inc=1, device_id=dev, device_id_type=MESH)

    zero8 = jnp.zeros((8, FR), F32)

    def loop(n, body, init):
        return lax.fori_loop(0, n, body, init)

    def collapse(v):
        return jnp.sum(v, axis=0, keepdims=True)

    def local_moments(rows, tile):
        total = loop(CH // BLK, lambda i, a: a + fold8(rows(row_block(i, BLK))), zero8)
        mean = collapse(total) / CH

        def body(i, a):
            c = rows(row_block(i, BLK)) - mean
            return a + fold8(c * c)

        put_tile(tile, mean, collapse(loop(CH // BLK, body, zero8)))

    def share(slot):
        st_r[slot, p] = st_s[slot]
        for k in range(1, TP):
            send(st_s.at[slot], st_r.at[slot, p], ("st", slot, k - 1), tp_dev(k))

    def shared(slot):
        for k in range(1, TP):
            arrived(st_r.at[slot, lax.rem(p + TP - k, TP)], ("st", slot, k - 1), tp_dev(k))
        return [st_r[slot, j] for j in range(TP)]

    def merged(parts):
        total = parts[0]
        for t in parts[1:]:
            total = total + t
        mean = total[0:4] / TP
        spread = total[4:8]
        for t in parts:
            off = t[0:4] - mean
            spread = spread + CH * (off * off)
        inverse = lax.rsqrt(spread / D + EPS)
        return tile_row(mean), tile_row(inverse)

    def summed(slot):
        parts = shared(slot)
        total = parts[0]
        for t in parts[1:]:
            total = total + t
        return tile_row(total[0:4]) / D, tile_row(total[4:8]) / D

    RIGHT, LEFT, SIDE = (1, 0), (3, 0), (0, 1)

    gather_plan = (
        ((0, 0), 0, RIGHT), ((0, 0), 1, RIGHT), ((0, 0), 1, LEFT), ((0, 0), 0, LEFT),
        ((0, 0), 0, SIDE), ((0, 0), 1, SIDE), ((3, 0), 0, RIGHT), ((1, 0), 1, LEFT),
        ((0, 1), 0, RIGHT), ((0, 1), 0, LEFT), ((3, 0), 1, SIDE), ((1, 0), 1, SIDE),
        ((2, 0), 1, SIDE), ((3, 1), 0, RIGHT),
    )

    def gather_put(buf, n, i):
        (dx, dy), h, to = gather_plan[i]
        piece = buf.at[at_tp(dx, dy), half(h), :]
        send(piece, piece, ("ag", n, i), hop(*to))

    def gather_got(buf, n, i):
        (dx, dy), h, to = gather_plan[i]
        piece = buf.at[at_tp(dx + 4 - to[0], dy + to[1]), half(h), :]
        arrived(piece, ("ag", n, i), hop(*to))

    def gather_send(buf, n):
        for i in (0, 2, 4, 1, 3, 5):
            gather_put(buf, n, i)

    def gather_relay(buf, n):
        gather_got(buf, n, 4)
        gather_put(buf, n, 8)
        gather_got(buf, n, 2)
        gather_put(buf, n, 7)
        gather_put(buf, n, 11)
        gather_got(buf, n, 0)
        gather_put(buf, n, 6)
        gather_put(buf, n, 9)
        gather_got(buf, n, 1)
        gather_put(buf, n, 10)

    def gather_last(buf, n):
        gather_got(buf, n, 7)
        gather_put(buf, n, 12)
        gather_got(buf, n, 8)
        gather_put(buf, n, 13)

    def gather_wait(buf, n):
        for i in (3, 5, 6, 9, 10, 11, 12, 13):
            gather_got(buf, n, i)

    scatter_plan = (
        ((3, 0), 0, LEFT), ((3, 0), 1, LEFT), ((1, 0), 1, RIGHT), ((1, 0), 0, RIGHT),
        ((0, 1), 0, SIDE), ((0, 1), 1, SIDE), ((2, 0), 0, LEFT), ((2, 0), 1, RIGHT),
        ((3, 1), 0, LEFT), ((1, 1), 0, RIGHT), ((3, 1), 1, SIDE), ((1, 1), 1, SIDE),
        ((2, 1), 1, SIDE), ((2, 1), 0, LEFT),
    )

    def scatter_put(buf, n, i, merge=()):
        (dx, dy), h, to = scatter_plan[i]
        d = at_tp(dx, dy)
        for m in merge:
            arrived(rs_r.at[n, m], ("rs", n, m), hop(*scatter_plan[m][2]))
        if merge:

            def body(j, c):
                r = pl.ds(pl.multiple_of(h * HALF + j * BLK, BLK), BLK)
                total = buf[d, r, :].astype(F32)
                for m in merge:
                    total = total + rs_r[n, m, row_block(j, BLK), :].astype(F32)
                buf[d, r, :] = total.astype(BF16)
                return c

            loop(HALF // BLK, body, 0)
        send(buf.at[d, half(h), :], rs_r.at[n, i], ("rs", n, i), hop(*to))

    def scatter_send(buf, n):
        for i in (13, 12, 9, 6, 10, 3, 11, 5):
            scatter_put(buf, n, i)

    def scatter_relay(buf, n):
        scatter_put(buf, n, 8, (13,))
        scatter_put(buf, n, 7, (12,))
        scatter_put(buf, n, 0, (6,))
        scatter_put(buf, n, 1, (10,))

    def scatter_last(buf, n):
        scatter_put(buf, n, 4, (8, 9))
        scatter_put(buf, n, 2, (7, 11))

    def scatter_wait(n):
        for m in range(6):
            arrived(rs_r.at[n, m], ("rs", n, m), hop(*scatter_plan[m][2]))

    def scatter_sum(buf, n, r, j, h):
        total = buf[p, r, :].astype(F32)
        for m in ((0, 3, 4), (1, 2, 5))[h]:
            total = total + rs_r[n, m, row_block(j, BLK), :].astype(F32)
        return total

    def halo_send(buf, n):
        send(buf.at[:, PAD : 2 * PAD], buf.at[:, PAD + FR : WIDE], ("ha", n, 0), left)
        send(buf.at[:, FR : FR + PAD], buf.at[:, 0:PAD], ("ha", n, 1), right)

    def halo_wait(buf, n):
        arrived(buf.at[:, PAD + FR : WIDE], ("ha", n, 0), left)
        arrived(buf.at[:, 0:PAD], ("ha", n, 1), right)

        @pl.when(q == 0)
        def _():
            buf[:, 0:PAD] = jnp.zeros((CH, PAD), buf.dtype)

        @pl.when(q == SEQ - 1)
        def _():
            buf[:, PAD + FR : WIDE] = jnp.zeros((CH, PAD), buf.dtype)

    def contract_rows(w, v):
        return lax.dot_general(w, v, (((0,), (0,)), ((), ())), preferred_element_type=F32)

    def contract_cols(a, b):
        return lax.dot_general(a, b, (((1,), (1,)), ((), ())), preferred_element_type=F32)

    for copy in loads[0:4]:
        copy.wait()
    par_t[...] = jnp.zeros((128, 2 * 128), F32)
    par_t[0:TAPS, 0:CH] = dk_ref[...]
    par_t[GAIN_CONV : GAIN_CONV + 1, 0:CH] = cg_ref[...]
    par_t[GAIN_NORM : GAIN_NORM + 1, 0:CH] = ng_ref[...]
    par_ref[...] = par_t[...].T[0:CH]

    local_moments(lambda r: x_all[p, r, :].astype(F32), st0_s)
    st0_s[8:16, :] = jnp.zeros((8, 128), F32)
    st0_s[8:9, :] = par_t[GAIN_NORM : GAIN_NORM + 1, 0:128]
    st0_s[9:10, :] = par_t[GAIN_NORM : GAIN_NORM + 1, 128:256]
    pl.semaphore_wait(barrier, len(peers))
    st0_r[p] = st0_s[...]
    for k in range(1, TP):
        send(st0_s, st0_r.at[p], ("st", 0, k - 1), tp_dev(k))
    gather_send(x_all, 0)

    loads[4].wait()
    loads[5].wait()
    def dact_body(d, c):
        lanes = pl.ds(pl.multiple_of(d * (2 * CH), 128), 2 * CH)
        term = contract_rows(wo_ref[:, lanes], cot_ref[...]).astype(BF16)
        da_s[2 * d] = term[0:CH]
        da_s[2 * d + 1] = term[CH : 2 * CH]
        return c

    loop(TP // 2, dact_body, 0)
    gather_relay(x_all, 0)
    gather_last(x_all, 0)

    for k in range(1, TP):
        arrived(st0_r.at[lax.rem(p + TP - k, TP)], ("st", 0, k - 1), tp_dev(k))
    gains_t[...] = jnp.zeros((128, 256), F32)
    for j in range(TP):
        gains_t[j : j + 1, 0:128] = st0_r[j, 8:9, :]
        gains_t[j : j + 1, 128:256] = st0_r[j, 9:10, :]
    gains[...] = gains_t[...].T
    mean_in, inv_in = merged([st0_r[j] for j in range(TP)])

    def own_body(i, c):
        r = row_block(i, BLK)
        h = (x_all[p, r, :].astype(F32) - mean_in) * inv_in
        hat_in[r, :] = h
        normed[p, r, :] = (h * par_ref[r, GAIN_NORM : GAIN_NORM + 1]).astype(BF16)
        return c

    loop(CH // BLK, own_body, 0)
    scatter_send(da_s, 0)
    loads[6].wait()
    loads[7].wait()
    gather_wait(x_all, 0)
    for j in range(TP):

        @pl.when(p != j)
        def _():
            def body(i, c):
                r = row_block(i, BLK)
                h = (x_all[j, r, :].astype(F32) - mean_in) * inv_in
                normed[j, r, :] = (h * gains[r, j : j + 1]).astype(BF16)
                return c

            loop(CH // BLK, body, 0)

    def glu_part(low, high):
        part = normed[:, :, low:high].reshape(D, high - low)
        v = jnp.dot(wv_ref[...], part, preferred_element_type=F32)
        s = jax.nn.sigmoid(jnp.dot(wg_ref[...], part, preferred_element_type=F32))
        value[:, low:high] = v
        sig[:, low:high] = s
        glu_w[:, PAD + low : PAD + high] = (v * s).astype(BF16)

    glu_part(0, 128)
    glu_part(FR - 128, FR)
    halo_send(glu_w, 0)
    glu_part(128, FR - 128)
    scatter_relay(da_s, 0)
    halo_wait(glu_w, 0)

    def conv_body(i, c):
        r = row_block(i, 16)
        w = glu_w[r, :].astype(F32)
        taps = par_ref[r, 0:TAPS]
        spans = ((0, FR + PAD), (0, FR + PAD), (PAD, FR + PAD), (PAD, WIDE))
        acc = [None] * 4
        for b in range(8):
            moved = pltpu.roll(w, WIDE - b, 1) if b else w
            for a in range(4):
                k = 8 * a + b
                term = taps[:, k : k + 1] * moved[:, spans[a][0] : spans[a][1]]
                acc[a] = term if acc[a] is None else acc[a] + term
        total = acc[2] + pltpu.roll(acc[0], 16, 1)[:, PAD:] + pltpu.roll(acc[1], 8, 1)[:, PAD:]
        conv[r, :] = total + pltpu.roll(acc[3], FR + PAD - 8, 1)[:, 0:FR]
        return c

    lax.fori_loop(0, CH // 32, conv_body, 0)
    scatter_last(da_s, 0)
    lax.fori_loop(CH // 32, CH // 16, conv_body, 0)
    local_moments(lambda r: conv[r, :], st_s.at[1])
    share(1)

    scatter_wait(0)
    for h in range(2):

        def dsum_body(j, c):
            r = pl.ds(pl.multiple_of(h * HALF + j * BLK, BLK), BLK)
            dact[r, :] = scatter_sum(da_s, 0, r, j, h)
            return c

        loop(HALF // BLK, dsum_body, 0)
    mean_c, inv_c = merged(shared(1))

    def act_body(i, carry):
        a, b = carry
        r = row_block(i, BLK)
        h = (conv[r, :] - mean_c) * inv_c
        hatc[r, :] = h
        g = par_ref[r, GAIN_CONV : GAIN_CONV + 1]
        scaled = h * g
        s = jax.nn.sigmoid(scaled)
        act_all[p, r, :] = (scaled * s).astype(BF16)
        ds = dact[r, :] * (s + scaled * s * (1.0 - s))
        sm_s[r, GAIN_CONV : GAIN_CONV + 1] = jnp.sum(ds * h, axis=1, keepdims=True)
        e = ds * g
        dact[r, :] = e
        return a + fold8(e), b + fold8(e * h)

    sm_s[...] = jnp.zeros((CH, 128), F32)
    first, second = loop(CH // BLK, act_body, (zero8, zero8))
    put_tile(st_s.at[2], collapse(first), collapse(second))
    share(2)
    gather_send(act_all, 1)
    first, second = summed(2)

    def dconv_body(i, c):
        r = row_block(i, BLK)
        dcv_w[r, PAD : PAD + FR] = ((dact[r, :] - first - hatc[r, :] * second) * inv_c).astype(BF16)
        return c

    loop(CH // BLK, dconv_body, 0)
    halo_send(dcv_w, 1)
    gather_relay(act_all, 1)
    halo_wait(dcv_w, 1)

    at_end = (q == SEQ - 1).astype(F32)

    def back_body(i, c):
        r = row_block(i, 16)
        w = dcv_w[r, :].astype(F32)
        taps = par_ref[r, 0:TAPS]
        u = glu_w[r, :].astype(F32)
        spans = ((PAD, WIDE), (PAD, WIDE), (PAD, FR + PAD), (0, FR + PAD))
        glus = []
        for a in range(4):
            g = pltpu.roll(u, (16 - 8 * a) % WIDE, 1) if a != 2 else u
            glus.append((g[:, PAD : PAD + FR], g[:, PAD + FR :] * at_end if a < 2 else None))
        acc = [None] * 4
        for b in range(8):
            moved = pltpu.roll(w, b, 1) if b else w
            for a in range(4):
                k = 8 * a + b
                term = taps[:, k : k + 1] * moved[:, spans[a][0] : spans[a][1]]
                acc[a] = term if acc[a] is None else acc[a] + term
                body, tail = glus[a]
                m = body * moved[:, PAD : PAD + FR]
                m = (m[:, 0:128] + m[:, 128:256]) + (m[:, 256:384] + m[:, 384:512])
                if tail is not None and b:
                    m = m + tail * moved[:, PAD + FR :]
                prod[k, r, :] = m
        total = acc[2] + pltpu.roll(acc[0], FR + PAD - 16, 1)[:, 0:FR]
        total = total + pltpu.roll(acc[1], FR + PAD - 8, 1)[:, 0:FR] + pltpu.roll(acc[3], 8, 1)[:, PAD:]
        s = sig[r, :]
        dv = total * s
        dv_b[r, :] = dv.astype(BF16)
        dg_b[r, :] = (dv * value[r, :] * (1.0 - s)).astype(BF16)
        return c

    lax.fori_loop(0, CH // 32, back_body, 0)
    gather_last(act_all, 1)
    lax.fori_loop(CH // 32, CH // 16, back_body, 0)

    other = pl.ds(pl.multiple_of((1 - core) * HALF, HALF), HALF)
    mine = pl.ds(pl.multiple_of(core * HALF, HALF), HALF)

    def pair_send(g):
        send(g16.at[g, other, :], c1.at[g], ("c1", g), mate)

    def weight_grad(g, left_ref, all_ref):
        g16[g] = contract_cols(left_ref[...], all_ref[...].reshape(D, FR)).astype(BF16)
        pair_send(g)

    weight_grad(0, dv_b, normed)
    weight_grad(1, dg_b, normed)

    def dn_pair(dx, entries):
        xx = lax.rem(tx + dx, 4)
        lanes = pl.ds(pl.multiple_of(xx * (2 * CH), 128), 2 * CH)
        term = contract_rows(wv_ref[:, lanes], dv_b[...]) + contract_rows(wg_ref[:, lanes], dg_b[...])
        term = term.astype(BF16)
        dn_s[2 * xx] = term[0:CH]
        dn_s[2 * xx + 1] = term[CH : 2 * CH]
        for i in entries:
            scatter_put(dn_s, 1, i)

    def z_block(zz):
        return (
            pl.ds(pl.multiple_of((zz // 4) * ZR, 16), ZR),
            pl.ds(pl.multiple_of(lax.rem(zz, 4) * ZL, 128), ZL),
        )

    def chains(g):
        sign = 1 if g % 2 == 0 else NZ - 1
        return ((0, 4, sign), (1, 3, NZ - sign))

    def z_start(g):
        arrived(c1.at[g], ("c1", g), mate)
        s16[g] = (g16[g, mine, :].astype(F32) + c1[g].astype(F32)).astype(BF16)
        z_hop(g, 1)

    def z_got(g, i, sign):
        arrived(zr.at[g, i], ("z", g, i), z_dev(sign))
        return zr[g, i].astype(F32)

    def z_hop(g, step):
        for chain, n, sign in chains(g):
            if step <= n:
                rr, ll = z_block(lax.rem(z + sign * (n + 1 - step), NZ))
                i = chain * 4 + step - 1
                if step > 1:
                    s16[g, rr, ll] = (s16[g, rr, ll].astype(F32) + z_got(g, i - 1, sign)).astype(BF16)
                send(s16.at[g, rr, ll], zr.at[g, i], ("z", g, i), z_dev(sign))

    def y_send(g):
        rr, ll = z_block(z)
        total = s16[g, rr, ll].astype(F32)
        for chain, n, sign in chains(g):
            total = total + z_got(g, chain * 4 + n - 1, sign)
        y16[g] = total.astype(BF16)
        yr[g, yh] = total.astype(BF16)
        for k in range(1, NY):
            send(y16.at[g], yr.at[g, yh], ("y", g, k - 1), y_dev(k))

    outs = (gval_out, ggate_out, gout_out)

    def out_block(zz, cc):
        rr, ll = z_block(zz)
        return pl.ds(pl.multiple_of(cc * HALF + (zz // 4) * ZR, 16), ZR), ll

    def w_start(g):
        for k in range(1, NY):
            arrived(yr.at[g, lax.rem(yh + NY - k, NY)], ("y", g, k - 1), y_dev(k))
        total = yr[g, 0].astype(F32)
        for j in range(1, NY):
            total = total + yr[g, j].astype(F32)
        r16[g] = (total * scale).astype(BF16)
        rr, ll = out_block(z, core)
        outs[g][rr, ll] = r16[g]
        for chain, n, sign in chains(g):
            send(r16.at[g], outs[g].at[rr, ll], ("w", g, chain * 4), z_dev(sign))
        send(r16.at[g], outs[g].at[rr, ll], ("f", g, 0), mate)

    def w_hop(g, step):
        for chain, n, sign in chains(g):
            if step <= n + 1:
                i = chain * 4 + step - 2
                rr, ll = out_block(lax.rem(z + (NZ - sign) * (step - 1), NZ), core)
                piece = outs[g].at[rr, ll]
                arrived(piece, ("w", g, i), z_dev(sign))
                if step <= n:
                    send(piece, piece, ("w", g, i + 1), z_dev(sign))
                send(piece, piece, ("f", g, 1 + i), mate)

    def f_wait(g):
        rr, ll = out_block(z, 1 - core)
        arrived(outs[g].at[rr, ll], ("f", g, 0), mate)
        for chain, n, sign in chains(g):
            for step in range(2, n + 2):
                rr, ll = out_block(lax.rem(z + (NZ - sign) * (step - 1), NZ), 1 - core)
                arrived(outs[g].at[rr, ll], ("f", g, 1 + chain * 4 + step - 2), mate)

    gather_wait(act_all, 1)
    weight_grad(2, cot_ref, act_all)
    z_start(0)
    z_start(1)
    dn_pair(2, (13, 12, 6))
    z_start(2)
    dn_pair(1, (9, 3, 11))
    z_hop(0, 2)
    z_hop(1, 2)
    dn_pair(3, (10,))
    dn_pair(0, (5,))
    z_hop(2, 2)
    z_hop(0, 3)
    z_hop(1, 3)
    scatter_relay(dn_s, 1)
    z_hop(2, 3)

    for k in range(TAPS):
        sm_s[:, k : k + 1] = jnp.sum(prod[k], axis=1, keepdims=True)
    send(sm_s, sm_c, ("sc", 0), mate)

    z_hop(0, 4)
    z_hop(1, 4)
    scatter_last(dn_s, 1)
    z_hop(2, 4)
    y_send(0)
    y_send(1)
    y_send(2)

    def sm_rows(zz):
        return pl.ds(pl.multiple_of(zz * SR, 8), SR)

    arrived(sm_c, ("sc", 0), mate)
    sm_t[...] = sm_s[...] + sm_c[...]

    for k in range(1, NZ):
        send(sm_t.at[sm_rows(lax.rem(z + k, NZ)), :], sm_z.at[z], ("sz", k - 1), z_dev(k))
    sm_z[z] = sm_t[sm_rows(z), :]

    value[...] = jnp.dot(wo_ref[...], act_all[...].reshape(D, FR), preferred_element_type=F32)

    def out_body(i, c):
        r = row_block(i, BLK)
        block_out[r, :] = (x_all[p, r, :].astype(F32) + value[r, :]).astype(BF16)
        return c

    loop(CH // BLK, out_body, 0)
    stores[0].start()

    ncol[...] = jnp.zeros((256, 128), F32)
    scatter_wait(1)

    carry = (zero8, zero8)
    for h in range(2):

        def dnorm_body(j, carry):
            a, b = carry
            r = pl.ds(pl.multiple_of(h * HALF + j * BLK, BLK), BLK)
            total = scatter_sum(dn_s, 1, r, j, h)
            hat = hat_in[r, :]
            ncol[r, 0:1] = jnp.sum(total * hat, axis=1, keepdims=True)
            e = total * par_ref[r, GAIN_NORM : GAIN_NORM + 1]
            dact[r, :] = e
            return a + fold8(e), b + fold8(e * hat)

        carry = loop(HALF // BLK, dnorm_body, carry)
    first, second = carry
    put_tile(st_s.at[3], collapse(first), collapse(second))
    share(3)

    def all_sum(buf, count):
        total = buf[0]
        for j in range(1, count):
            total = total + buf[j]
        return total

    flat = ncol[...].T
    nt_s[0] = jnp.zeros((8, 128), F32)
    nt_s[0, 0:1] = flat[0:1, 0:128]
    nt_s[0, 1:2] = flat[0:1, 128:256]
    nt_z[z] = nt_s[0]
    for k in range(1, NZ):
        send(nt_s.at[0], nt_z.at[z], ("nz", k - 1), z_dev(k))

    for k in range(1, NZ):
        arrived(sm_z.at[lax.rem(z + NZ - k, NZ)], ("sz", k - 1), z_dev(k))
    total = all_sum(sm_z, NZ)
    sm_r[0] = total
    sm_y[yh] = total
    for k in range(1, NY):
        send(sm_r.at[0], sm_y.at[yh], ("sy", k - 1), y_dev(k))

    w_start(0)
    w_start(1)
    w_start(2)
    w_hop(0, 2)
    w_hop(1, 2)

    first, second = summed(3)

    def grad_body(i, c):
        r = row_block(i, BLK)
        back = (dact[r, :] - first - hat_in[r, :] * second) * inv_in
        input_grad[r, :] = (cot_ref[r, :].astype(F32) + back).astype(BF16)
        return c

    loop(CH // BLK, grad_body, 0)
    stores[1].start()
    for k in range(1, NZ):
        arrived(nt_z.at[lax.rem(z + NZ - k, NZ)], ("nz", k - 1), z_dev(k))
    nt_s[1] = all_sum(nt_z, NZ)
    nt_y[yh] = nt_s[1]
    for k in range(1, NY):
        send(nt_s.at[1], nt_y.at[yh], ("ny", k - 1), y_dev(k))

    for k in range(1, NY):
        arrived(sm_y.at[lax.rem(yh + NY - k, NY)], ("sy", k - 1), y_dev(k))
    total = all_sum(sm_y, NY)
    sm_r[1] = total * scale
    small_out[sm_rows(z), :] = total * scale
    for k in range(1, NZ):
        send(sm_r.at[1], small_out.at[sm_rows(z), :], ("sw", k - 1), z_dev(k))

    w_hop(2, 2)
    w_hop(0, 3)
    w_hop(1, 3)
    w_hop(2, 3)
    w_hop(0, 4)
    w_hop(1, 4)
    for k in range(1, NY):
        arrived(nt_y.at[lax.rem(yh + NY - k, NY)], ("ny", k - 1), y_dev(k))
    nt_s[2] = all_sum(nt_y, NY)
    send(nt_s.at[2], nt_c, ("nc", 0), mate)

    w_hop(2, 4)
    w_hop(0, 5)
    w_hop(1, 5)
    w_hop(2, 5)
    for k in range(1, NZ):
        arrived(small_out.at[sm_rows(lax.rem(z + NZ - k, NZ)), :], ("sw", k - 1), z_dev(k))
    stores[5].start()
    arrived(nt_c, ("nc", 0), mate)
    norm_out[...] = (nt_s[2] + nt_c[...]) * scale
    stores[6].start()
    for g in range(3):
        f_wait(g)
        stores[2 + g].start()
    for copy in sends:
        copy.wait_send()
    for copy in stores:
        copy.wait()


def copy_out(*refs):
    ins, outs, stage, small, norm, sem = refs[0:7], refs[7:15], refs[15:20], refs[20], refs[21], refs[22]
    loads = [pltpu.make_async_copy(ins[i], stage[i], sem.at[i]) for i in range(5)]
    stores = [pltpu.make_async_copy(stage[i], outs[i], sem.at[5 + i]) for i in range(5)]
    last = [pltpu.make_async_copy(ins[5], small, sem.at[10]), pltpu.make_async_copy(ins[6], norm, sem.at[11])]
    for copy in last + loads:
        copy.start()
    for copy in last:
        copy.wait()
    outs[7][:, 0:128] = norm[0:1, :]
    outs[7][:, 128:CH] = norm[1:2, 0 : CH - 128]
    for i in range(5):
        loads[i].wait()
        stores[i].start()
    cols = jnp.concatenate([small[...], jnp.zeros((2 * 128 - CH, 128), F32)], axis=0).T
    outs[5][...] = cols[0:TAPS, 0:CH]
    outs[6][...] = cols[GAIN_CONV : GAIN_CONV + 1, 0:CH]
    for copy in stores:
        copy.wait()


def local(
    frames_in, norm_gain, value_weight, gate_weight, depth_kernel, conv_gain, out_weight, cotangent
):
    act = jax.ShapeDtypeStruct((CH, FR), BF16)
    mat = jax.ShapeDtypeStruct((CH, D), BF16)
    row = jax.ShapeDtypeStruct((1, CH), F32)
    vm = pltpu.VMEM
    dma = pltpu.SemaphoreType.DMA
    full = vm((CH, FR), F32)
    eight = vm((TP, CH, FR), BF16)
    wide = vm((CH, WIDE), BF16)
    block = vm((CH, FR), BF16)
    weight = vm((CH, D), BF16)
    small = vm((CH, 128), F32)
    line = vm((1, CH), F32)
    tile = vm((8, 128), F32)
    scratch = [block, block, weight, weight, weight, small, tile]
    scratch += [line, weight, weight, vm((TAPS, CH), F32), line, weight, block, vm((128, 256), F32), small] + [full] * 6
    scratch += [eight, vm((128, 256), F32), vm((256, 128), F32), vm((16, 128), F32), vm((TP, 16, 128), F32)]
    scratch += [eight] * 4
    scratch += [vm((2, 14, HALF, FR), BF16), wide, wide, block, block, vm((TAPS, CH, 128), F32)]
    scratch += [vm((4, 8, 128), F32), vm((4, TP, 8, 128), F32)]
    scratch += [
        vm((3, CH, D), BF16),
        vm((3, HALF, D), BF16),
        vm((3, HALF, D), BF16),
        vm((3, 8, ZR, ZL), BF16),
        vm((3, ZR, ZL), BF16),
        vm((3, NY, ZR, ZL), BF16),
        vm((3, ZR, ZL), BF16),
    ]
    scratch += [vm((256, 128), F32), vm((3, 8, 128), F32), vm((NZ, 8, 128), F32), vm((NY, 8, 128), F32), tile]
    scratch += [small, small, small, vm((NZ, SR, 128), F32), vm((NY, SR, 128), F32), vm((2, SR, 128), F32)]
    scratch += [dma((8,)), dma((7,))]
    for shape in ((4, 7), (2, 14), (2, 14), (2, 2), (3,), (3, 8), (3, 3), (3, 8), (3, 8), (7,), (3,), (1,), (1,), (7,), (3,), (7,)):
        scratch += [dma(shape), dma(shape)]
    vmem = pl.BlockSpec(memory_space=pltpu.VMEM)
    anywhere = pl.BlockSpec(memory_space=pl.ANY)
    results = pl.pallas_call(
        kernel,
        out_shape=(act, act, mat, mat, mat, jax.ShapeDtypeStruct((CH, 128), F32), jax.ShapeDtypeStruct((8, 128), F32)),
        in_specs=[anywhere] * 8,
        out_specs=(anywhere,) * 7,
        scratch_shapes=scratch,
        compiler_params=pltpu.CompilerParams(
            collective_id=0, has_side_effects=True, vmem_limit_bytes=VMEM_LIMIT
        ),
    )(
        frames_in,
        norm_gain.reshape(1, CH),
        value_weight,
        gate_weight,
        depth_kernel.T,
        conv_gain.reshape(1, CH),
        out_weight,
        cotangent,
    )
    block_out, input_grad, gval, ggate, gout, gkernel, gconv, gnorm = pl.pallas_call(
        copy_out,
        out_shape=(act, act, mat, mat, mat, jax.ShapeDtypeStruct((TAPS, CH), F32), row, row),
        in_specs=[anywhere] * 7,
        out_specs=(anywhere,) * 5 + (vmem,) * 3,
        scratch_shapes=[block, block, weight, weight, weight, small, tile, dma((12,))],
    )(*results)
    return (
        block_out,
        input_grad,
        gnorm.reshape(CH),
        gval,
        ggate,
        gkernel.T,
        gconv.reshape(CH),
        gout,
    )


def solution(mesh):
    return jax.shard_map(
        local,
        mesh=mesh,
        in_specs=(
            P("tp", "seq"),
            P("tp"),
            P("tp", None),
            P("tp", None),
            P("tp", None),
            P("tp"),
            P("tp", None),
            P("tp", "seq"),
        ),
        out_specs=(
            P("tp", "seq"),
            P("tp", "seq"),
            P("tp"),
            P("tp", None),
            P("tp", None),
            P("tp", None),
            P("tp"),
            P("tp", None),
        ),
        check_vma=False,
    )
```

```python
import functools

import jax
import jax.numpy as jnp
from jax import lax
from jax.experimental import pallas as pl
from jax.experimental.pallas import tpu as pltpu
from jax.sharding import PartitionSpec as P

EPS = 1e-05
F32 = jnp.float32
BF16 = jnp.bfloat16
MESH = pl.DeviceIdType.MESH

TP = 8
SEQ = 64
NZ = 8
NY = 4
CH = 192
FR = 512
D = CH * TP
TAPS = 32
REACH = TAPS // 2
PAD = 128
WIDE = FR + 2 * PAD
HALF = CH // 2
ZR = HALF // 2
ZL = D // 4
SR = CH // NZ
BLK = 32
VMEM_LIMIT = 48 * 1024 * 1024
GAIN_CONV = TAPS
GAIN_NORM = TAPS + 1


def fold8(v):
    out = v[0:8]
    for i in range(8, v.shape[0], 8):
        out = out + v[i : i + 8]
    return out


def row_block(i, blk):
    return pl.ds(pl.multiple_of(i * blk, blk), blk)


def put_tile(ref, a, b):
    for j in range(4):
        ref[j : j + 1, :] = a[:, 128 * j : 128 * j + 128]
        ref[4 + j : 5 + j, :] = b[:, 128 * j : 128 * j + 128]


def tile_row(t):
    return jnp.concatenate([t[j : j + 1] for j in range(4)], axis=1)


def kernel(
    x_hbm, ng_hbm, wv_hbm, wg_hbm, dk_hbm, cg_hbm, wo_hbm, cot_hbm,
    *rest,
):
    landed, rest = rest[0:7], rest[7:]
    block_out, input_grad, gval_out, ggate_out, gout_out, small_out, norm_out = landed
    (
        ng_ref, wv_ref, wg_ref, dk_ref, cg_ref, wo_ref, cot_ref, par_t, par_ref,
        hat_in, value, sig, conv, hatc, dact,
        x_all, gains_t, gains, st0_s, st0_r, normed, act_all, da_s, dn_s, rs_r,
        glu_w, dcv_w, dv_b, dg_b, prod,
        st_s, st_r,
        g16, c1, s16, zr, y16, yr, r16,
        ncol, nt_s, nt_z, nt_y, nt_c, sm_s, sm_c, sm_t, sm_z, sm_y, sm_r,
        ld,
        st_ss, st_rs, ag_ss, ag_rs, rs_ss, rs_rs, ha_ss, ha_rs,
        c1_ss, c1_rs, z_ss, z_rs, y_ss, y_rs, w_ss, w_rs, f_ss, f_rs,
        nz_ss, nz_rs, ny_ss, ny_rs, nc_ss, nc_rs, sc_ss, sc_rs, sz_ss, sz_rs, sy_ss, sy_rs, sw_ss, sw_rs,
    ) = rest
    p = lax.axis_index("tp")
    fetch = (
        (x_hbm, x_all.at[p]), (dk_hbm, dk_ref), (cg_hbm, cg_ref), (ng_hbm, ng_ref),
        (wo_hbm, wo_ref), (cot_hbm, cot_ref), (wv_hbm, wv_ref), (wg_hbm, wg_ref),
    )
    loads = [pltpu.make_async_copy(src, dst, ld.at[i]) for i, (src, dst) in enumerate(fetch)]
    for copy in loads:
        copy.start()
    q = lax.axis_index("seq")
    core = lax.rem(q, 2)
    chip = q // 2
    z = lax.rem(chip, NZ)
    yh = chip // NZ
    scale = float(FR * SEQ) ** (-0.5)
    sends = []

    sems = {
        "st": (st_ss, st_rs), "ag": (ag_ss, ag_rs), "rs": (rs_ss, rs_rs), "ha": (ha_ss, ha_rs),
        "c1": (c1_ss, c1_rs), "z": (z_ss, z_rs), "y": (y_ss, y_rs), "w": (w_ss, w_rs), "f": (f_ss, f_rs),
        "nz": (nz_ss, nz_rs), "ny": (ny_ss, ny_rs), "nc": (nc_ss, nc_rs), "sc": (sc_ss, sc_rs), "sz": (sz_ss, sz_rs), "sy": (sy_ss, sy_rs), "sw": (sw_ss, sw_rs),
    }

    def remote(src, dst, key, dev):
        out, into = sems[key[0]]
        return pltpu.make_async_remote_copy(
            src_ref=src, dst_ref=dst, send_sem=out.at[key[1:]], recv_sem=into.at[key[1:]],
            device_id=dev, device_id_type=MESH,
        )

    def send(src, dst, key, dev):
        copy = remote(src, dst, key, dev)
        copy.start()
        sends.append(copy)

    def arrived(dst, key, dev):
        remote(dst, dst, key, dev).wait_recv()

    tx, ty = p // 2, lax.rem(p, 2)

    def at_tp(dx, dy):
        return lax.rem(tx + dx, 4) * 2 + lax.rem(ty + dy, 2)

    def hop(dx, dy):
        return {"tp": at_tp(dx, dy), "seq": q}

    def half(h):
        return pl.ds(h * HALF, HALF)

    def tp_dev(k):
        return {"tp": lax.rem(p + k, TP), "seq": q}

    def z_dev(k):
        return {"tp": p, "seq": (yh * NZ + lax.rem(z + k, NZ)) * 2 + core}

    def y_dev(k):
        return {"tp": p, "seq": (lax.rem(yh + k, NY) * NZ + z) * 2 + core}

    mate = {"tp": p, "seq": chip * 2 + (1 - core)}
    right = {"tp": p, "seq": lax.rem(q + 1, SEQ)}
    left = {"tp": p, "seq": lax.rem(q + SEQ - 1, SEQ)}

    barrier = pltpu.get_barrier_semaphore()
    peers = [tp_dev(k) for k in range(1, TP)] + [z_dev(k) for k in range(1, NZ)]
    peers += [y_dev(k) for k in range(1, NY)] + [mate, right, left]
    for dev in peers:
        pl.semaphore_signal(barrier, inc=1, device_id=dev, device_id_type=MESH)

    zero8 = jnp.zeros((8, FR), F32)

    def loop(n, body, init):
        return lax.fori_loop(0, n, body, init)

    def collapse(v):
        return jnp.sum(v, axis=0, keepdims=True)

    def local_moments(rows, tile):
        total = loop(CH // BLK, lambda i, a: a + fold8(rows(row_block(i, BLK))), zero8)
        mean = collapse(total) / CH

        def body(i, a):
            c = rows(row_block(i, BLK)) - mean
            return a + fold8(c * c)

        put_tile(tile, mean, collapse(loop(CH // BLK, body, zero8)))

    def share(slot):
        st_r[slot, p] = st_s[slot]
        for k in range(1, TP):
            send(st_s.at[slot], st_r.at[slot, p], ("st", slot, k - 1), tp_dev(k))

    def shared(slot):
        for k in range(1, TP):
            arrived(st_r.at[slot, lax.rem(p + TP - k, TP)], ("st", slot, k - 1), tp_dev(k))
        return [st_r[slot, j] for j in range(TP)]

    def merged(parts):
        total = parts[0]
        for t in parts[1:]:
            total = total + t
        mean = total[0:4] / TP
        spread = total[4:8]
        for t in parts:
            off = t[0:4] - mean
            spread = spread + CH * (off * off)
        inverse = lax.rsqrt(spread / D + EPS)
        return tile_row(mean), tile_row(inverse)

    def summed(slot):
        parts = shared(slot)
        total = parts[0]
        for t in parts[1:]:
            total = total + t
        return tile_row(total[0:4]) / D, tile_row(total[4:8]) / D

    RIGHT, LEFT, SIDE = (1, 0), (3, 0), (0, 1)

    gather_plan = (
        ((0, 0), 0, RIGHT), ((0, 0), 1, RIGHT), ((0, 0), 1, LEFT), ((0, 0), 0, LEFT),
        ((0, 0), 0, SIDE), ((0, 0), 1, SIDE), ((3, 0), 0, RIGHT), ((1, 0), 1, LEFT),
        ((0, 1), 0, RIGHT), ((0, 1), 0, LEFT), ((3, 0), 1, SIDE), ((1, 0), 1, SIDE),
        ((2, 0), 1, SIDE), ((3, 1), 0, RIGHT),
    )

    def gather_put(buf, n, i):
        (dx, dy), h, to = gather_plan[i]
        piece = buf.at[at_tp(dx, dy), half(h), :]
        send(piece, piece, ("ag", n, i), hop(*to))

    def gather_got(buf, n, i):
        (dx, dy), h, to = gather_plan[i]
        piece = buf.at[at_tp(dx + 4 - to[0], dy + to[1]), half(h), :]
        arrived(piece, ("ag", n, i), hop(*to))

    def gather_send(buf, n):
        for i in (0, 2, 4, 1, 3, 5):
            gather_put(buf, n, i)

    def gather_relay(buf, n):
        gather_got(buf, n, 4)
        gather_put(buf, n, 8)
        gather_got(buf, n, 2)
        gather_put(buf, n, 7)
        gather_put(buf, n, 11)
        gather_got(buf, n, 0)
        gather_put(buf, n, 6)
        gather_put(buf, n, 9)
        gather_got(buf, n, 1)
        gather_put(buf, n, 10)

    def gather_last(buf, n):
        gather_got(buf, n, 7)
        gather_put(buf, n, 12)
        gather_got(buf, n, 8)
        gather_put(buf, n, 13)

    def gather_wait(buf, n):
        for i in (3, 5, 6, 9, 10, 11, 12, 13):
            gather_got(buf, n, i)

    scatter_plan = (
        ((3, 0), 0, LEFT), ((3, 0), 1, LEFT), ((1, 0), 1, RIGHT), ((1, 0), 0, RIGHT),
        ((0, 1), 0, SIDE), ((0, 1), 1, SIDE), ((2, 0), 0, LEFT), ((2, 0), 1, RIGHT),
        ((3, 1), 0, LEFT), ((1, 1), 0, RIGHT), ((3, 1), 1, SIDE), ((1, 1), 1, SIDE),
        ((2, 1), 1, SIDE), ((2, 1), 0, LEFT),
    )

    def scatter_put(buf, n, i, merge=()):
        (dx, dy), h, to = scatter_plan[i]
        d = at_tp(dx, dy)
        for m in merge:
            arrived(rs_r.at[n, m], ("rs", n, m), hop(*scatter_plan[m][2]))
        if merge:

            def body(j, c):
                r = pl.ds(pl.multiple_of(h * HALF + j * BLK, BLK), BLK)
                total = buf[d, r, :].astype(F32)
                for m in merge:
                    total = total + rs_r[n, m, row_block(j, BLK), :].astype(F32)
                buf[d, r, :] = total.astype(BF16)
                return c

            loop(HALF // BLK, body, 0)
        send(buf.at[d, half(h), :], rs_r.at[n, i], ("rs", n, i), hop(*to))

    def scatter_send(buf, n):
        for i in (13, 12, 9, 6, 10, 3, 11, 5):
            scatter_put(buf, n, i)

    def scatter_relay(buf, n):
        scatter_put(buf, n, 8, (13,))
        scatter_put(buf, n, 7, (12,))
        scatter_put(buf, n, 0, (6,))
        scatter_put(buf, n, 1, (10,))

    def scatter_last(buf, n):
        scatter_put(buf, n, 4, (8, 9))
        scatter_put(buf, n, 2, (7, 11))

    def scatter_wait(n):
        for m in range(6):
            arrived(rs_r.at[n, m], ("rs", n, m), hop(*scatter_plan[m][2]))

    def scatter_sum(buf, n, r, j, h):
        total = buf[p, r, :].astype(F32)
        for m in ((0, 3, 4), (1, 2, 5))[h]:
            total = total + rs_r[n, m, row_block(j, BLK), :].astype(F32)
        return total

    def halo_send(buf, n):
        send(buf.at[:, PAD : 2 * PAD], buf.at[:, PAD + FR : WIDE], ("ha", n, 0), left)
        send(buf.at[:, FR : FR + PAD], buf.at[:, 0:PAD], ("ha", n, 1), right)

    def halo_wait(buf, n):
        arrived(buf.at[:, PAD + FR : WIDE], ("ha", n, 0), left)
        arrived(buf.at[:, 0:PAD], ("ha", n, 1), right)

        @pl.when(q == 0)
        def _():
            buf[:, 0:PAD] = jnp.zeros((CH, PAD), buf.dtype)

        @pl.when(q == SEQ - 1)
        def _():
            buf[:, PAD + FR : WIDE] = jnp.zeros((CH, PAD), buf.dtype)

    def contract_rows(w, v):
        return lax.dot_general(w, v, (((0,), (0,)), ((), ())), preferred_element_type=F32)

    def contract_cols(a, b):
        return lax.dot_general(a, b, (((1,), (1,)), ((), ())), preferred_element_type=F32)

    for copy in loads[0:4]:
        copy.wait()
    par_t[...] = jnp.zeros((128, 2 * 128), F32)
    par_t[0:TAPS, 0:CH] = dk_ref[...]
    par_t[GAIN_CONV : GAIN_CONV + 1, 0:CH] = cg_ref[...]
    par_t[GAIN_NORM : GAIN_NORM + 1, 0:CH] = ng_ref[...]
    par_ref[...] = par_t[...].T[0:CH]

    local_moments(lambda r: x_all[p, r, :].astype(F32), st0_s)
    st0_s[8:16, :] = jnp.zeros((8, 128), F32)
    st0_s[8:9, :] = par_t[GAIN_NORM : GAIN_NORM + 1, 0:128]
    st0_s[9:10, :] = par_t[GAIN_NORM : GAIN_NORM + 1, 128:256]
    pl.semaphore_wait(barrier, len(peers))
    st0_r[p] = st0_s[...]
    for k in range(1, TP):
        send(st0_s, st0_r.at[p], ("st", 0, k - 1), tp_dev(k))
    gather_send(x_all, 0)

    loads[4].wait()
    loads[5].wait()
    def dact_body(d, c):
        lanes = pl.ds(pl.multiple_of(d * (2 * CH), 128), 2 * CH)
        term = contract_rows(wo_ref[:, lanes], cot_ref[...]).astype(BF16)
        da_s[2 * d] = term[0:CH]
        da_s[2 * d + 1] = term[CH : 2 * CH]
        return c

    loop(TP // 2, dact_body, 0)
    gather_relay(x_all, 0)
    gather_last(x_all, 0)

    for k in range(1, TP):
        arrived(st0_r.at[lax.rem(p + TP - k, TP)], ("st", 0, k - 1), tp_dev(k))
    gains_t[...] = jnp.zeros((128, 256), F32)
    for j in range(TP):
        gains_t[j : j + 1, 0:128] = st0_r[j, 8:9, :]
        gains_t[j : j + 1, 128:256] = st0_r[j, 9:10, :]
    gains[...] = gains_t[...].T
    mean_in, inv_in = merged([st0_r[j] for j in range(TP)])

    def own_body(i, c):
        r = row_block(i, BLK)
        h = (x_all[p, r, :].astype(F32) - mean_in) * inv_in
        hat_in[r, :] = h
        normed[p, r, :] = (h * par_ref[r, GAIN_NORM : GAIN_NORM + 1]).astype(BF16)
        return c

    loop(CH // BLK, own_body, 0)
    scatter_send(da_s, 0)
    loads[6].wait()
    loads[7].wait()
    gather_wait(x_all, 0)
    for j in range(TP):

        @pl.when(p != j)
        def _():
            def body(i, c):
                r = row_block(i, BLK)
                h = (x_all[j, r, :].astype(F32) - mean_in) * inv_in
                normed[j, r, :] = (h * gains[r, j : j + 1]).astype(BF16)
                return c

            loop(CH // BLK, body, 0)

    def glu_part(low, high):
        part = normed[:, :, low:high].reshape(D, high - low)
        v = jnp.dot(wv_ref[...], part, preferred_element_type=F32)
        s = jax.nn.sigmoid(jnp.dot(wg_ref[...], part, preferred_element_type=F32))
        value[:, low:high] = v
        sig[:, low:high] = s
        glu_w[:, PAD + low : PAD + high] = (v * s).astype(BF16)

    glu_part(0, 128)
    glu_part(FR - 128, FR)
    halo_send(glu_w, 0)
    glu_part(128, FR - 128)
    scatter_relay(da_s, 0)
    halo_wait(glu_w, 0)

    def conv_body(i, c):
        r = row_block(i, 16)
        w = glu_w[r, :].astype(F32)
        taps = par_ref[r, 0:TAPS]
        spans = ((0, FR + PAD), (0, FR + PAD), (PAD, FR + PAD), (PAD, WIDE))
        acc = [None] * 4
        for b in range(8):
            moved = pltpu.roll(w, WIDE - b, 1) if b else w
            for a in range(4):
                k = 8 * a + b
                term = taps[:, k : k + 1] * moved[:, spans[a][0] : spans[a][1]]
                acc[a] = term if acc[a] is None else acc[a] + term
        total = acc[2] + pltpu.roll(acc[0], 16, 1)[:, PAD:] + pltpu.roll(acc[1], 8, 1)[:, PAD:]
        conv[r, :] = total + pltpu.roll(acc[3], FR + PAD - 8, 1)[:, 0:FR]
        return c

    lax.fori_loop(0, CH // 32, conv_body, 0)
    scatter_last(da_s, 0)
    lax.fori_loop(CH // 32, CH // 16, conv_body, 0)
    local_moments(lambda r: conv[r, :], st_s.at[1])
    share(1)

    scatter_wait(0)
    for h in range(2):

        def dsum_body(j, c):
            r = pl.ds(pl.multiple_of(h * HALF + j * BLK, BLK), BLK)
            dact[r, :] = scatter_sum(da_s, 0, r, j, h)
            return c

        loop(HALF // BLK, dsum_body, 0)
    mean_c, inv_c = merged(shared(1))

    def act_body(i, carry):
        a, b = carry
        r = row_block(i, BLK)
        h = (conv[r, :] - mean_c) * inv_c
        hatc[r, :] = h
        g = par_ref[r, GAIN_CONV : GAIN_CONV + 1]
        scaled = h * g
        s = jax.nn.sigmoid(scaled)
        act_all[p, r, :] = (scaled * s).astype(BF16)
        ds = dact[r, :] * (s + scaled * s * (1.0 - s))
        sm_s[r, GAIN_CONV : GAIN_CONV + 1] = jnp.sum(ds * h, axis=1, keepdims=True)
        e = ds * g
        dact[r, :] = e
        return a + fold8(e), b + fold8(e * h)

    sm_s[...] = jnp.zeros((CH, 128), F32)
    first, second = loop(CH // BLK, act_body, (zero8, zero8))
    put_tile(st_s.at[2], collapse(first), collapse(second))
    share(2)
    gather_send(act_all, 1)
    first, second = summed(2)

    def dconv_body(i, c):
        r = row_block(i, BLK)
        dcv_w[r, PAD : PAD + FR] = ((dact[r, :] - first - hatc[r, :] * second) * inv_c).astype(BF16)
        return c

    loop(CH // BLK, dconv_body, 0)
    halo_send(dcv_w, 1)
    gather_relay(act_all, 1)
    halo_wait(dcv_w, 1)

    at_end = (q == SEQ - 1).astype(F32)

    def back_body(i, c):
        r = row_block(i, 16)
        w = dcv_w[r, :].astype(F32)
        taps = par_ref[r, 0:TAPS]
        u = glu_w[r, :].astype(F32)
        spans = ((PAD, WIDE), (PAD, WIDE), (PAD, FR + PAD), (0, FR + PAD))
        glus = []
        for a in range(4):
            g = pltpu.roll(u, (16 - 8 * a) % WIDE, 1) if a != 2 else u
            glus.append((g[:, PAD : PAD + FR], g[:, PAD + FR :] * at_end if a < 2 else None))
        acc = [None] * 4
        for b in range(8):
            moved = pltpu.roll(w, b, 1) if b else w
            for a in range(4):
                k = 8 * a + b
                term = taps[:, k : k + 1] * moved[:, spans[a][0] : spans[a][1]]
                acc[a] = term if acc[a] is None else acc[a] + term
                body, tail = glus[a]
                m = body * moved[:, PAD : PAD + FR]
                m = (m[:, 0:128] + m[:, 128:256]) + (m[:, 256:384] + m[:, 384:512])
                if tail is not None and b:
                    m = m + tail * moved[:, PAD + FR :]
                prod[k, r, :] = m
        total = acc[2] + pltpu.roll(acc[0], FR + PAD - 16, 1)[:, 0:FR]
        total = total + pltpu.roll(acc[1], FR + PAD - 8, 1)[:, 0:FR] + pltpu.roll(acc[3], 8, 1)[:, PAD:]
        s = sig[r, :]
        dv = total * s
        dv_b[r, :] = dv.astype(BF16)
        dg_b[r, :] = (dv * value[r, :] * (1.0 - s)).astype(BF16)
        return c

    lax.fori_loop(0, CH // 32, back_body, 0)
    gather_last(act_all, 1)
    lax.fori_loop(CH // 32, CH // 16, back_body, 0)

    other = pl.ds(pl.multiple_of((1 - core) * HALF, HALF), HALF)
    mine = pl.ds(pl.multiple_of(core * HALF, HALF), HALF)

    def pair_send(g):
        send(g16.at[g, other, :], c1.at[g], ("c1", g), mate)

    def weight_grad(g, left_ref, all_ref):
        g16[g] = contract_cols(left_ref[...], all_ref[...].reshape(D, FR)).astype(BF16)
        pair_send(g)

    weight_grad(0, dv_b, normed)
    weight_grad(1, dg_b, normed)

    def dn_pair(dx, entries):
        xx = lax.rem(tx + dx, 4)
        lanes = pl.ds(pl.multiple_of(xx * (2 * CH), 128), 2 * CH)
        term = contract_rows(wv_ref[:, lanes], dv_b[...]) + contract_rows(wg_ref[:, lanes], dg_b[...])
        term = term.astype(BF16)
        dn_s[2 * xx] = term[0:CH]
        dn_s[2 * xx + 1] = term[CH : 2 * CH]
        for i in entries:
            scatter_put(dn_s, 1, i)

    def z_block(zz):
        return (
            pl.ds(pl.multiple_of((zz // 4) * ZR, 16), ZR),
            pl.ds(pl.multiple_of(lax.rem(zz, 4) * ZL, 128), ZL),
        )

    def chains(g):
        sign = 1 if g % 2 == 0 else NZ - 1
        return ((0, 4, sign), (1, 3, NZ - sign))

    def z_start(g):
        arrived(c1.at[g], ("c1", g), mate)
        s16[g] = (g16[g, mine, :].astype(F32) + c1[g].astype(F32)).astype(BF16)
        z_hop(g, 1)

    def z_got(g, i, sign):
        arrived(zr.at[g, i], ("z", g, i), z_dev(sign))
        return zr[g, i].astype(F32)

    def z_hop(g, step):
        for chain, n, sign in chains(g):
            if step <= n:
                rr, ll = z_block(lax.rem(z + sign * (n + 1 - step), NZ))
                i = chain * 4 + step - 1
                if step > 1:
                    s16[g, rr, ll] = (s16[g, rr, ll].astype(F32) + z_got(g, i - 1, sign)).astype(BF16)
                send(s16.at[g, rr, ll], zr.at[g, i], ("z", g, i), z_dev(sign))

    def y_send(g):
        rr, ll = z_block(z)
        total = s16[g, rr, ll].astype(F32)
        for chain, n, sign in chains(g):
            total = total + z_got(g, chain * 4 + n - 1, sign)
        y16[g] = total.astype(BF16)
        yr[g, yh] = total.astype(BF16)
        for k in range(1, NY):
            send(y16.at[g], yr.at[g, yh], ("y", g, k - 1), y_dev(k))

    outs = (gval_out, ggate_out, gout_out)

    def out_block(zz, cc):
        rr, ll = z_block(zz)
        return pl.ds(pl.multiple_of(cc * HALF + (zz // 4) * ZR, 16), ZR), ll

    def w_start(g):
        for k in range(1, NY):
            arrived(yr.at[g, lax.rem(yh + NY - k, NY)], ("y", g, k - 1), y_dev(k))
        total = yr[g, 0].astype(F32)
        for j in range(1, NY):
            total = total + yr[g, j].astype(F32)
        r16[g] = (total * scale).astype(BF16)
        rr, ll = out_block(z, core)
        outs[g][rr, ll] = r16[g]
        for chain, n, sign in chains(g):
            send(r16.at[g], outs[g].at[rr, ll], ("w", g, chain * 4), z_dev(sign))
        send(r16.at[g], outs[g].at[rr, ll], ("f", g, 0), mate)

    def w_hop(g, step):
        for chain, n, sign in chains(g):
            if step <= n + 1:
                i = chain * 4 + step - 2
                rr, ll = out_block(lax.rem(z + (NZ - sign) * (step - 1), NZ), core)
                piece = outs[g].at[rr, ll]
                arrived(piece, ("w", g, i), z_dev(sign))
                if step <= n:
                    send(piece, piece, ("w", g, i + 1), z_dev(sign))
                send(piece, piece, ("f", g, 1 + i), mate)

    def f_wait(g):
        rr, ll = out_block(z, 1 - core)
        arrived(outs[g].at[rr, ll], ("f", g, 0), mate)
        for chain, n, sign in chains(g):
            for step in range(2, n + 2):
                rr, ll = out_block(lax.rem(z + (NZ - sign) * (step - 1), NZ), 1 - core)
                arrived(outs[g].at[rr, ll], ("f", g, 1 + chain * 4 + step - 2), mate)

    gather_wait(act_all, 1)
    weight_grad(2, cot_ref, act_all)
    z_start(0)
    z_start(1)
    dn_pair(2, (13, 12, 6))
    z_start(2)
    dn_pair(1, (9, 3, 11))
    z_hop(0, 2)
    z_hop(1, 2)
    dn_pair(3, (10,))
    dn_pair(0, (5,))
    z_hop(2, 2)
    z_hop(0, 3)
    z_hop(1, 3)
    scatter_relay(dn_s, 1)
    z_hop(2, 3)

    for k in range(TAPS):
        sm_s[:, k : k + 1] = jnp.sum(prod[k], axis=1, keepdims=True)
    send(sm_s, sm_c, ("sc", 0), mate)

    z_hop(0, 4)
    z_hop(1, 4)
    scatter_last(dn_s, 1)
    z_hop(2, 4)
    y_send(0)
    y_send(1)
    y_send(2)

    def sm_rows(zz):
        return pl.ds(pl.multiple_of(zz * SR, 8), SR)

    arrived(sm_c, ("sc", 0), mate)
    sm_t[...] = sm_s[...] + sm_c[...]

    for k in range(1, NZ):
        send(sm_t.at[sm_rows(lax.rem(z + k, NZ)), :], sm_z.at[z], ("sz", k - 1), z_dev(k))
    sm_z[z] = sm_t[sm_rows(z), :]

    value[...] = jnp.dot(wo_ref[...], act_all[...].reshape(D, FR), preferred_element_type=F32)

    def out_body(i, c):
        r = row_block(i, BLK)
        block_out[r, :] = (x_all[p, r, :].astype(F32) + value[r, :]).astype(BF16)
        return c

    loop(CH // BLK, out_body, 0)

    ncol[...] = jnp.zeros((256, 128), F32)
    scatter_wait(1)

    carry = (zero8, zero8)
    for h in range(2):

        def dnorm_body(j, carry):
            a, b = carry
            r = pl.ds(pl.multiple_of(h * HALF + j * BLK, BLK), BLK)
            total = scatter_sum(dn_s, 1, r, j, h)
            hat = hat_in[r, :]
            ncol[r, 0:1] = jnp.sum(total * hat, axis=1, keepdims=True)
            e = total * par_ref[r, GAIN_NORM : GAIN_NORM + 1]
            dact[r, :] = e
            return a + fold8(e), b + fold8(e * hat)

        carry = loop(HALF // BLK, dnorm_body, carry)
    first, second = carry
    put_tile(st_s.at[3], collapse(first), collapse(second))
    share(3)

    def all_sum(buf, count):
        total = buf[0]
        for j in range(1, count):
            total = total + buf[j]
        return total

    flat = ncol[...].T
    nt_s[0] = jnp.zeros((8, 128), F32)
    nt_s[0, 0:1] = flat[0:1, 0:128]
    nt_s[0, 1:2] = flat[0:1, 128:256]
    nt_z[z] = nt_s[0]
    for k in range(1, NZ):
        send(nt_s.at[0], nt_z.at[z], ("nz", k - 1), z_dev(k))

    for k in range(1, NZ):
        arrived(sm_z.at[lax.rem(z + NZ - k, NZ)], ("sz", k - 1), z_dev(k))
    total = all_sum(sm_z, NZ)
    sm_r[0] = total
    sm_y[yh] = total
    for k in range(1, NY):
        send(sm_r.at[0], sm_y.at[yh], ("sy", k - 1), y_dev(k))

    w_start(0)
    w_start(1)
    w_start(2)
    w_hop(0, 2)
    w_hop(1, 2)

    first, second = summed(3)

    def grad_body(i, c):
        r = row_block(i, BLK)
        back = (dact[r, :] - first - hat_in[r, :] * second) * inv_in
        input_grad[r, :] = (cot_ref[r, :].astype(F32) + back).astype(BF16)
        return c

    loop(CH // BLK, grad_body, 0)
    for k in range(1, NZ):
        arrived(nt_z.at[lax.rem(z + NZ - k, NZ)], ("nz", k - 1), z_dev(k))
    nt_s[1] = all_sum(nt_z, NZ)
    nt_y[yh] = nt_s[1]
    for k in range(1, NY):
        send(nt_s.at[1], nt_y.at[yh], ("ny", k - 1), y_dev(k))

    for k in range(1, NY):
        arrived(sm_y.at[lax.rem(yh + NY - k, NY)], ("sy", k - 1), y_dev(k))
    total = all_sum(sm_y, NY)
    sm_r[1] = total * scale
    small_out[sm_rows(z), :] = total * scale
    for k in range(1, NZ):
        send(sm_r.at[1], small_out.at[sm_rows(z), :], ("sw", k - 1), z_dev(k))

    w_hop(2, 2)
    w_hop(0, 3)
    w_hop(1, 3)
    w_hop(2, 3)
    w_hop(0, 4)
    w_hop(1, 4)
    for k in range(1, NY):
        arrived(nt_y.at[lax.rem(yh + NY - k, NY)], ("ny", k - 1), y_dev(k))
    nt_s[2] = all_sum(nt_y, NY)
    send(nt_s.at[2], nt_c, ("nc", 0), mate)

    w_hop(2, 4)
    w_hop(0, 5)
    w_hop(1, 5)
    w_hop(2, 5)
    for k in range(1, NZ):
        arrived(small_out.at[sm_rows(lax.rem(z + NZ - k, NZ)), :], ("sw", k - 1), z_dev(k))
    arrived(nt_c, ("nc", 0), mate)
    norm_out[...] = (nt_s[2] + nt_c[...]) * scale
    for g in range(3):
        f_wait(g)
    for copy in sends:
        copy.wait_send()


def copy_out(*refs):
    ins, outs, sem = refs[0:7], refs[7:15], refs[15]
    small, norm = ins[5], ins[6]
    stores = [pltpu.make_async_copy(ins[i], outs[i], sem.at[i]) for i in range(5)]
    for copy in stores:
        copy.start()
    outs[7][:, 0:128] = norm[0:1, :]
    outs[7][:, 128:CH] = norm[1:2, 0 : CH - 128]
    cols = jnp.concatenate([small[...], jnp.zeros((2 * 128 - CH, 128), F32)], axis=0).T
    outs[5][...] = cols[0:TAPS, 0:CH]
    outs[6][...] = cols[GAIN_CONV : GAIN_CONV + 1, 0:CH]
    for copy in stores:
        copy.wait()


def local(
    frames_in, norm_gain, value_weight, gate_weight, depth_kernel, conv_gain, out_weight, cotangent
):
    act = jax.ShapeDtypeStruct((CH, FR), BF16)
    mat = jax.ShapeDtypeStruct((CH, D), BF16)
    row = jax.ShapeDtypeStruct((1, CH), F32)
    vm = pltpu.VMEM
    dma = pltpu.SemaphoreType.DMA
    full = vm((CH, FR), F32)
    eight = vm((TP, CH, FR), BF16)
    wide = vm((CH, WIDE), BF16)
    block = vm((CH, FR), BF16)
    weight = vm((CH, D), BF16)
    small = vm((CH, 128), F32)
    line = vm((1, CH), F32)
    tile = vm((8, 128), F32)
    scratch = [line, weight, weight, vm((TAPS, CH), F32), line, weight, block, vm((128, 256), F32), small] + [full] * 6
    scratch += [eight, vm((128, 256), F32), vm((256, 128), F32), vm((16, 128), F32), vm((TP, 16, 128), F32)]
    scratch += [eight] * 4
    scratch += [vm((2, 14, HALF, FR), BF16), wide, wide, block, block, vm((TAPS, CH, 128), F32)]
    scratch += [vm((4, 8, 128), F32), vm((4, TP, 8, 128), F32)]
    scratch += [
        vm((3, CH, D), BF16),
        vm((3, HALF, D), BF16),
        vm((3, HALF, D), BF16),
        vm((3, 8, ZR, ZL), BF16),
        vm((3, ZR, ZL), BF16),
        vm((3, NY, ZR, ZL), BF16),
        vm((3, ZR, ZL), BF16),
    ]
    scratch += [vm((256, 128), F32), vm((3, 8, 128), F32), vm((NZ, 8, 128), F32), vm((NY, 8, 128), F32), tile]
    scratch += [small, small, small, vm((NZ, SR, 128), F32), vm((NY, SR, 128), F32), vm((2, SR, 128), F32)]
    scratch += [dma((8,))]
    for shape in ((4, 7), (2, 14), (2, 14), (2, 2), (3,), (3, 8), (3, 3), (3, 8), (3, 8), (7,), (3,), (1,), (1,), (7,), (3,), (7,)):
        scratch += [dma(shape), dma(shape)]
    vmem = pl.BlockSpec(memory_space=pltpu.VMEM)
    anywhere = pl.BlockSpec(memory_space=pl.ANY)
    hbm = pl.BlockSpec(memory_space=pltpu.HBM)
    results = pl.pallas_call(
        kernel,
        out_shape=(act, act, mat, mat, mat, jax.ShapeDtypeStruct((CH, 128), F32), jax.ShapeDtypeStruct((8, 128), F32)),
        in_specs=[hbm] * 8,
        out_specs=(vmem,) * 7,
        scratch_shapes=scratch,
        compiler_params=pltpu.CompilerParams(
            collective_id=0, has_side_effects=True, vmem_limit_bytes=VMEM_LIMIT
        ),
    )(
        pltpu.with_memory_space_constraint(frames_in, pltpu.HBM),
        pltpu.with_memory_space_constraint(norm_gain.reshape(1, CH), pltpu.HBM),
        pltpu.with_memory_space_constraint(value_weight, pltpu.HBM),
        pltpu.with_memory_space_constraint(gate_weight, pltpu.HBM),
        pltpu.with_memory_space_constraint(depth_kernel.T, pltpu.HBM),
        pltpu.with_memory_space_constraint(conv_gain.reshape(1, CH), pltpu.HBM),
        pltpu.with_memory_space_constraint(out_weight, pltpu.HBM),
        pltpu.with_memory_space_constraint(cotangent, pltpu.HBM),
    )
    block_out, input_grad, gval, ggate, gout, gkernel, gconv, gnorm = pl.pallas_call(
        copy_out,
        out_shape=(act, act, mat, mat, mat, jax.ShapeDtypeStruct((TAPS, CH), F32), row, row),
        in_specs=[vmem] * 7,
        out_specs=(anywhere,) * 5 + (vmem,) * 3,
        scratch_shapes=[dma((5,))],
        compiler_params=pltpu.CompilerParams(vmem_limit_bytes=8 * 1024 * 1024),
    )(*results)
    return (
        block_out,
        input_grad,
        gnorm.reshape(CH),
        gval,
        ggate,
        gkernel.T,
        gconv.reshape(CH),
        gout,
    )


def solution(mesh):
    return jax.shard_map(
        local,
        mesh=mesh,
        in_specs=(
            P("tp", "seq"),
            P("tp"),
            P("tp", None),
            P("tp", None),
            P("tp", None),
            P("tp"),
            P("tp", None),
            P("tp", "seq"),
        ),
        out_specs=(
            P("tp", "seq"),
            P("tp", "seq"),
            P("tp"),
            P("tp", None),
            P("tp", None),
            P("tp", None),
            P("tp"),
            P("tp", None),
        ),
        check_vma=False,
    )
```

```python
import functools

import jax
import jax.numpy as jnp
from jax import lax
from jax.experimental import pallas as pl
from jax.experimental.pallas import tpu as pltpu
from jax.sharding import PartitionSpec as P

EPS = 1e-05
F32 = jnp.float32
BF16 = jnp.bfloat16
MESH = pl.DeviceIdType.MESH

TP = 8
SEQ = 64
NZ = 8
NY = 4
CH = 192
FR = 512
D = CH * TP
TAPS = 32
REACH = TAPS // 2
PAD = 128
WIDE = FR + 2 * PAD
HALF = CH // 2
ZR = HALF // 2
ZL = D // 4
SR = CH // NZ
BLK = 32
VMEM_LIMIT = 48 * 1024 * 1024
GAIN_CONV = TAPS
GAIN_NORM = TAPS + 1


def fold8(v):
    out = v[0:8]
    for i in range(8, v.shape[0], 8):
        out = out + v[i : i + 8]
    return out


def row_block(i, blk):
    return pl.ds(pl.multiple_of(i * blk, blk), blk)


def put_tile(ref, a, b):
    for j in range(4):
        ref[j : j + 1, :] = a[:, 128 * j : 128 * j + 128]
        ref[4 + j : 5 + j, :] = b[:, 128 * j : 128 * j + 128]


def tile_row(t):
    return jnp.concatenate([t[j : j + 1] for j in range(4)], axis=1)


def kernel(
    x_hbm, ng_hbm, wv_hbm, wg_hbm, dk_hbm, cg_hbm, wo_hbm, cot_hbm,
    *rest,
):
    landed, rest = rest[0:7], rest[7:]
    block_out, input_grad, gval_out, ggate_out, gout_out, small_out, norm_out = landed
    (
        ng_ref, wv_ref, wg_ref, dk_ref, cg_ref, wo_ref, cot_ref, par_t, par_ref,
        hat_in, value, sig, conv, hatc, dact,
        x_all, gains_t, gains, st0_s, st0_r, normed, act_all, da_s, dn_s, rs_r,
        glu_w, dcv_w, dv_b, dg_b, prod,
        st_s, st_r,
        g16, c1, s16, zr, y16, yr, r16,
        ncol, nt_s, nt_z, nt_y, nt_c, sm_s, sm_c, sm_t, sm_z, sm_y, sm_r,
        ld,
        st_ss, st_rs, ag_ss, ag_rs, rs_ss, rs_rs, ha_ss, ha_rs,
        c1_ss, c1_rs, z_ss, z_rs, y_ss, y_rs, w_ss, w_rs, f_ss, f_rs,
        nz_ss, nz_rs, ny_ss, ny_rs, nc_ss, nc_rs, sc_ss, sc_rs, sz_ss, sz_rs, sy_ss, sy_rs, sw_ss, sw_rs,
    ) = rest
    p = lax.axis_index("tp")
    fetch = (
        (x_hbm, x_all.at[p]), (dk_hbm, dk_ref), (cg_hbm, cg_ref), (ng_hbm, ng_ref),
        (wo_hbm, wo_ref), (cot_hbm, cot_ref), (wv_hbm, wv_ref), (wg_hbm, wg_ref),
    )
    loads = [pltpu.make_async_copy(src, dst, ld.at[i]) for i, (src, dst) in enumerate(fetch)]
    for copy in loads:
        copy.start()
    q = lax.axis_index("seq")
    core = lax.rem(q, 2)
    chip = q // 2
    z = lax.rem(chip, NZ)
    yh = chip // NZ
    scale = float(FR * SEQ) ** (-0.5)
    sends = []

    sems = {
        "st": (st_ss, st_rs), "ag": (ag_ss, ag_rs), "rs": (rs_ss, rs_rs), "ha": (ha_ss, ha_rs),
        "c1": (c1_ss, c1_rs), "z": (z_ss, z_rs), "y": (y_ss, y_rs), "w": (w_ss, w_rs), "f": (f_ss, f_rs),
        "nz": (nz_ss, nz_rs), "ny": (ny_ss, ny_rs), "nc": (nc_ss, nc_rs), "sc": (sc_ss, sc_rs), "sz": (sz_ss, sz_rs), "sy": (sy_ss, sy_rs), "sw": (sw_ss, sw_rs),
    }

    def remote(src, dst, key, dev):
        out, into = sems[key[0]]
        return pltpu.make_async_remote_copy(
            src_ref=src, dst_ref=dst, send_sem=out.at[key[1:]], recv_sem=into.at[key[1:]],
            device_id=dev, device_id_type=MESH,
        )

    def send(src, dst, key, dev):
        copy = remote(src, dst, key, dev)
        copy.start()
        sends.append(copy)

    def arrived(dst, key, dev):
        remote(dst, dst, key, dev).wait_recv()

    tx, ty = p // 2, lax.rem(p, 2)

    def at_tp(dx, dy):
        return lax.rem(tx + dx, 4) * 2 + lax.rem(ty + dy, 2)

    def hop(dx, dy):
        return {"tp": at_tp(dx, dy), "seq": q}

    def half(h):
        return pl.ds(h * HALF, HALF)

    def tp_dev(k):
        return {"tp": lax.rem(p + k, TP), "seq": q}

    def z_dev(k):
        return {"tp": p, "seq": (yh * NZ + lax.rem(z + k, NZ)) * 2 + core}

    def y_dev(k):
        return {"tp": p, "seq": (lax.rem(yh + k, NY) * NZ + z) * 2 + core}

    mate = {"tp": p, "seq": chip * 2 + (1 - core)}
    right = {"tp": p, "seq": lax.rem(q + 1, SEQ)}
    left = {"tp": p, "seq": lax.rem(q + SEQ - 1, SEQ)}

    barrier = pltpu.get_barrier_semaphore()
    peers = [tp_dev(k) for k in range(1, TP)] + [z_dev(k) for k in range(1, NZ)]
    peers += [y_dev(k) for k in range(1, NY)] + [mate, right, left]
    for dev in peers:
        pl.semaphore_signal(barrier, inc=1, device_id=dev, device_id_type=MESH)

    zero8 = jnp.zeros((8, FR), F32)

    def loop(n, body, init):
        return lax.fori_loop(0, n, body, init)

    def collapse(v):
        return jnp.sum(v, axis=0, keepdims=True)

    def local_moments(rows, tile):
        total = loop(CH // BLK, lambda i, a: a + fold8(rows(row_block(i, BLK))), zero8)
        mean = collapse(total) / CH

        def body(i, a):
            c = rows(row_block(i, BLK)) - mean
            return a + fold8(c * c)

        put_tile(tile, mean, collapse(loop(CH // BLK, body, zero8)))

    def share(slot):
        st_r[slot, p] = st_s[slot]
        for k in range(1, TP):
            send(st_s.at[slot], st_r.at[slot, p], ("st", slot, k - 1), tp_dev(k))

    def shared(slot):
        for k in range(1, TP):
            arrived(st_r.at[slot, lax.rem(p + TP - k, TP)], ("st", slot, k - 1), tp_dev(k))
        return [st_r[slot, j] for j in range(TP)]

    def merged(parts):
        total = parts[0]
        for t in parts[1:]:
            total = total + t
        mean = total[0:4] / TP
        spread = total[4:8]
        for t in parts:
            off = t[0:4] - mean
            spread = spread + CH * (off * off)
        inverse = lax.rsqrt(spread / D + EPS)
        return tile_row(mean), tile_row(inverse)

    def summed(slot):
        parts = shared(slot)
        total = parts[0]
        for t in parts[1:]:
            total = total + t
        return tile_row(total[0:4]) / D, tile_row(total[4:8]) / D

    RIGHT, LEFT, SIDE = (1, 0), (3, 0), (0, 1)

    gather_plan = (
        ((0, 0), 0, RIGHT), ((0, 0), 1, RIGHT), ((0, 0), 1, LEFT), ((0, 0), 0, LEFT),
        ((0, 0), 0, SIDE), ((0, 0), 1, SIDE), ((3, 0), 0, RIGHT), ((1, 0), 1, LEFT),
        ((0, 1), 0, RIGHT), ((0, 1), 0, LEFT), ((3, 0), 1, SIDE), ((1, 0), 1, SIDE),
        ((2, 0), 1, SIDE), ((3, 1), 0, RIGHT),
    )

    def gather_put(buf, n, i):
        (dx, dy), h, to = gather_plan[i]
        piece = buf.at[at_tp(dx, dy), half(h), :]
        send(piece, piece, ("ag", n, i), hop(*to))

    def gather_got(buf, n, i):
        (dx, dy), h, to = gather_plan[i]
        piece = buf.at[at_tp(dx + 4 - to[0], dy + to[1]), half(h), :]
        arrived(piece, ("ag", n, i), hop(*to))

    def gather_send(buf, n):
        for i in (0, 2, 4, 1, 3, 5):
            gather_put(buf, n, i)

    def gather_relay(buf, n):
        gather_got(buf, n, 4)
        gather_put(buf, n, 8)
        gather_got(buf, n, 2)
        gather_put(buf, n, 7)
        gather_put(buf, n, 11)
        gather_got(buf, n, 0)
        gather_put(buf, n, 6)
        gather_put(buf, n, 9)
        gather_got(buf, n, 1)
        gather_put(buf, n, 10)

    def gather_last(buf, n):
        gather_got(buf, n, 7)
        gather_put(buf, n, 12)
        gather_got(buf, n, 8)
        gather_put(buf, n, 13)

    def gather_wait(buf, n):
        for i in (3, 5, 6, 9, 10, 11, 12, 13):
            gather_got(buf, n, i)

    scatter_plan = (
        ((3, 0), 0, LEFT), ((3, 0), 1, LEFT), ((1, 0), 1, RIGHT), ((1, 0), 0, RIGHT),
        ((0, 1), 0, SIDE), ((0, 1), 1, SIDE), ((2, 0), 0, LEFT), ((2, 0), 1, RIGHT),
        ((3, 1), 0, LEFT), ((1, 1), 0, RIGHT), ((3, 1), 1, SIDE), ((1, 1), 1, SIDE),
        ((2, 1), 1, SIDE), ((2, 1), 0, LEFT),
    )

    def scatter_put(buf, n, i, merge=()):
        (dx, dy), h, to = scatter_plan[i]
        d = at_tp(dx, dy)
        for m in merge:
            arrived(rs_r.at[n, m], ("rs", n, m), hop(*scatter_plan[m][2]))
        if merge:

            def body(j, c):
                r = pl.ds(pl.multiple_of(h * HALF + j * BLK, BLK), BLK)
                total = buf[d, r, :].astype(F32)
                for m in merge:
                    total = total + rs_r[n, m, row_block(j, BLK), :].astype(F32)
                buf[d, r, :] = total.astype(BF16)
                return c

            loop(HALF // BLK, body, 0)
        send(buf.at[d, half(h), :], rs_r.at[n, i], ("rs", n, i), hop(*to))

    def scatter_send(buf, n):
        for i in (13, 12, 9, 6, 10, 3, 11, 5):
            scatter_put(buf, n, i)

    def scatter_relay(buf, n):
        scatter_put(buf, n, 8, (13,))
        scatter_put(buf, n, 7, (12,))
        scatter_put(buf, n, 0, (6,))
        scatter_put(buf, n, 1, (10,))

    def scatter_last(buf, n):
        scatter_put(buf, n, 4, (8, 9))
        scatter_put(buf, n, 2, (7, 11))

    def scatter_wait(n):
        for m in range(6):
            arrived(rs_r.at[n, m], ("rs", n, m), hop(*scatter_plan[m][2]))

    def scatter_sum(buf, n, r, j, h):
        total = buf[p, r, :].astype(F32)
        for m in ((0, 3, 4), (1, 2, 5))[h]:
            total = total + rs_r[n, m, row_block(j, BLK), :].astype(F32)
        return total

    def halo_send(buf, n):
        send(buf.at[:, PAD : 2 * PAD], buf.at[:, PAD + FR : WIDE], ("ha", n, 0), left)
        send(buf.at[:, FR : FR + PAD], buf.at[:, 0:PAD], ("ha", n, 1), right)

    def halo_wait(buf, n):
        arrived(buf.at[:, PAD + FR : WIDE], ("ha", n, 0), left)
        arrived(buf.at[:, 0:PAD], ("ha", n, 1), right)

        @pl.when(q == 0)
        def _():
            buf[:, 0:PAD] = jnp.zeros((CH, PAD), buf.dtype)

        @pl.when(q == SEQ - 1)
        def _():
            buf[:, PAD + FR : WIDE] = jnp.zeros((CH, PAD), buf.dtype)

    def contract_rows(w, v):
        return lax.dot_general(w, v, (((0,), (0,)), ((), ())), preferred_element_type=F32)

    def contract_cols(a, b):
        return lax.dot_general(a, b, (((1,), (1,)), ((), ())), preferred_element_type=F32)

    for copy in loads[0:4]:
        copy.wait()
    par_t[...] = jnp.zeros((128, 2 * 128), F32)
    par_t[0:TAPS, 0:CH] = dk_ref[...]
    par_t[GAIN_CONV : GAIN_CONV + 1, 0:CH] = cg_ref[...]
    par_t[GAIN_NORM : GAIN_NORM + 1, 0:CH] = ng_ref[...]
    par_ref[...] = par_t[...].T[0:CH]

    local_moments(lambda r: x_all[p, r, :].astype(F32), st0_s)
    st0_s[8:16, :] = jnp.zeros((8, 128), F32)
    st0_s[8:9, :] = par_t[GAIN_NORM : GAIN_NORM + 1, 0:128]
    st0_s[9:10, :] = par_t[GAIN_NORM : GAIN_NORM + 1, 128:256]
    pl.semaphore_wait(barrier, len(peers))
    st0_r[p] = st0_s[...]
    for k in range(1, TP):
        send(st0_s, st0_r.at[p], ("st", 0, k - 1), tp_dev(k))
    gather_send(x_all, 0)

    loads[4].wait()
    loads[5].wait()
    def dact_body(d, c):
        lanes = pl.ds(pl.multiple_of(d * (2 * CH), 128), 2 * CH)
        term = contract_rows(wo_ref[:, lanes], cot_ref[...]).astype(BF16)
        da_s[2 * d] = term[0:CH]
        da_s[2 * d + 1] = term[CH : 2 * CH]
        return c

    loop(TP // 2, dact_body, 0)
    gather_relay(x_all, 0)
    gather_last(x_all, 0)

    for k in range(1, TP):
        arrived(st0_r.at[lax.rem(p + TP - k, TP)], ("st", 0, k - 1), tp_dev(k))
    gains_t[...] = jnp.zeros((128, 256), F32)
    for j in range(TP):
        gains_t[j : j + 1, 0:128] = st0_r[j, 8:9, :]
        gains_t[j : j + 1, 128:256] = st0_r[j, 9:10, :]
    gains[...] = gains_t[...].T
    mean_in, inv_in = merged([st0_r[j] for j in range(TP)])

    def own_body(i, c):
        r = row_block(i, BLK)
        h = (x_all[p, r, :].astype(F32) - mean_in) * inv_in
        hat_in[r, :] = h
        normed[p, r, :] = (h * par_ref[r, GAIN_NORM : GAIN_NORM + 1]).astype(BF16)
        return c

    loop(CH // BLK, own_body, 0)
    scatter_send(da_s, 0)
    loads[6].wait()
    loads[7].wait()

    def near(j):
        return (j == at_tp(1, 0)) | (j == at_tp(3, 0)) | (j == at_tp(0, 1))

    def far(j):
        return (j == at_tp(2, 0)) | (j == at_tp(1, 1)) | (j == at_tp(3, 1)) | (j == at_tp(2, 1))

    for which, pieces in ((near, (3, 5)), (far, (6, 9, 10, 11, 12, 13))):
        for i in pieces:
            gather_got(x_all, 0, i)
        for j in range(TP):

            @pl.when(which(j))
            def _():
                def body(i, c):
                    r = row_block(i, BLK)
                    h = (x_all[j, r, :].astype(F32) - mean_in) * inv_in
                    normed[j, r, :] = (h * gains[r, j : j + 1]).astype(BF16)
                    return c

                loop(CH // BLK, body, 0)

    def glu_part(low, high):
        part = normed[:, :, low:high].reshape(D, high - low)
        v = jnp.dot(wv_ref[...], part, preferred_element_type=F32)
        s = jax.nn.sigmoid(jnp.dot(wg_ref[...], part, preferred_element_type=F32))
        value[:, low:high] = v
        sig[:, low:high] = s
        glu_w[:, PAD + low : PAD + high] = (v * s).astype(BF16)

    glu_part(0, 128)
    glu_part(FR - 128, FR)
    halo_send(glu_w, 0)
    glu_part(128, FR - 128)
    scatter_relay(da_s, 0)
    halo_wait(glu_w, 0)

    def conv_body(i, c):
        r = row_block(i, 16)
        w = glu_w[r, :].astype(F32)
        taps = par_ref[r, 0:TAPS]
        spans = ((0, FR + PAD), (0, FR + PAD), (PAD, FR + PAD), (PAD, WIDE))
        acc = [None] * 4
        for b in range(8):
            moved = pltpu.roll(w, WIDE - b, 1) if b else w
            for a in range(4):
                k = 8 * a + b
                term = taps[:, k : k + 1] * moved[:, spans[a][0] : spans[a][1]]
                acc[a] = term if acc[a] is None else acc[a] + term
        total = acc[2] + pltpu.roll(acc[0], 16, 1)[:, PAD:] + pltpu.roll(acc[1], 8, 1)[:, PAD:]
        conv[r, :] = total + pltpu.roll(acc[3], FR + PAD - 8, 1)[:, 0:FR]
        return c

    lax.fori_loop(0, CH // 32, conv_body, 0)
    scatter_last(da_s, 0)
    lax.fori_loop(CH // 32, CH // 16, conv_body, 0)
    local_moments(lambda r: conv[r, :], st_s.at[1])
    share(1)

    scatter_wait(0)
    for h in range(2):

        def dsum_body(j, c):
            r = pl.ds(pl.multiple_of(h * HALF + j * BLK, BLK), BLK)
            dact[r, :] = scatter_sum(da_s, 0, r, j, h)
            return c

        loop(HALF // BLK, dsum_body, 0)
    mean_c, inv_c = merged(shared(1))

    def act_body(i, carry):
        a, b = carry
        r = row_block(i, BLK)
        h = (conv[r, :] - mean_c) * inv_c
        hatc[r, :] = h
        g = par_ref[r, GAIN_CONV : GAIN_CONV + 1]
        scaled = h * g
        s = jax.nn.sigmoid(scaled)
        act_all[p, r, :] = (scaled * s).astype(BF16)
        ds = dact[r, :] * (s + scaled * s * (1.0 - s))
        sm_s[r, GAIN_CONV : GAIN_CONV + 1] = jnp.sum(ds * h, axis=1, keepdims=True)
        e = ds * g
        dact[r, :] = e
        return a + fold8(e), b + fold8(e * h)

    sm_s[...] = jnp.zeros((CH, 128), F32)
    first, second = loop(CH // BLK, act_body, (zero8, zero8))
    put_tile(st_s.at[2], collapse(first), collapse(second))
    share(2)
    gather_send(act_all, 1)
    first, second = summed(2)

    def dconv_body(i, c):
        r = row_block(i, BLK)
        dcv_w[r, PAD : PAD + FR] = ((dact[r, :] - first - hatc[r, :] * second) * inv_c).astype(BF16)
        return c

    loop(CH // BLK, dconv_body, 0)
    halo_send(dcv_w, 1)
    gather_relay(act_all, 1)
    halo_wait(dcv_w, 1)

    at_end = (q == SEQ - 1).astype(F32)

    def back_body(i, c):
        r = row_block(i, 16)
        w = dcv_w[r, :].astype(F32)
        taps = par_ref[r, 0:TAPS]
        u = glu_w[r, :].astype(F32)
        spans = ((PAD, WIDE), (PAD, WIDE), (PAD, FR + PAD), (0, FR + PAD))
        glus = []
        for a in range(4):
            g = pltpu.roll(u, (16 - 8 * a) % WIDE, 1) if a != 2 else u
            glus.append((g[:, PAD : PAD + FR], g[:, PAD + FR :] * at_end if a < 2 else None))
        acc = [None] * 4
        for b in range(8):
            moved = pltpu.roll(w, b, 1) if b else w
            for a in range(4):
                k = 8 * a + b
                term = taps[:, k : k + 1] * moved[:, spans[a][0] : spans[a][1]]
                acc[a] = term if acc[a] is None else acc[a] + term
                body, tail = glus[a]
                m = body * moved[:, PAD : PAD + FR]
                m = (m[:, 0:128] + m[:, 128:256]) + (m[:, 256:384] + m[:, 384:512])
                if tail is not None and b:
                    m = m + tail * moved[:, PAD + FR :]
                prod[k, r, :] = m
        total = acc[2] + pltpu.roll(acc[0], FR + PAD - 16, 1)[:, 0:FR]
        total = total + pltpu.roll(acc[1], FR + PAD - 8, 1)[:, 0:FR] + pltpu.roll(acc[3], 8, 1)[:, PAD:]
        s = sig[r, :]
        dv = total * s
        dv_b[r, :] = dv.astype(BF16)
        dg_b[r, :] = (dv * value[r, :] * (1.0 - s)).astype(BF16)
        return c

    lax.fori_loop(0, CH // 32, back_body, 0)
    gather_last(act_all, 1)
    lax.fori_loop(CH // 32, CH // 16, back_body, 0)

    other = pl.ds(pl.multiple_of((1 - core) * HALF, HALF), HALF)
    mine = pl.ds(pl.multiple_of(core * HALF, HALF), HALF)

    def pair_send(g):
        send(g16.at[g, other, :], c1.at[g], ("c1", g), mate)

    def weight_grad(g, left_ref, all_ref):
        g16[g] = contract_cols(left_ref[...], all_ref[...].reshape(D, FR)).astype(BF16)
        pair_send(g)

    weight_grad(0, dv_b, normed)
    weight_grad(1, dg_b, normed)

    def dn_pair(dx, entries):
        xx = lax.rem(tx + dx, 4)
        lanes = pl.ds(pl.multiple_of(xx * (2 * CH), 128), 2 * CH)
        term = contract_rows(wv_ref[:, lanes], dv_b[...]) + contract_rows(wg_ref[:, lanes], dg_b[...])
        term = term.astype(BF16)
        dn_s[2 * xx] = term[0:CH]
        dn_s[2 * xx + 1] = term[CH : 2 * CH]
        for i in entries:
            scatter_put(dn_s, 1, i)

    def z_block(zz):
        return (
            pl.ds(pl.multiple_of((zz // 4) * ZR, 16), ZR),
            pl.ds(pl.multiple_of(lax.rem(zz, 4) * ZL, 128), ZL),
        )

    def chains(g):
        sign = 1 if g % 2 == 0 else NZ - 1
        return ((0, 4, sign), (1, 3, NZ - sign))

    def z_start(g):
        arrived(c1.at[g], ("c1", g), mate)
        s16[g] = (g16[g, mine, :].astype(F32) + c1[g].astype(F32)).astype(BF16)
        z_hop(g, 1)

    def z_got(g, i, sign):
        arrived(zr.at[g, i], ("z", g, i), z_dev(sign))
        return zr[g, i].astype(F32)

    def z_hop(g, step):
        for chain, n, sign in chains(g):
            if step <= n:
                rr, ll = z_block(lax.rem(z + sign * (n + 1 - step), NZ))
                i = chain * 4 + step - 1
                if step > 1:
                    s16[g, rr, ll] = (s16[g, rr, ll].astype(F32) + z_got(g, i - 1, sign)).astype(BF16)
                send(s16.at[g, rr, ll], zr.at[g, i], ("z", g, i), z_dev(sign))

    def y_send(g):
        rr, ll = z_block(z)
        total = s16[g, rr, ll].astype(F32)
        for chain, n, sign in chains(g):
            total = total + z_got(g, chain * 4 + n - 1, sign)
        y16[g] = total.astype(BF16)
        yr[g, yh] = total.astype(BF16)
        for k in range(1, NY):
            send(y16.at[g], yr.at[g, yh], ("y", g, k - 1), y_dev(k))

    outs = (gval_out, ggate_out, gout_out)

    def out_block(zz, cc):
        rr, ll = z_block(zz)
        return pl.ds(pl.multiple_of(cc * HALF + (zz // 4) * ZR, 16), ZR), ll

    def w_start(g):
        for k in range(1, NY):
            arrived(yr.at[g, lax.rem(yh + NY - k, NY)], ("y", g, k - 1), y_dev(k))
        total = yr[g, 0].astype(F32)
        for j in range(1, NY):
            total = total + yr[g, j].astype(F32)
        r16[g] = (total * scale).astype(BF16)
        rr, ll = out_block(z, core)
        outs[g][rr, ll] = r16[g]
        for chain, n, sign in chains(g):
            send(r16.at[g], outs[g].at[rr, ll], ("w", g, chain * 4), z_dev(sign))
        send(r16.at[g], outs[g].at[rr, ll], ("f", g, 0), mate)

    def w_hop(g, step):
        for chain, n, sign in chains(g):
            if step <= n + 1:
                i = chain * 4 + step - 2
                rr, ll = out_block(lax.rem(z + (NZ - sign) * (step - 1), NZ), core)
                piece = outs[g].at[rr, ll]
                arrived(piece, ("w", g, i), z_dev(sign))
                if step <= n:
                    send(piece, piece, ("w", g, i + 1), z_dev(sign))
                send(piece, piece, ("f", g, 1 + i), mate)

    def f_wait(g):
        rr, ll = out_block(z, 1 - core)
        arrived(outs[g].at[rr, ll], ("f", g, 0), mate)
        for chain, n, sign in chains(g):
            for step in range(2, n + 2):
                rr, ll = out_block(lax.rem(z + (NZ - sign) * (step - 1), NZ), 1 - core)
                arrived(outs[g].at[rr, ll], ("f", g, 1 + chain * 4 + step - 2), mate)

    z_start(0)
    gather_wait(act_all, 1)
    weight_grad(2, cot_ref, act_all)
    z_start(1)
    dn_pair(2, (13, 12, 6))
    z_start(2)
    dn_pair(1, (9, 3, 11))
    z_hop(0, 2)
    z_hop(1, 2)
    dn_pair(3, (10,))
    dn_pair(0, (5,))
    z_hop(2, 2)
    z_hop(0, 3)
    z_hop(1, 3)
    scatter_relay(dn_s, 1)
    z_hop(2, 3)

    for k in range(TAPS):
        sm_s[:, k : k + 1] = jnp.sum(prod[k], axis=1, keepdims=True)
    send(sm_s, sm_c, ("sc", 0), mate)

    z_hop(0, 4)
    z_hop(1, 4)
    scatter_last(dn_s, 1)
    z_hop(2, 4)
    y_send(0)
    y_send(1)
    y_send(2)

    def sm_rows(zz):
        return pl.ds(pl.multiple_of(zz * SR, 8), SR)

    arrived(sm_c, ("sc", 0), mate)
    sm_t[...] = sm_s[...] + sm_c[...]

    for k in range(1, NZ):
        send(sm_t.at[sm_rows(lax.rem(z + k, NZ)), :], sm_z.at[z], ("sz", k - 1), z_dev(k))
    sm_z[z] = sm_t[sm_rows(z), :]

    value[...] = jnp.dot(wo_ref[...], act_all[...].reshape(D, FR), preferred_element_type=F32)

    def out_body(i, c):
        r = row_block(i, BLK)
        block_out[r, :] = (x_all[p, r, :].astype(F32) + value[r, :]).astype(BF16)
        return c

    loop(CH // BLK, out_body, 0)

    ncol[...] = jnp.zeros((256, 128), F32)
    scatter_wait(1)

    carry = (zero8, zero8)
    for h in range(2):

        def dnorm_body(j, carry):
            a, b = carry
            r = pl.ds(pl.multiple_of(h * HALF + j * BLK, BLK), BLK)
            total = scatter_sum(dn_s, 1, r, j, h)
            hat = hat_in[r, :]
            ncol[r, 0:1] = jnp.sum(total * hat, axis=1, keepdims=True)
            e = total * par_ref[r, GAIN_NORM : GAIN_NORM + 1]
            dact[r, :] = e
            return a + fold8(e), b + fold8(e * hat)

        carry = loop(HALF // BLK, dnorm_body, carry)
    first, second = carry
    put_tile(st_s.at[3], collapse(first), collapse(second))
    share(3)

    def all_sum(buf, count):
        total = buf[0]
        for j in range(1, count):
            total = total + buf[j]
        return total

    flat = ncol[...].T
    nt_s[0] = jnp.zeros((8, 128), F32)
    nt_s[0, 0:1] = flat[0:1, 0:128]
    nt_s[0, 1:2] = flat[0:1, 128:256]
    nt_z[z] = nt_s[0]
    for k in range(1, NZ):
        send(nt_s.at[0], nt_z.at[z], ("nz", k - 1), z_dev(k))

    for k in range(1, NZ):
        arrived(sm_z.at[lax.rem(z + NZ - k, NZ)], ("sz", k - 1), z_dev(k))
    total = all_sum(sm_z, NZ)
    sm_r[0] = total
    sm_y[yh] = total
    for k in range(1, NY):
        send(sm_r.at[0], sm_y.at[yh], ("sy", k - 1), y_dev(k))

    w_start(0)
    w_start(1)
    w_start(2)
    w_hop(0, 2)
    w_hop(1, 2)

    first, second = summed(3)

    def grad_body(i, c):
        r = row_block(i, BLK)
        back = (dact[r, :] - first - hat_in[r, :] * second) * inv_in
        input_grad[r, :] = (cot_ref[r, :].astype(F32) + back).astype(BF16)
        return c

    loop(CH // BLK, grad_body, 0)
    for k in range(1, NZ):
        arrived(nt_z.at[lax.rem(z + NZ - k, NZ)], ("nz", k - 1), z_dev(k))
    nt_s[1] = all_sum(nt_z, NZ)
    nt_y[yh] = nt_s[1]
    for k in range(1, NY):
        send(nt_s.at[1], nt_y.at[yh], ("ny", k - 1), y_dev(k))

    for k in range(1, NY):
        arrived(sm_y.at[lax.rem(yh + NY - k, NY)], ("sy", k - 1), y_dev(k))
    total = all_sum(sm_y, NY)
    sm_r[1] = total * scale
    small_out[sm_rows(z), :] = total * scale
    for k in range(1, NZ):
        send(sm_r.at[1], small_out.at[sm_rows(z), :], ("sw", k - 1), z_dev(k))

    w_hop(2, 2)
    w_hop(0, 3)
    w_hop(1, 3)
    w_hop(2, 3)
    w_hop(0, 4)
    w_hop(1, 4)
    for k in range(1, NY):
        arrived(nt_y.at[lax.rem(yh + NY - k, NY)], ("ny", k - 1), y_dev(k))
    nt_s[2] = all_sum(nt_y, NY)
    send(nt_s.at[2], nt_c, ("nc", 0), mate)

    w_hop(2, 4)
    w_hop(0, 5)
    w_hop(1, 5)
    w_hop(2, 5)
    for k in range(1, NZ):
        arrived(small_out.at[sm_rows(lax.rem(z + NZ - k, NZ)), :], ("sw", k - 1), z_dev(k))
    arrived(nt_c, ("nc", 0), mate)
    norm_out[...] = (nt_s[2] + nt_c[...]) * scale
    for g in range(3):
        f_wait(g)
    for copy in sends:
        copy.wait_send()


def copy_out(*refs):
    ins, outs, sem = refs[0:7], refs[7:15], refs[15]
    small, norm = ins[5], ins[6]
    stores = [pltpu.make_async_copy(ins[i], outs[i], sem.at[i]) for i in range(5)]
    for copy in stores:
        copy.start()
    outs[7][:, 0:128] = norm[0:1, :]
    outs[7][:, 128:CH] = norm[1:2, 0 : CH - 128]
    cols = jnp.concatenate([small[...], jnp.zeros((2 * 128 - CH, 128), F32)], axis=0).T
    outs[5][...] = cols[0:TAPS, 0:CH]
    outs[6][...] = cols[GAIN_CONV : GAIN_CONV + 1, 0:CH]
    for copy in stores:
        copy.wait()


def local(
    frames_in, norm_gain, value_weight, gate_weight, depth_kernel, conv_gain, out_weight, cotangent
):
    act = jax.ShapeDtypeStruct((CH, FR), BF16)
    mat = jax.ShapeDtypeStruct((CH, D), BF16)
    row = jax.ShapeDtypeStruct((1, CH), F32)
    vm = pltpu.VMEM
    dma = pltpu.SemaphoreType.DMA
    full = vm((CH, FR), F32)
    eight = vm((TP, CH, FR), BF16)
    wide = vm((CH, WIDE), BF16)
    block = vm((CH, FR), BF16)
    weight = vm((CH, D), BF16)
    small = vm((CH, 128), F32)
    line = vm((1, CH), F32)
    tile = vm((8, 128), F32)
    scratch = [line, weight, weight, vm((TAPS, CH), F32), line, weight, block, vm((128, 256), F32), small] + [full] * 6
    scratch += [eight, vm((128, 256), F32), vm((256, 128), F32), vm((16, 128), F32), vm((TP, 16, 128), F32)]
    scratch += [eight] * 4
    scratch += [vm((2, 14, HALF, FR), BF16), wide, wide, block, block, vm((TAPS, CH, 128), F32)]
    scratch += [vm((4, 8, 128), F32), vm((4, TP, 8, 128), F32)]
    scratch += [
        vm((3, CH, D), BF16),
        vm((3, HALF, D), BF16),
        vm((3, HALF, D), BF16),
        vm((3, 8, ZR, ZL), BF16),
        vm((3, ZR, ZL), BF16),
        vm((3, NY, ZR, ZL), BF16),
        vm((3, ZR, ZL), BF16),
    ]
    scratch += [vm((256, 128), F32), vm((3, 8, 128), F32), vm((NZ, 8, 128), F32), vm((NY, 8, 128), F32), tile]
    scratch += [small, small, small, vm((NZ, SR, 128), F32), vm((NY, SR, 128), F32), vm((2, SR, 128), F32)]
    scratch += [dma((8,))]
    for shape in ((4, 7), (2, 14), (2, 14), (2, 2), (3,), (3, 8), (3, 3), (3, 8), (3, 8), (7,), (3,), (1,), (1,), (7,), (3,), (7,)):
        scratch += [dma(shape), dma(shape)]
    vmem = pl.BlockSpec(memory_space=pltpu.VMEM)
    anywhere = pl.BlockSpec(memory_space=pl.ANY)
    hbm = pl.BlockSpec(memory_space=pltpu.HBM)
    results = pl.pallas_call(
        kernel,
        out_shape=(act, act, mat, mat, mat, jax.ShapeDtypeStruct((CH, 128), F32), jax.ShapeDtypeStruct((8, 128), F32)),
        in_specs=[hbm] * 8,
        out_specs=(vmem,) * 7,
        scratch_shapes=scratch,
        compiler_params=pltpu.CompilerParams(
            collective_id=0, has_side_effects=True, vmem_limit_bytes=VMEM_LIMIT
        ),
    )(
        pltpu.with_memory_space_constraint(frames_in, pltpu.HBM),
        pltpu.with_memory_space_constraint(norm_gain.reshape(1, CH), pltpu.HBM),
        pltpu.with_memory_space_constraint(value_weight, pltpu.HBM),
        pltpu.with_memory_space_constraint(gate_weight, pltpu.HBM),
        pltpu.with_memory_space_constraint(depth_kernel.T, pltpu.HBM),
        pltpu.with_memory_space_constraint(conv_gain.reshape(1, CH), pltpu.HBM),
        pltpu.with_memory_space_constraint(out_weight, pltpu.HBM),
        pltpu.with_memory_space_constraint(cotangent, pltpu.HBM),
    )
    block_out, input_grad, gval, ggate, gout, gkernel, gconv, gnorm = pl.pallas_call(
        copy_out,
        out_shape=(act, act, mat, mat, mat, jax.ShapeDtypeStruct((TAPS, CH), F32), row, row),
        in_specs=[vmem] * 7,
        out_specs=(anywhere,) * 5 + (vmem,) * 3,
        scratch_shapes=[dma((5,))],
        compiler_params=pltpu.CompilerParams(vmem_limit_bytes=8 * 1024 * 1024),
    )(*results)
    return (
        block_out,
        input_grad,
        gnorm.reshape(CH),
        gval,
        ggate,
        gkernel.T,
        gconv.reshape(CH),
        gout,
    )


def solution(mesh):
    return jax.shard_map(
        local,
        mesh=mesh,
        in_specs=(
            P("tp", "seq"),
            P("tp"),
            P("tp", None),
            P("tp", None),
            P("tp", None),
            P("tp"),
            P("tp", None),
            P("tp", "seq"),
        ),
        out_specs=(
            P("tp", "seq"),
            P("tp", "seq"),
            P("tp"),
            P("tp", None),
            P("tp", None),
            P("tp", None),
            P("tp"),
            P("tp", None),
        ),
        check_vma=False,
    )
```
